32 devices in a mesh: head: 4 (over y, x), blk: 8 (over z, core).
Axes of the slice: x: 2, y: 2, z: 4, core: 2. Of those that a mesh axis runs over, the one named last changes fastest.
Arguments:
- inputs: bfloat16 [8, 3072, 1024], P('blk', 'head'), may hold values from -13 to 13
- seg_ids: int32 [8, 3072], replicated, may hold values from 0 to 48, as said below
- var_ids: int32 [8, 3072], replicated, may hold values from 0 to 7
- time_ids: int32 [8, 3072], replicated, may hold values from 0 to 4095
- valid_mask: int32 [8, 3072], replicated, may hold values 0 or 1
- w_query: bfloat16 [1024, 1024], P(('head', 'blk')), may hold values from -0.1875 to 0.1875
- w_key: bfloat16 [1024, 1024], P(('head', 'blk')), may hold values from -0.1875 to 0.1875
- w_value: bfloat16 [1024, 1024], P(('head', 'blk')), may hold values from -0.1875 to 0.1875
- w_out: bfloat16 [1024, 1024], P(('head', 'blk')), may hold values from -1.5 to 1.5
- w_gate: bfloat16 [1024, 4096], P(('head', 'blk')), may hold values from -0.1875 to 0.1875
- w_up: bfloat16 [1024, 4096], P(('head', 'blk')), may hold values from -0.1875 to 0.1875
- w_down: bfloat16 [4096, 1024], P(('head', 'blk')), may hold values from -0.09375 to 0.09375
- gain_attn: float32 [1024], replicated, may hold values from 0.5 to 1.5
- gain_ffn: float32 [1024], replicated, may hold values from 0.5 to 1.5
- gain_query: float32 [64], replicated, may hold values from 0.25 to 1.75
- gain_key: float32 [64], replicated, may hold values from 0.25 to 1.75
- variate_bias: float32 [2, 16], replicated, may hold values from -1 to 1
- out_grad: bfloat16 [8, 3072, 1024], P('blk', 'head'), may hold values from -6 to 6
Outputs:
- layer_out: bfloat16 [8, 3072, 1024], P('blk', 'head')
- grad_inputs: bfloat16 [8, 3072, 1024], P('blk', 'head')
- grad_w_query: float32 [1024, 1024], P(('head', 'blk'))
- grad_w_key: float32 [1024, 1024], P(('head', 'blk'))
- grad_w_value: float32 [1024, 1024], P(('head', 'blk'))
- grad_w_out: float32 [1024, 1024], P(('head', 'blk'))
- grad_w_gate: float32 [1024, 4096], P(('head', 'blk'))
- grad_w_up: float32 [1024, 4096], P(('head', 'blk'))
- grad_w_down: float32 [4096, 1024], P(('head', 'blk'))
- grad_gain_attn: float32 [1024], replicated
- grad_gain_ffn: float32 [1024], replicated
- grad_gain_query: float32 [64], replicated
- grad_gain_key: float32 [64], replicated
- grad_variate_bias: float32 [2, 16], replicated
- rms_values: float32 [3], replicated
The draws below stay inside these ranges and needn't reach their ends.
Inputs may be any that keep to these rules, and one draw needn't show every extreme that they name: `seg_ids`: document numbers never fall along the order of tokens and need not be consecutive; each document spans at most 4096 tokens and one spans exactly 4096.
All inputs are finite; a program needn't handle non-finite values.
Results may differ from the reference program's by a relative error of at most 0.018.
Values may be sent and summed in bfloat16 or wider, within the bound.
No kernel may reach another device: no remote copies, remote signals or barrier semaphores. Data moves between devices by JAX's collectives and lax.ppermute only.
A program may use at most 192 MiB of HBM per device.

```python
import math
import jax
import jax.numpy as jnp
from jax import lax

D = 1024
H = 16
HD = 64
FF = 4096
QBLK = 512
VARS = 8
MAXPOS = 4096
SEGMOST = 4096
HALF = 512
BLOCK = 3072
NBLOCKS = 8
TOKENS = 24576


def draw_inputs(key, part):
    position = jnp.arange(TOKENS, dtype=jnp.float32) / TOKENS
    trend = 0.5 * jnp.exp(position * math.log(3.0))
    spread = jnp.exp(jax.random.uniform(jax.random.fold_in(key, 11), (TOKENS,), minval=-0.35, maxval=0.35))
    entries = jnp.clip(jax.random.normal(jax.random.fold_in(key, 12), (TOKENS, D), dtype=jnp.float32), -6.0, 6.0)
    scaled = entries * trend[:, None] * spread[:, None]
    return scaled.reshape(NBLOCKS, BLOCK, D).astype(jnp.bfloat16)


def draw_seg_ids(key, part):
    shortest = SEGMOST // 8
    doc_total = TOKENS // shortest + 1
    lengths = jax.random.randint(jax.random.fold_in(key, 21), (doc_total,), shortest, SEGMOST + 1)
    longest = jax.random.randint(jax.random.fold_in(key, 22), (), 0, 4)
    lengths = jnp.where(jnp.arange(doc_total) == longest, SEGMOST, lengths)
    doc_ends = jnp.cumsum(lengths)
    numbers = jnp.searchsorted(doc_ends, jnp.arange(TOKENS), side='right').astype(jnp.int32)
    top_number = TOKENS // shortest
    numbers = jnp.where(numbers == numbers[TOKENS - 1], top_number, numbers)
    return numbers.astype(jnp.int32).reshape(NBLOCKS, BLOCK)


def place_ends(values, own_key, least, high):
    longest = values.shape.index(max(values.shape))
    spots = []
    for shift in (0, 1):
        where = [jax.random.randint(jax.random.fold_in(own_key, axis), (), 0, length) for axis, length in enumerate(values.shape)]
        where[longest] = (where[longest] + shift) % values.shape[longest]
        spots.append(tuple(where))
    return values.at[spots[0]].set(least).at[spots[1]].set(high)


def block_scale(own_key, extent, shards, smallest, high):
    loudness, own = 1.0, jax.random.fold_in(own_key, 6)
    for dim, parts in shards:
        steps = jnp.exp(jax.random.uniform(jax.random.fold_in(own, dim), (parts,), jnp.float32, smallest / len(shards), high / len(shards)))
        loudness = loudness * jnp.repeat(steps, extent[dim] // parts).reshape([-1 if axis == dim else 1 for axis in range(len(extent))])
    return loudness


def normal_values(own_key, extent, scale, bound, shards=(), held_as=jnp.bfloat16):
    factor_of = block_scale(own_key, extent, shards, -0.22, 0.18) if shards else 1.0
    drawn = jax.random.normal(own_key, extent, jnp.float32) * scale * factor_of
    return jnp.minimum(jnp.maximum(drawn, -bound), bound).astype(held_as)


def setup_inputs(seed: int = 0) -> dict:
    key_of = jax.random.split(jax.random.key(seed), 19)
    return {
        "inputs": draw_inputs(jax.random.fold_in(key_of[18], 71), 0),
        "seg_ids": draw_seg_ids(jax.random.fold_in(key_of[18], 71), 0),
        "var_ids": place_ends(jax.random.randint(key_of[2], (NBLOCKS, BLOCK), 0, VARS), jax.random.fold_in(key_of[2], 1), 0, VARS - 1).astype(jnp.int32),
        "time_ids": place_ends(jax.random.randint(key_of[3], (NBLOCKS, BLOCK), 0, MAXPOS), jax.random.fold_in(key_of[3], 1), 0, MAXPOS - 1).astype(jnp.int32),
        "valid_mask": place_ends((jax.random.randint(key_of[4], (NBLOCKS, BLOCK), 0, 8) < 7).astype(jnp.int32), jax.random.fold_in(key_of[4], 1), 0, 1),
        "w_query": normal_values(key_of[5], (D, D), D ** -0.5, 0.1875, ((0, 32),)),
        "w_key": normal_values(key_of[6], (D, D), D ** -0.5, 0.1875, ((0, 32),)),
        "w_value": normal_values(key_of[7], (D, D), D ** -0.5, 0.1875, ((0, 32),)),
        "w_out": normal_values(key_of[8], (D, D), (D // 64) ** -0.5, 1.5, ((0, 32),)),
        "w_gate": normal_values(key_of[9], (D, FF), D ** -0.5, 0.1875, ((0, 32),)),
        "w_up": normal_values(key_of[10], (D, FF), D ** -0.5, 0.1875, ((0, 32),)),
        "w_down": normal_values(key_of[11], (FF, D), FF ** -0.5, 0.09375, ((0, 32),)),
        "gain_attn": jnp.clip(1.0 + 0.1 * jax.random.normal(key_of[12], (D,), jnp.float32), 0.5, 1.5),
        "gain_ffn": jnp.clip(1.0 + 0.1 * jax.random.normal(key_of[13], (D,), jnp.float32), 0.5, 1.5),
        "gain_query": jnp.clip(1.0 + 0.15 * jax.random.normal(key_of[14], (HD,), jnp.float32), 0.25, 1.75),
        "gain_key": jnp.clip(1.0 + 0.15 * jax.random.normal(key_of[15], (HD,), jnp.float32), 0.25, 1.75),
        "variate_bias": jnp.clip(jax.random.uniform(key_of[16], (2, H), jnp.float32, -1.0, 1.0), -1.0, 1.0),
        "out_grad": normal_values(key_of[17], (NBLOCKS, BLOCK, D), 1.0, 6.0, ((0, 8), (1, 4))),
    }


norm_eps = 1e-05
exact_mode = lax.Precision.HIGHEST

@jax.custom_vjp
def low(v):
    return lax.optimization_barrier(v.astype(jnp.bfloat16)).astype(jnp.float32)

@jax.custom_vjp
def low_back(v):
    return v

def low_keep(v):
    return (low(v), None)

def low_pass(kept, grad):
    return (grad,)

def back_keep(v):
    return (v, None)

def back_low(kept, grad):
    return (low(grad),)
low.defvjp(low_keep, low_pass)
low_back.defvjp(back_keep, back_low)

def rms_norm(values, gain_vec):
    return values * lax.rsqrt(lax.optimization_barrier(jnp.mean(values * values, axis=-1, keepdims=True)) + norm_eps) * gain_vec

def rotate(values, cosine, sine_values):
    middle = values.shape[-1] // 2
    first_half = values[..., :middle]
    second_half = values[..., middle:]
    return jnp.concatenate([first_half * cosine - second_half * sine_values, second_half * cosine + first_half * sine_values], axis=-1)

def attend(queries, key_rows, value_rows, bias_table, seg_flat, var_flat, valid_flat):
    key_span = QBLK + 2 * HALF
    score_scale = HD ** (-0.5)
    keys_pad = jnp.pad(key_rows, ((HALF, HALF), (0, 0), (0, 0)))
    values_pad = jnp.pad(value_rows, ((HALF, HALF), (0, 0), (0, 0)))
    seg_pad = jnp.pad(seg_flat, HALF, constant_values=-1)
    var_pad = jnp.pad(var_flat, HALF)
    valid_pad = jnp.pad(valid_flat, HALF)

    def one_block(row_start):
        query_part = lax.dynamic_slice_in_dim(queries, row_start, QBLK, 0)
        key_part = lax.dynamic_slice_in_dim(keys_pad, row_start, key_span, 0)
        value_part = lax.dynamic_slice_in_dim(values_pad, row_start, key_span, 0)
        seg_query = lax.dynamic_slice_in_dim(seg_flat, row_start, QBLK, 0)
        seg_key = lax.dynamic_slice_in_dim(seg_pad, row_start, key_span, 0)
        var_query = lax.dynamic_slice_in_dim(var_flat, row_start, QBLK, 0)
        var_key = lax.dynamic_slice_in_dim(var_pad, row_start, key_span, 0)
        valid_key = lax.dynamic_slice_in_dim(valid_pad, row_start, key_span, 0)
        distance = jnp.arange(QBLK, dtype=jnp.int32)[:, None] + HALF - jnp.arange(key_span, dtype=jnp.int32)[None, :]
        allowed = (seg_query[:, None] == seg_key[None, :]) & (jnp.abs(distance) < HALF) & ((valid_key[None, :] == 1) | (distance == 0))
        same_variate = var_query[:, None] == var_key[None, :]
        scores = jnp.einsum('qhd,khd->hqk', query_part, key_part, precision=exact_mode) * score_scale
        scores = scores + jnp.where(same_variate[None], bias_table[0][:, None, None], bias_table[1][:, None, None])
        scores = low_back(scores)
        scores = jnp.where(allowed[None], scores, -1e+30)
        row_peak = lax.optimization_barrier(jnp.max(scores, axis=-1, keepdims=True))
        weights = jnp.exp(scores - row_peak)
        weights = weights / lax.optimization_barrier(jnp.sum(weights, axis=-1, keepdims=True))
        return jnp.einsum('hqk,khd->qhd', low(weights), value_part, precision=exact_mode)
    starts = jnp.arange(TOKENS // QBLK, dtype=jnp.int32) * QBLK
    attended = lax.map(jax.checkpoint(one_block), starts)
    return attended.reshape(TOKENS, H * HD)

def reference(inputs, seg_ids, var_ids, time_ids, valid_mask, w_query, w_key, w_value, w_out, w_gate, w_up, w_down, gain_attn, gain_ffn, gain_query, gain_key, variate_bias, out_grad):
    seg_flat = seg_ids.reshape(-1).astype(jnp.int32)
    var_flat = var_ids.reshape(-1).astype(jnp.int32)
    valid_flat = valid_mask.reshape(-1).astype(jnp.int32)
    frequency = 10000.0 ** (-jnp.arange(HD // 2, dtype=jnp.float32) * 2.0 / HD)
    angles = time_ids.reshape(-1).astype(jnp.float32)[:, None, None] * frequency[None, None, :]
    cosine = jnp.cos(angles)
    sine_values = jnp.sin(angles)

    def forward(x_float, query_w, key_w, value_w, out_w, gate_w, up_w, down_w, attn_gain, ffn_gain, query_gain, key_gain, bias_table):
        normed_one = low(rms_norm(x_float, attn_gain))
        query_proj = low_back(jnp.dot(normed_one, query_w, precision=exact_mode)).reshape(TOKENS, H, HD)
        key_proj = low_back(jnp.dot(normed_one, key_w, precision=exact_mode)).reshape(TOKENS, H, HD)
        value_proj = low(low_back(jnp.dot(normed_one, value_w, precision=exact_mode))).reshape(TOKENS, H, HD)
        queries = low(low_back(rotate(rms_norm(query_proj, query_gain), cosine, sine_values)))
        key_rows = low(low_back(rotate(rms_norm(key_proj, key_gain), cosine, sine_values)))
        attended = low(low_back(attend(queries, key_rows, value_proj, bias_table, seg_flat, var_flat, valid_flat)))
        branch = low_back(jnp.dot(attended, out_w, precision=exact_mode))
        resid = x_float + branch
        normed_two = low(rms_norm(resid, ffn_gain))
        gate_value = low_back(jnp.dot(normed_two, gate_w, precision=exact_mode))
        up_value = low_back(jnp.dot(normed_two, up_w, precision=exact_mode))
        hidden = low(jax.nn.silu(gate_value) * up_value)
        ffn_out = jnp.dot(hidden, down_w, precision=exact_mode)
        return (resid + ffn_out, (branch, ffn_out))
    result, pullback, extras = jax.vjp(forward, inputs.reshape(TOKENS, D).astype(jnp.float32), w_query.astype(jnp.float32), w_key.astype(jnp.float32), w_value.astype(jnp.float32), w_out.astype(jnp.float32), w_gate.astype(jnp.float32), w_up.astype(jnp.float32), w_down.astype(jnp.float32), gain_attn.astype(jnp.float32), gain_ffn.astype(jnp.float32), gain_query.astype(jnp.float32), gain_key.astype(jnp.float32), variate_bias.astype(jnp.float32), has_aux=True)
    gradients = pullback(out_grad.reshape(TOKENS, D).astype(jnp.float32))
    branch, ffn_out = extras
    row_weight = valid_flat.astype(jnp.float32)[:, None]
    valid_count = jnp.maximum(jnp.sum(valid_flat.astype(jnp.float32)), 1.0)
    rms_values = jnp.stack([jnp.sqrt(jnp.sum(row_weight * result * result) / (valid_count * D)), jnp.sqrt(jnp.sum(row_weight * branch * branch) / (valid_count * D)), jnp.sqrt(jnp.sum(row_weight * ffn_out * ffn_out) / (valid_count * D))])
    return (result.astype(jnp.bfloat16).reshape(NBLOCKS, BLOCK, D), gradients[0].astype(jnp.bfloat16).reshape(NBLOCKS, BLOCK, D), gradients[1], gradients[2], gradients[3], gradients[4], gradients[5], gradients[6], gradients[7], gradients[8], gradients[9], gradients[10], gradients[11], gradients[12], rms_values)
```

```python
import functools

import jax
import jax.numpy as jnp
from jax import lax
from jax.experimental import pallas as pl
from jax.experimental.pallas import tpu as pltpu
from jax.sharding import Mesh
from jax.sharding import PartitionSpec as P

HALF = 512
ROWS = 256
FF_TILE = 512
VARS = 8
CODES = 8
CODE_SIZE = 64.0
OUTSIDE = 256.0
LOG2E = 1.4426950408889634
EPS = 1e-05
MIB = 1 << 20

LANE_HIGH = 64
LANE_LOW = 72
LANE_CODE = 80
LANE_ONE = 88
LANE_LSE = 90

SEG, VAR, VALID = 0, 1, 2

f32 = jnp.float32
bf16 = jnp.bfloat16
shape_of = jax.ShapeDtypeStruct


def mm(a, b):
    return lax.dot_general(a, b, (((1,), (0,)), ((), ())), preferred_element_type=f32)


def mm_nt(a, b):
    return lax.dot_general(a, b, (((1,), (1,)), ((), ())), preferred_element_type=f32)


def mm_tn(a, b):
    return lax.dot_general(a, b, (((0,), (0,)), ((), ())), preferred_element_type=f32)


def params(vmem=56):
    return pltpu.CompilerParams(vmem_limit_bytes=vmem * MIB)


def cost(us):
    return pl.CostEstimate(flops=int(us * 1e9), bytes_accessed=1 << 20, transcendentals=0)


def whole(shape):
    return pl.BlockSpec(shape, lambda *_: (0,) * len(shape), pipeline_mode=pl.Buffered(1))


def lane_of(shape):
    return lax.broadcasted_iota(jnp.int32, shape, len(shape) - 1)


def row_of(shape):
    return lax.broadcasted_iota(jnp.int32, shape, len(shape) - 2)


def head_ones():
    shape = (128, 128)
    return jnp.where((row_of(shape) // 64) == (lane_of(shape) // 64), 1.0, 0.0).astype(bf16)


def head_mean(values, ones):
    high = values.astype(bf16)
    low = (values - high.astype(f32)).astype(bf16)
    return (mm(high, ones) + mm(low, ones)) * (1.0 / 64.0)


def swap_halves(values):
    first = (lane_of(values.shape) % 64) < 32
    return jnp.where(first, pltpu.roll(values, 96, 1), pltpu.roll(values, 32, 1))


def fold_rows(values):
    rows, width = values.shape
    return jnp.sum(values.reshape(rows // 8, 8, width), axis=0)


def flag(ids_ref, rows=slice(None)):
    return jnp.where(ids_ref[rows, VALID : VALID + 1] == 1, 1.0, 0.0)


def key_extra(ids):
    lane = lane_of((ids.shape[0], 128))
    var = ids[:, VAR : VAR + 1]
    seg = ids[:, SEG : SEG + 1]
    invalid = jnp.where(ids[:, VALID : VALID + 1] == 1, 0.0, 1.0)
    bit = jnp.right_shift(seg, jnp.clip(lane - LANE_CODE, 0, CODES - 1)) & 1
    extra = jnp.where((var == lane - LANE_HIGH) | (var == lane - LANE_LOW) & (lane >= LANE_LOW), 1.0, 0.0)
    extra = jnp.where(lane >= LANE_CODE, CODE_SIZE * (2 * bit - 1).astype(f32), extra)
    extra = jnp.where(lane >= LANE_ONE, -CODE_SIZE * (CODES + 2.0 * invalid), extra)
    extra = jnp.where(lane > LANE_ONE, jnp.where((lane >= LANE_LSE) & (lane < LANE_LSE + 3), 1.0, 0.0), extra)
    return extra


def query_extra(ids):
    lane = lane_of((ids.shape[0], 128))
    var = ids[:, VAR : VAR + 1]
    seg = ids[:, SEG : SEG + 1]
    bit = jnp.right_shift(seg, jnp.clip(lane - LANE_CODE, 0, CODES - 1)) & 1
    extra = jnp.where((var == lane - LANE_HIGH) | (var == lane - LANE_LOW) & (lane >= LANE_LOW), 1.0, 0.0)
    extra = jnp.where(lane >= LANE_CODE, (2 * bit - 1).astype(f32), extra)
    return jnp.where(lane >= LANE_ONE, jnp.where(lane == LANE_ONE, 1.0, 0.0), extra)


def part(ref, index, rows):
    block = ref[:, index * rows : (index + 1) * rows, :]
    return block.reshape(block.shape[0] * rows, block.shape[2])


def core_at(slot, cores):
    if cores == 1:
        return 0
    own = lax.axis_index("core")
    return own if slot == 0 else 1 - own


def fill_weights(full_ref, w_refs):
    parts, _, cores, rows, _ = full_ref.shape
    for slot in range(cores):
        for index in range(parts):
            full_ref[index, :, core_at(slot, cores)] = w_refs[slot][:, index * rows : (index + 1) * rows, :]


def weight(full_ref, index):
    width = full_ref.shape[4]
    return full_ref[index].reshape(width, width)


def put_grads(out_refs, acc_ref, first):
    _, cores, rows, _ = acc_ref.shape
    for slot in range(cores):
        out_refs[slot][:, first : first + rows, :] = acc_ref[:, core_at(slot, cores)].astype(bf16)


def project_kernel(
    own_first, own_last, cores,
    x_ref, gain_ref, cos_ref, sin_ref, gq_ref, gk_ref, ids_ref, diff_ref, *refs,
):
    w_refs = refs[:cores]
    n1_ref, q0_ref, k0_ref, q_ref, k_ref, v_ref, full_ref = refs[cores:]
    step = pl.program_id(0)

    @pl.when(step == 0)
    def _():
        fill_weights(full_ref, w_refs)

    x = x_ref[...].astype(f32)
    factor = lax.rsqrt(jnp.mean(x * x, axis=-1, keepdims=True) + EPS)
    n1 = (x * factor * gain_ref[...]).astype(bf16)
    n1_ref[...] = n1
    ones = head_ones()
    cosine = cos_ref[...]
    sine = sin_ref[...]
    kaug = key_extra(ids_ref[...])
    own_lane = lane_of(kaug.shape) < 64
    pairs = x.shape[1] // 128

    k0 = mm(n1, weight(full_ref, 1))
    k0_ref[...] = k0
    value = mm(n1, weight(full_ref, 2))
    vaug = jnp.where(lane_of(kaug.shape) < 67, 1.0, 0.0)
    for pair in range(pairs):
        cols = slice(pair * 128, pair * 128 + 128)
        raw = k0[:, cols]
        normed = raw * lax.rsqrt(head_mean(raw * raw, ones) + EPS) * gk_ref[...]
        turned = normed * cosine + swap_halves(normed) * sine
        k_ref[2 * pair] = jnp.where(own_lane, turned, kaug).astype(bf16)
        k_ref[2 * pair + 1] = jnp.where(own_lane, pltpu.roll(turned, 64, 1), kaug).astype(bf16)
        val = value[:, cols]
        v_ref[2 * pair] = jnp.where(own_lane, val, vaug).astype(bf16)
        v_ref[2 * pair + 1] = jnp.where(own_lane, pltpu.roll(val, 64, 1), vaug).astype(bf16)

    @pl.when((step >= own_first) & (step < own_last))
    def _():
        q0 = mm(n1, weight(full_ref, 0))
        q0_ref[...] = q0
        qaug = query_extra(ids_ref[...])
        for pair in range(pairs):
            raw = q0[:, pair * 128 : pair * 128 + 128]
            normed = raw * lax.rsqrt(head_mean(raw * raw, ones) + EPS) * gq_ref[...]
            turned = (normed * cosine + swap_halves(normed) * sine) * (0.125 * LOG2E)
            first = qaug * diff_ref[2 * pair : 2 * pair + 1, :]
            second = qaug * diff_ref[2 * pair + 1 : 2 * pair + 2, :]
            q_ref[2 * pair] = jnp.where(own_lane, turned, first).astype(bf16)
            q_ref[2 * pair + 1] = jnp.where(own_lane, pltpu.roll(turned, 64, 1), second).astype(bf16)


def full_weights(w, rows):
    chips, total, width = w[0].shape
    return pltpu.VMEM((total // rows, chips, len(w), rows, width), bf16)


def project(x_ext, gain, w, w_rows, cosine, sine, gq, gk, ids, diff, tok, heads):
    ext, width = x_ext.shape
    own_first = HALF // ROWS
    own_last = own_first + tok // ROWS
    row = lambda i: (i, 0)
    own = lambda i: (jnp.clip(i - own_first, 0, own_last - own_first - 1), 0)
    head_row = lambda i: (0, i, 0)
    head_own = lambda i: (0, own(i)[0], 0)
    return pl.pallas_call(
        functools.partial(project_kernel, own_first, own_last, len(w)),
        name="project",
        grid=(ext // ROWS,),
        in_specs=[
            pl.BlockSpec((ROWS, width), row),
            whole((1, width)),
            pl.BlockSpec((ROWS, 128), row),
            pl.BlockSpec((ROWS, 128), row),
            whole((1, 128)),
            whole((1, 128)),
            pl.BlockSpec((ROWS, ids.shape[1]), row),
            whole(diff.shape),
        ]
        + [whole(each.shape) for each in w],
        out_specs=[
            pl.BlockSpec((ROWS, width), row),
            pl.BlockSpec((ROWS, width), own),
            pl.BlockSpec((ROWS, width), row),
            pl.BlockSpec((heads, ROWS, 128), head_own),
            pl.BlockSpec((heads, ROWS, 128), head_row),
            pl.BlockSpec((heads, ROWS, 128), head_row),
        ],
        out_shape=[
            shape_of((ext, width), bf16),
            shape_of((tok, width), f32),
            shape_of((ext, width), f32),
            shape_of((heads, tok, 128), bf16),
            shape_of((heads, ext, 128), bf16),
            shape_of((heads, ext, 128), bf16),
        ],
        scratch_shapes=[full_weights(w, w_rows)],
        compiler_params=params(),
        cost_estimate=cost(27),
    )(x_ext, gain, cosine, sine, gq, gk, ids, diff, *w)


def fill_masks(ids_ref, diag_ref, edge_ref, key_axis):
    shape = (ROWS, ROWS)
    key = lax.broadcasted_iota(jnp.int32, shape, key_axis)
    query = lax.broadcasted_iota(jnp.int32, shape, 1 - key_axis)
    edge_ref[0] = jnp.where(key > query, 0.0, -OUTSIDE)
    edge_ref[1] = jnp.where(key < query, 0.0, -OUTSIDE)
    for i in range(diag_ref.shape[0] // ROWS):
        rows = slice(i * ROWS, i * ROWS + ROWS)
        diag_ref[rows, :] = jnp.where(key == query, 2.0 * CODE_SIZE * (1.0 - flag(ids_ref, rows)), 0.0)


def attend_kernel(q_ref, k_ref, v_ref, ids_ref, o_ref, qb_ref, diag_ref, edge_ref):
    @pl.when(pl.program_id(0) == 0)
    def _():
        fill_masks(ids_ref, diag_ref, edge_ref, 1)

    tiles = 1 + 2 * HALF // ROWS
    tok = q_ref.shape[1]

    def block(i, carry):
        first_row = pl.multiple_of(i * ROWS, ROWS)
        outs = []
        for head in range(2):
            query = q_ref[head, pl.ds(first_row, ROWS), :]
            total = jnp.zeros((ROWS, 128), f32)
            for j in range(tiles):
                keys = pl.ds(first_row + j * ROWS, ROWS)
                score = mm_nt(query, k_ref[head, keys, :])
                if j == 0:
                    score = score + edge_ref[0]
                elif j == tiles - 1:
                    score = score + edge_ref[1]
                elif j == tiles // 2:
                    score = score + diag_ref[pl.ds(first_row, ROWS), :]
                total = total + mm(jnp.exp2(score).astype(bf16), v_ref[head, keys, :])
            weight = total[:, 64:65]
            outs.append(total / weight)
            lse = jnp.log2(weight)
            high = lse.astype(bf16).astype(f32)
            middle = (lse - high).astype(bf16).astype(f32)
            low = lse - high - middle
            lane = lane_of((ROWS, 128))
            updated = jnp.where(lane == LANE_LSE, -high, query.astype(f32))
            updated = jnp.where(lane == LANE_LSE + 1, -middle, updated)
            updated = jnp.where(lane == LANE_LSE + 2, -low, updated)
            qb_ref[head, pl.ds(first_row, ROWS), :] = updated.astype(bf16)
        lane = lane_of((ROWS, 128))
        joined = jnp.where(lane < 64, outs[0], pltpu.roll(outs[1], 64, 1))
        o_ref[pl.ds(first_row, ROWS), :] = joined.astype(bf16)
        return carry

    lax.fori_loop(0, tok // ROWS, block, 0)


def attend(q, k, v, ids):
    heads, tok, _ = q.shape
    ext = k.shape[1]
    pair = lambda p: (p, 0, 0)
    return pl.pallas_call(
        attend_kernel,
        name="attend",
        grid=(heads // 2,),
        in_specs=[
            pl.BlockSpec((2, tok, 128), pair),
            pl.BlockSpec((2, ext, 128), pair),
            pl.BlockSpec((2, ext, 128), pair),
            whole(ids.shape),
        ],
        out_specs=[
            pl.BlockSpec((tok, 128), lambda p: (0, p)),
            pl.BlockSpec((2, tok, 128), pair),
        ],
        out_shape=[shape_of((tok, heads * 64), bf16), shape_of((heads, tok, 128), bf16)],
        scratch_shapes=[pltpu.VMEM((tok, ROWS), f32), pltpu.VMEM((2, ROWS, ROWS), f32)],
        compiler_params=params(),
        cost_estimate=cost(36),
    )(q, k, v, ids)


def attend_back_kernel(
    q_ref, k_ref, v_ref, o_ref, do_ref, ids_ref,
    dq_ref, dk_ref, dv_ref, bias_ref,
    diag_ref, edge_ref, kt_ref, dkey_ref, dval_ref, dout_ref, dqt_ref,
):
    @pl.when(pl.program_id(0) == 0)
    def _():
        fill_masks(ids_ref, diag_ref, edge_ref, 0)

    tiles = 1 + 2 * HALF // ROWS
    tok = q_ref.shape[1]
    ext = k_ref.shape[1]
    blocks = tok // ROWS

    def one_head(head, carry):
        for i in range(blocks):
            rows = slice(i * ROWS, i * ROWS + ROWS)
            lane = lane_of((ROWS, 128))
            dout = do_ref[rows, :].astype(f32)
            shift = head * 64
            dout = pltpu.roll(dout, shift, 1)
            product = pltpu.roll(o_ref[rows, :].astype(f32), shift, 1) * dout
            delta = jnp.sum(jnp.where(lane < 64, product, 0.0), axis=-1, keepdims=True)
            high = delta.astype(bf16).astype(f32)
            middle = (delta - high).astype(bf16).astype(f32)
            low = delta - high - middle
            aug = jnp.where(lane == 64, -high, jnp.where(lane == 65, -middle, jnp.where(lane == 66, -low, 0.0)))
            dout_ref[rows, :] = jnp.where(lane < 64, dout, aug).astype(bf16)
        for t in range(ext // ROWS):
            rows = slice(t * ROWS, t * ROWS + ROWS)
            kt_ref[:, rows] = k_ref[head, rows, :].T
            dkey_ref[rows, :] = jnp.zeros((ROWS, 128), f32)
            dval_ref[rows, :] = jnp.zeros((ROWS, 128), f32)

        for i in range(blocks):
            rows = slice(i * ROWS, i * ROWS + ROWS)
            query = q_ref[head, rows, :]
            dout = dout_ref[rows, :]
            dqt = jnp.zeros((128, ROWS), f32)
            for j in range(tiles):
                keys = slice((i + j) * ROWS, (i + j + 1) * ROWS)
                score = mm_nt(k_ref[head, keys, :], query)
                if j == 0:
                    score = score + edge_ref[0]
                elif j == tiles - 1:
                    score = score + edge_ref[1]
                elif j == tiles // 2:
                    score = score + diag_ref[rows, :]
                weight = jnp.exp2(score)
                dscore = (weight * mm_nt(v_ref[head, keys, :], dout)).astype(bf16)
                dval_ref[keys, :] += mm(weight.astype(bf16), dout)
                dkey_ref[keys, :] += mm(dscore, query)
                dqt = dqt + mm(kt_ref[:, keys], dscore)
            dqt_ref[:, rows] = dqt

        dquery = dqt_ref[...].T
        base = query_extra(ids_ref[...])
        same = jnp.sum(dquery * base, axis=0, keepdims=True)
        every = jnp.sum(dquery, axis=0, keepdims=True)
        bias_ref[pl.ds(2 * head, 1), :] = same
        bias_ref[pl.ds(2 * head + 1, 1), :] = every

        @pl.when(head == 0)
        def _():
            dq_ref[...] = (dquery * 0.125).astype(bf16)
            dk_ref[...] = (dkey_ref[...] * (1.0 / LOG2E)).astype(bf16)
            dv_ref[...] = dval_ref[...].astype(bf16)

        @pl.when(head == 1)
        def _():
            def join(ref, rows, values):
                lane = lane_of(values.shape)
                kept = ref[rows, :].astype(f32)
                ref[rows, :] = jnp.where(lane < 64, kept, pltpu.roll(values, 64, 1)).astype(bf16)

            join(dq_ref, slice(0, tok), dquery * 0.125)
            for t in range(ext // ROWS):
                rows = slice(t * ROWS, t * ROWS + ROWS)
                join(dk_ref, rows, dkey_ref[rows, :] * (1.0 / LOG2E))
                join(dv_ref, rows, dval_ref[rows, :])

        return carry

    lax.fori_loop(0, 2, one_head, 0)


def attend_back(q, k, v, o, do, ids):
    heads, tok, _ = q.shape
    ext = k.shape[1]
    pair = lambda p: (p, 0, 0)
    cols = lambda p: (0, p)
    return pl.pallas_call(
        attend_back_kernel,
        name="attend_back",
        grid=(heads // 2,),
        in_specs=[
            pl.BlockSpec((2, tok, 128), pair),
            pl.BlockSpec((2, ext, 128), pair),
            pl.BlockSpec((2, ext, 128), pair),
            pl.BlockSpec((tok, 128), cols),
            pl.BlockSpec((tok, 128), cols),
            whole(ids.shape),
        ],
        out_specs=[
            pl.BlockSpec((tok, 128), cols),
            pl.BlockSpec((ext, 128), cols),
            pl.BlockSpec((ext, 128), cols),
            pl.BlockSpec((8, 128), lambda p: (p, 0)),
        ],
        out_shape=[
            shape_of((tok, heads * 64), bf16),
            shape_of((ext, heads * 64), bf16),
            shape_of((ext, heads * 64), bf16),
            shape_of((heads // 2 * 8, 128), f32),
        ],
        scratch_shapes=[
            pltpu.VMEM((tok, ROWS), f32),
            pltpu.VMEM((2, ROWS, ROWS), f32),
            pltpu.VMEM((128, ext), bf16),
            pltpu.VMEM((ext, 128), f32),
            pltpu.VMEM((ext, 128), f32),
            pltpu.VMEM((tok, 128), bf16),
            pltpu.VMEM((128, tok), f32),
        ],
        compiler_params=params(),
        cost_estimate=cost(71),
    )(q, k, v, o, do, ids)


def branch_kernel(o_ref, x_ref, w_ref, gain_ref, ids_ref, h_ref, n2_ref, sum_ref):
    branch = mm(o_ref[...], part(w_ref, 0, w_ref.shape[1]))
    h = x_ref[...].astype(f32) + branch
    h_ref[...] = h
    factor = lax.rsqrt(jnp.mean(h * h, axis=-1, keepdims=True) + EPS)
    n2_ref[...] = (h * factor * gain_ref[...]).astype(bf16)

    @pl.when(pl.program_id(0) == 0)
    def _():
        sum_ref[...] = jnp.zeros_like(sum_ref)

    sum_ref[...] += fold_rows(branch * branch * flag(ids_ref))


def branch_forward(o, x, w, w_spec, gain, ids):
    tok, width = x.shape
    row = lambda i: (i, 0)
    return pl.pallas_call(
        branch_kernel,
        name="branch",
        grid=(tok // ROWS,),
        in_specs=[
            pl.BlockSpec((ROWS, width), row),
            pl.BlockSpec((ROWS, width), row),
            w_spec,
            whole((1, width)),
            pl.BlockSpec((ROWS, ids.shape[1]), row),
        ],
        out_specs=[
            pl.BlockSpec((ROWS, width), row),
            pl.BlockSpec((ROWS, width), row),
            pl.BlockSpec((8, width), lambda i: (0, 0)),
        ],
        out_shape=[
            shape_of((tok, width), f32),
            shape_of((tok, width), bf16),
            shape_of((8, width), f32),
        ],
        compiler_params=params(),
        cost_estimate=cost(7),
    )(o, x, w, gain, ids)


def ffn_grads_kernel(
    places, n2_ref, dy_ref, wg_ref, wu_ref, wd_ref,
    hidden_ref, dgate_ref, dup_ref, out_ref,
    n2t_ref, gate_stage, up_stage, down_stage, sems,
):
    j = pl.program_id(0)
    last = pl.num_programs(0) - 1
    slot = lax.rem(j, 2)

    def copies(which, at):
        stages = (gate_stage, up_stage, down_stage)
        return [
            pltpu.make_async_copy(stage.at[at], out_ref.at[place], sems.at[index, at])
            for index, (stage, place) in enumerate(zip(stages, places(which)))
        ]

    @pl.when(j == 0)
    def _():
        n2t_ref[...] = n2_ref[...].T

    width = n2_ref.shape[1]
    n2 = n2_ref[...]
    dy = dy_ref[...]
    wd = wd_ref[...].reshape(FF_TILE, width)
    gate = mm(n2, wg_ref[...].reshape(width, FF_TILE))
    up = mm(n2, wu_ref[...].reshape(width, FF_TILE))
    dhid = mm_nt(dy, wd)
    sig = 1.0 / (1.0 + jnp.exp(-gate))
    act = gate * sig
    hidden = (act * up).astype(bf16)
    dgate = (dhid * up * sig * (1.0 + gate * (1.0 - sig))).astype(bf16)
    dup = (dhid * act).astype(bf16)
    hidden_ref[...] = hidden
    dgate_ref[...] = dgate
    dup_ref[...] = dup

    @pl.when(j >= 2)
    def _():
        for copy in copies(j - 2, slot):
            copy.wait()

    n2t = n2t_ref[...]
    gate_stage[slot] = mm(n2t, dgate).astype(bf16).reshape(gate_stage.shape[1:])
    up_stage[slot] = mm(n2t, dup).astype(bf16).reshape(up_stage.shape[1:])
    down_stage[slot] = mm_tn(hidden, dy).astype(bf16).reshape(down_stage.shape[1:])
    for copy in copies(j, slot):
        copy.start()

    @pl.when(j == last)
    def _():
        for copy in copies(j - 1, 1 - slot):
            copy.wait()
        for copy in copies(j, slot):
            copy.wait()


def ffn_sums_kernel(hidden_ref, dgate_ref, dup_ref, wg_ref, wu_ref, wd_ref, f_ref, dn2_ref):
    width = f_ref.shape[1]
    wg = wg_ref[...].reshape(width, FF_TILE)
    wu = wu_ref[...].reshape(width, FF_TILE)
    wd = wd_ref[...].reshape(FF_TILE, width)

    @pl.when(pl.program_id(0) == 0)
    def _():
        f_ref[...] = jnp.zeros_like(f_ref)
        dn2_ref[...] = jnp.zeros_like(dn2_ref)

    f_ref[...] += mm(hidden_ref[...], wd)
    dn2_ref[...] += mm_nt(dgate_ref[...], wg) + mm_nt(dup_ref[...], wu)


def ffn_blocks(width, devices, rows, blocks):
    parts = width // FF_TILE
    down_rows = blocks * rows
    if devices > 1:
        down_block = (FF_TILE // down_rows, down_rows, width)
        down_map = lambda j: (j, 0, 0)
    else:
        down_block = (1, FF_TILE, width)
        down_map = lambda j: (0, j, 0)
    side_block = (devices, rows, FF_TILE)
    specs = [
        pl.BlockSpec(side_block, lambda j: (0, blocks + j // parts, j % parts)),
        pl.BlockSpec(side_block, lambda j: (0, 2 * blocks + j // parts, j % parts)),
        pl.BlockSpec(down_block, down_map),
    ]
    return specs, side_block, down_block


def ffn_grads(n2, dy, w, devices, rows, blocks):
    tok, width = n2.shape
    ff = blocks * width
    parts = width // FF_TILE
    down_rows = blocks * rows
    w_specs, side_block, down_block = ffn_blocks(width, devices, rows, blocks)

    def places(j):
        cols = pl.ds(pl.multiple_of(lax.rem(j, parts) * FF_TILE, FF_TILE), FF_TILE)
        first = pl.multiple_of(down_rows + (j // parts) * rows, rows)
        second = pl.multiple_of(2 * down_rows + (j // parts) * rows, rows)
        if devices > 1:
            down_at = (pl.ds(j * down_block[0], down_block[0]), pl.ds(0, down_rows))
        else:
            down_at = (slice(None), pl.ds(pl.multiple_of(j * FF_TILE, FF_TILE), FF_TILE))
        return (slice(None), pl.ds(first, rows), cols), (slice(None), pl.ds(second, rows), cols), down_at

    tile = pl.BlockSpec((tok, FF_TILE), lambda j: (0, j))
    return pl.pallas_call(
        functools.partial(ffn_grads_kernel, places),
        name="ffn_grads",
        grid=(ff // FF_TILE,),
        in_specs=[whole((tok, width)), whole((tok, width))] + w_specs,
        out_specs=[tile, tile, tile, pl.BlockSpec(memory_space=pl.ANY)],
        out_shape=[shape_of((tok, ff), bf16)] * 3 + [shape_of((devices, 3 * down_rows, width), bf16)],
        scratch_shapes=[
            pltpu.VMEM((width, tok), bf16),
            pltpu.VMEM((2,) + side_block, bf16),
            pltpu.VMEM((2,) + side_block, bf16),
            pltpu.VMEM((2,) + down_block, bf16),
            pltpu.SemaphoreType.DMA((3, 2)),
        ],
        compiler_params=params(60),
        cost_estimate=cost(50),
    )(n2, dy, w, w, w)


def ffn_sums(hidden, dgate, dup, w, devices, rows, blocks):
    tok, ff = hidden.shape
    width = ff // blocks
    w_specs, _, _ = ffn_blocks(width, devices, rows, blocks)
    tile = pl.BlockSpec((tok, FF_TILE), lambda j: (0, j))
    return pl.pallas_call(
        ffn_sums_kernel,
        name="ffn_sums",
        grid=(ff // FF_TILE,),
        in_specs=[tile, tile, tile] + w_specs,
        out_specs=[whole((tok, width)), whole((tok, width))],
        out_shape=[shape_of((tok, width), f32)] * 2,
        compiler_params=params(60),
        cost_estimate=cost(25),
    )(hidden, dgate, dup, w, w, w)


def residual_back_kernel(
    h_ref, f_ref, dn2_ref, dy_ref, o_ref, w_ref, gain_ref, ids_ref,
    out_ref, dh_ref, do_ref, sum_ref, *refs,
):
    dw_refs, acc_ref = refs[:-1], refs[-1]
    step = pl.program_id(0)
    h = h_ref[...]
    f = f_ref[...]
    y = h + f
    out_ref[...] = y.astype(bf16)
    valid = flag(ids_ref)
    factor = lax.rsqrt(jnp.mean(h * h, axis=-1, keepdims=True) + EPS)
    unit = h * factor
    dn2 = dn2_ref[...]
    dunit = dn2 * gain_ref[...]
    inner = jnp.mean(dunit * unit, axis=-1, keepdims=True)
    dh = dy_ref[...].astype(f32) + factor * (dunit - unit * inner)
    dh_ref[...] = dh
    da = dh.astype(bf16)
    do_ref[...] = mm_nt(da, part(w_ref, 0, w_ref.shape[1])).astype(bf16)

    @pl.when(step == 0)
    def _():
        sum_ref[...] = jnp.zeros_like(sum_ref)
        acc_ref[...] = jnp.zeros_like(acc_ref)

    sum_ref[0] += fold_rows(y * y * valid)
    sum_ref[1] += fold_rows(f * f * valid)
    sum_ref[2] += fold_rows(dn2 * unit)
    acc_ref[...] += mm_tn(o_ref[...], da).reshape(acc_ref.shape)

    @pl.when(step == pl.num_programs(0) - 1)
    def _():
        put_grads(dw_refs, acc_ref, 0)


def residual_back(h, f, dn2, dy, o, w, w_spec, gain, ids, grad_shape):
    chips, cores, rows_each, _ = grad_shape
    tok, width = h.shape
    row = lambda i: (i, 0)
    rows = pl.BlockSpec((ROWS, width), row)
    return pl.pallas_call(
        residual_back_kernel,
        name="residual_back",
        grid=(tok // ROWS,),
        in_specs=[
            rows, rows, rows, rows, rows, w_spec, whole((1, width)),
            pl.BlockSpec((ROWS, ids.shape[1]), row),
        ],
        out_specs=[
            rows,
            rows,
            rows,
            pl.BlockSpec((3, 8, width), lambda i: (0, 0, 0)),
        ]
        + [whole((chips, rows_each, width))] * cores,
        out_shape=[
            shape_of((tok, width), bf16),
            shape_of((tok, width), f32),
            shape_of((tok, width), bf16),
            shape_of((3, 8, width), f32),
        ]
        + [shape_of((chips, rows_each, width), bf16)] * cores,
        scratch_shapes=[pltpu.VMEM(grad_shape, f32)],
        compiler_params=params(),
        cost_estimate=cost(13),
    )(h, f, dn2, dy, o, w, gain, ids)


def project_back_kernel(
    own_first, own_last, cores,
    dq_ref, dk_ref, dv_ref, q0_ref, k0_ref, n1_ref, x_ref, cos_ref, sin_ref, gq_ref, gk_ref, *refs,
):
    w_refs, (dn1_ref, gain_ref, rows_ref), refs = refs[:cores], refs[cores : cores + 3], refs[cores + 3 :]
    dw_refs, (accq_ref, acck_ref, accv_ref, low_ref, full_ref) = refs[:cores], refs[cores:]
    step = pl.program_id(0)

    @pl.when(step == 0)
    def _():
        fill_weights(full_ref, w_refs)
        accq_ref[...] = jnp.zeros_like(accq_ref)
        acck_ref[...] = jnp.zeros_like(acck_ref)
        accv_ref[...] = jnp.zeros_like(accv_ref)
        gain_ref[...] = jnp.zeros_like(gain_ref)
        rows_ref[...] = jnp.zeros_like(rows_ref)

    ones = head_ones()
    cosine = cos_ref[...]
    sine = sin_ref[...]
    n1 = n1_ref[...]
    n1t = n1.T
    pairs = n1.shape[1] // 128

    def through_norm(grad_ref, raw_ref, gain, index):
        for pair in range(pairs):
            cols = slice(pair * 128, pair * 128 + 128)
            grad = grad_ref[:, cols].astype(f32)
            grad = grad * cosine - swap_halves(grad) * sine
            raw = raw_ref[:, cols]
            factor = lax.rsqrt(head_mean(raw * raw, ones) + EPS)
            unit = raw * factor
            gain_ref[index, :, cols] += fold_rows(grad * unit)
            dunit = grad * gain
            inner = head_mean(dunit * unit, ones)
            low_ref[:, cols] = (factor * (dunit - unit * inner)).astype(bf16)
        return low_ref[...]

    dk0 = through_norm(dk_ref, k0_ref, gk_ref[...], 1)
    dv = dv_ref[...]
    acck_ref[...] += mm(n1t, dk0).reshape(acck_ref.shape)
    accv_ref[...] += mm(n1t, dv).reshape(accv_ref.shape)
    dn1_ref[...] = mm_nt(dk0, weight(full_ref, 1)) + mm_nt(dv, weight(full_ref, 2))

    @pl.when((step >= own_first) & (step < own_last))
    def _():
        dq0 = through_norm(dq_ref, q0_ref, gq_ref[...], 0)
        accq_ref[...] += mm(n1t, dq0).reshape(accq_ref.shape)
        dn1_ref[...] += mm_nt(dq0, weight(full_ref, 0))

    x = x_ref[...].astype(f32)
    unit = x * lax.rsqrt(jnp.mean(x * x, axis=-1, keepdims=True) + EPS)
    rows_ref[...] += fold_rows(dn1_ref[...] * unit)

    @pl.when(step == pl.num_programs(0) - 1)
    def _():
        for index, ref in enumerate((accq_ref, acck_ref, accv_ref)):
            put_grads(dw_refs, ref, index * ref.shape[2])


def project_back(dq, dk, dv, q0, k0, n1, x_ext, cosine, sine, gq, gk, w, w_rows):
    ext, width = n1.shape
    tok = dq.shape[0]
    own_first = HALF // ROWS
    own_last = own_first + tok // ROWS
    acc_shape = (w[0].shape[0], len(w), w_rows, width)
    row = lambda i: (i, 0)
    own = lambda i: (jnp.clip(i - own_first, 0, own_last - own_first - 1), 0)
    return pl.pallas_call(
        functools.partial(project_back_kernel, own_first, own_last, len(w)),
        name="project_back",
        grid=(ext // ROWS,),
        in_specs=[
            pl.BlockSpec((ROWS, width), own),
            pl.BlockSpec((ROWS, width), row),
            pl.BlockSpec((ROWS, width), row),
            pl.BlockSpec((ROWS, width), own),
            pl.BlockSpec((ROWS, width), row),
            pl.BlockSpec((ROWS, width), row),
            pl.BlockSpec((ROWS, width), row),
            pl.BlockSpec((ROWS, 128), row),
            pl.BlockSpec((ROWS, 128), row),
            whole((1, 128)),
            whole((1, 128)),
        ]
        + [whole(each.shape) for each in w],
        out_specs=[
            pl.BlockSpec((ROWS, width), row),
            whole((2, 8, width)),
            whole((8, width)),
        ]
        + [whole(each.shape) for each in w],
        out_shape=[
            shape_of((ext, width), f32),
            shape_of((2, 8, width), f32),
            shape_of((8, width), f32),
        ]
        + [shape_of(each.shape, bf16) for each in w],
        scratch_shapes=[pltpu.VMEM(acc_shape, f32)] * 3 + [pltpu.VMEM((ROWS, width), bf16), full_weights(w, w_rows)],
        compiler_params=params(60),
        cost_estimate=cost(41),
    )(dq, dk, dv, q0, k0, n1, x_ext, cosine, sine, gq, gk, *w)


def local(
    inputs, seg_ids, var_ids, time_ids, valid_mask,
    w_query, w_key, w_value, w_out, w_gate, w_up, w_down,
    gain_attn, gain_ffn, gain_query, gain_key, variate_bias, out_grad,
):
    axes = ("head", "chip", "core")
    head_count, chip_count, core_count = (lax.axis_size(axis) for axis in axes)
    blk_count = chip_count * core_count
    devices = head_count * blk_count
    chips = head_count * chip_count
    tok, width = inputs.shape[1:]
    heads = variate_bias.shape[1]
    head_dim = gain_query.shape[0]
    rows = w_query.shape[0]
    blocks = w_gate.shape[1] // width
    ext = tok + 2 * HALF
    blk = lax.axis_index("chip") * core_count + lax.axis_index("core")
    place = blk * head_count + lax.axis_index("head")
    fast = rows % 16 == 0
    k_cores, k_devices, k_rows = (core_count, devices, rows) if fast else (1, 1, width)
    k_chips = k_devices // k_cores

    def flat(p):
        return (p % head_count) * blk_count + p // head_count

    onward = [(flat(p), flat(p + 1)) for p in range(devices - 1)]
    back = [(b, a) for a, b in onward]

    def exchange(values, axis):
        return lax.all_to_all(values, axis, split_axis=0, concat_axis=0, tiled=True)

    def swap_cores(values):
        return lax.ppermute(values, "core", [(0, 1), (1, 0)])

    def spread(shard, axis, count):
        return exchange(jnp.broadcast_to(shard[None], (count,) + shard.shape), axis)

    def spread_to_all(full, parts):
        full = spread(full, "head", head_count).reshape(chips, parts * rows, width)
        other = swap_cores(full)
        if fast:
            return [full, other]
        swapped = lax.axis_index("core") == 1
        both = jnp.stack([jnp.where(swapped, other, full), jnp.where(swapped, full, other)])
        pieces = both.reshape(core_count, chips, parts, rows, width).transpose(2, 1, 0, 3, 4)
        return [pieces.reshape(1, parts * width, width)]

    def total(values):
        return jnp.sum(values.astype(f32), axis=0)

    def reduce_cores(grads, parts):
        if not fast:
            pieces = grads[0].reshape(parts, chips, core_count, rows, width).transpose(2, 1, 0, 3, 4)
            core = lax.axis_index("core")
            grads = [lax.dynamic_index_in_dim(pieces, at, 0, False) for at in (core, 1 - core)]
        mine, other = (each.reshape(head_count, chip_count, parts * rows, width) for each in grads)
        return (mine.astype(f32) + swap_cores(other).astype(f32)).astype(bf16)

    def reduce_heads(grads):
        return total(exchange(grads, "head")).astype(bf16)

    def reduce_chips(grads):
        return total(exchange(grads, "chip"))

    def gather_rest(shard):
        full = lax.all_gather(shard, axes, axis=0, tiled=False)
        if fast:
            return full
        parts = shard.shape[0] // rows
        down = full[:, : blocks * rows].reshape(1, blocks * width, width)
        rest = full[:, blocks * rows :].reshape(devices, parts - blocks, rows, width)
        rest = rest.transpose(1, 0, 2, 3).reshape(1, (parts - blocks) * width, width)
        return jnp.concatenate([down, rest], axis=1)

    def scatter_rest(grads):
        if not fast:
            down = grads[0, : blocks * width].reshape(devices, blocks * rows, width)
            rest = grads[0, blocks * width :].reshape(2 * blocks, devices, rows, width).transpose(1, 0, 2, 3)
            grads = jnp.concatenate([down, rest.reshape(devices, -1, width)], axis=1)
        grads = grads.reshape(devices * 3 * blocks * rows, width)
        return lax.psum_scatter(grads, axes, scatter_dimension=0, tiled=True).astype(f32)

    def columns(shard):
        return [shard[:, i * width : (i + 1) * width] for i in range(blocks)]

    def sides(owned):
        return jnp.concatenate([owned[i * rows : (i + 1) * rows] for i in range(blocks)], axis=1)

    rest_w = gather_rest(jnp.concatenate([w_down] + columns(w_gate) + columns(w_up) + [w_out], axis=0))
    x = inputs[0]
    before = lax.ppermute(x[tok - HALF :], axes, onward)
    after = lax.ppermute(x[:HALF], axes, back)
    attn_w = spread(jnp.concatenate([w_query, w_key, w_value], axis=0), "chip", chip_count)
    attn_w, before, after = lax.optimization_barrier((attn_w, before, after))
    attn_w = spread_to_all(attn_w, 3)
    x_ext = jnp.concatenate([before, x, after], axis=0)

    ids = jnp.stack([seg_ids, var_ids, valid_mask, time_ids]).reshape(4, -1)
    ids = jnp.pad(ids, ((0, 0), (HALF, HALF)))
    ids = lax.dynamic_slice_in_dim(ids, place * tok, ext, 1).T
    own = slice(HALF, HALF + tok)
    own_ids = ids[own]
    quarter = jnp.arange(128) % (head_dim // 2)
    frequency = 10000.0 ** (-quarter.astype(f32) * 2.0 / head_dim)
    angles = ids[:, 3:].astype(f32) * frequency[None, :]
    cosine = jnp.cos(angles)
    sine = jnp.sin(angles) * jnp.where(jnp.arange(128) % head_dim < head_dim // 2, -1.0, 1.0)
    diff = (variate_bias[0] - variate_bias[1]) * LOG2E
    diff_high = lax.reduce_precision(diff, 8, 7)
    diff_low = diff - diff_high
    lane = jnp.arange(128)[None, :]
    diff_rows = jnp.where(lane < LANE_LOW, diff_high[:, None], jnp.where(lane < LANE_CODE, diff_low[:, None], 1.0))
    gq = jnp.tile(gain_query, 2)[None]
    gk = jnp.tile(gain_key, 2)[None]

    n1, q0, k0, q, k, v = project(
        x_ext, gain_attn[None], attn_w, k_rows, cosine, sine, gq, gk, ids, diff_rows, tok, heads
    )
    o, qb = attend(q, k, v, own_ids)

    out_spec = pl.BlockSpec((k_devices, k_rows, width), lambda i: (0, 3 * blocks, 0), pipeline_mode=pl.Buffered(1))
    h, n2, branch_sum = branch_forward(o, x, rest_w, out_spec, gain_ffn[None], own_ids)
    dy = out_grad[0]
    hidden, dgate, dup, ff_grads = ffn_grads(n2, dy, rest_w, k_devices, k_rows, blocks)
    ff_owned = scatter_rest(ff_grads)
    f, dn2 = ffn_sums(hidden, dgate, dup, rest_w, k_devices, k_rows, blocks)
    layer_out, dh, do, sums, *out_grads = residual_back(
        h, f, dn2, dy, o, rest_w, out_spec, gain_ffn[None], own_ids, (k_chips, k_cores, k_rows, width)
    )
    early = reduce_cores(out_grads, 1)
    do, early = lax.optimization_barrier((do, early))
    early = reduce_heads(early)
    dq, dk, dv, bias_rows = attend_back(qb, k, v, o, do, own_ids)
    dq, early = lax.optimization_barrier((dq, early))
    early_owned = reduce_chips(early)
    dn1_ext, gain_rows, attn_rows, *attn_grads = project_back(
        dq, dk, dv, q0, k0, n1, x_ext, cosine, sine, gq, gk, attn_w, k_rows
    )
    attn_grads, early_owned = lax.optimization_barrier((attn_grads, early_owned))
    attn_owned = reduce_chips(reduce_heads(reduce_cores(attn_grads, 3)))

    from_left = lax.ppermute(dn1_ext[HALF + tok :].astype(bf16), axes, onward)
    from_right = lax.ppermute(dn1_ext[:HALF].astype(bf16), axes, back)
    dn1 = (
        dn1_ext[own]
        + jnp.pad(from_left.astype(f32), ((0, tok - HALF), (0, 0)))
        + jnp.pad(from_right.astype(f32), ((tok - HALF, 0), (0, 0)))
    )
    x_float = x.astype(f32)
    factor = lax.rsqrt(jnp.mean(x_float * x_float, axis=-1, keepdims=True) + EPS)
    unit = x_float * factor
    dunit = dn1 * gain_attn
    inner = jnp.mean(dunit * unit, axis=-1, keepdims=True)
    grad_inputs = (dh + factor * (dunit - unit * inner)).astype(bf16)
    grad_gain_attn = attn_rows.sum(0)

    bias_rows = bias_rows.reshape(heads // 2, 8, 128)[:, :4].reshape(heads, 2, 128)[:, :, 64 : 64 + VARS].sum(-1)
    bias_grad = jnp.stack([bias_rows[:, 0], bias_rows[:, 1] - bias_rows[:, 0]])
    gain_heads = gain_rows.sum(1).reshape(2, heads, head_dim).sum(1)
    squares = jnp.stack([sums[0].sum(), branch_sum.sum(), sums[1].sum()])
    small = jnp.concatenate(
        [grad_gain_attn, sums[2].sum(0), gain_heads.reshape(-1), bias_grad.reshape(-1), squares]
    )
    filled = -small.shape[0] % 1024
    small = jnp.pad(small, (0, filled)).reshape(-1, 128)
    for axis, count in (("core", core_count), ("head", head_count), ("chip", chip_count)):
        small = total(exchange(jnp.broadcast_to(small[None], (count,) + small.shape), axis))
    small = small.reshape(-1)
    at = 2 * width
    valid_count = jnp.maximum(jnp.sum((valid_mask == 1).astype(f32)), 1.0)
    rms_values = jnp.sqrt(small[at + 2 * head_dim + 2 * heads :][:3] / (valid_count * width))

    return (
        layer_out[None],
        grad_inputs[None],
        attn_owned[:rows],
        attn_owned[rows : 2 * rows],
        attn_owned[2 * rows :],
        early_owned,
        sides(ff_owned[blocks * rows : 2 * blocks * rows]),
        sides(ff_owned[2 * blocks * rows :]),
        ff_owned[: blocks * rows],
        small[:width],
        small[width : 2 * width],
        small[at : at + head_dim],
        small[at + head_dim : at + 2 * head_dim],
        small[at + 2 * head_dim : at + 2 * head_dim + 2 * heads].reshape(2, heads),
        rms_values,
    )


def solution(mesh):
    heads, blks = mesh.devices.shape
    cores = 2 if blks % 2 == 0 else 1
    mesh = Mesh(mesh.devices.reshape(heads, blks // cores, cores), ("head", "chip", "core"))
    tokens = P(("chip", "core"), "head", None)
    weights = P(("head", "chip", "core"), None)
    in_specs = (tokens,) + (P(),) * 4 + (weights,) * 7 + (P(),) * 5 + (tokens,)
    out_specs = (tokens,) * 2 + (weights,) * 7 + (P(),) * 6
    return jax.shard_map(local, mesh=mesh, in_specs=in_specs, out_specs=out_specs, check_vma=False)
```

```python
import functools

import jax
import jax.numpy as jnp
from jax import lax
from jax.experimental import pallas as pl
from jax.experimental.pallas import tpu as pltpu
from jax.sharding import Mesh
from jax.sharding import PartitionSpec as P

HALF = 512
ROWS = 256
FF_TILE = 512
VARS = 8
CODES = 8
CODE_SIZE = 64.0
OUTSIDE = 256.0
LOG2E = 1.4426950408889634
EPS = 1e-05
MIB = 1 << 20

LANE_HIGH = 64
LANE_LOW = 72
LANE_CODE = 80
LANE_ONE = 88
LANE_LSE = 90

SEG, VAR, VALID = 0, 1, 2

f32 = jnp.float32
bf16 = jnp.bfloat16
shape_of = jax.ShapeDtypeStruct


def mm(a, b):
    return lax.dot_general(a, b, (((1,), (0,)), ((), ())), preferred_element_type=f32)


def mm_nt(a, b):
    return lax.dot_general(a, b, (((1,), (1,)), ((), ())), preferred_element_type=f32)


def mm_tn(a, b):
    return lax.dot_general(a, b, (((0,), (0,)), ((), ())), preferred_element_type=f32)


def params(vmem=56):
    return pltpu.CompilerParams(vmem_limit_bytes=vmem * MIB)


def cost(us):
    return pl.CostEstimate(flops=int(us * 1e9), bytes_accessed=1 << 20, transcendentals=0)


def whole(shape):
    return pl.BlockSpec(shape, lambda *_: (0,) * len(shape), pipeline_mode=pl.Buffered(1))


def lane_of(shape):
    return lax.broadcasted_iota(jnp.int32, shape, len(shape) - 1)


def row_of(shape):
    return lax.broadcasted_iota(jnp.int32, shape, len(shape) - 2)


def head_ones():
    shape = (128, 128)
    return jnp.where((row_of(shape) // 64) == (lane_of(shape) // 64), 1.0, 0.0).astype(bf16)


def head_mean(values, ones):
    high = values.astype(bf16)
    low = (values - high.astype(f32)).astype(bf16)
    return (mm(high, ones) + mm(low, ones)) * (1.0 / 64.0)


def swap_halves(values):
    first = (lane_of(values.shape) % 64) < 32
    return jnp.where(first, pltpu.roll(values, 96, 1), pltpu.roll(values, 32, 1))


def fold_rows(values):
    rows, width = values.shape
    return jnp.sum(values.reshape(rows // 8, 8, width), axis=0)


def flag(ids_ref, rows=slice(None)):
    return jnp.where(ids_ref[rows, VALID : VALID + 1] == 1, 1.0, 0.0)


def key_extra(ids):
    lane = lane_of((ids.shape[0], 128))
    var = ids[:, VAR : VAR + 1]
    seg = ids[:, SEG : SEG + 1]
    invalid = jnp.where(ids[:, VALID : VALID + 1] == 1, 0.0, 1.0)
    bit = jnp.right_shift(seg, jnp.clip(lane - LANE_CODE, 0, CODES - 1)) & 1
    extra = jnp.where((var == lane - LANE_HIGH) | (var == lane - LANE_LOW) & (lane >= LANE_LOW), 1.0, 0.0)
    extra = jnp.where(lane >= LANE_CODE, CODE_SIZE * (2 * bit - 1).astype(f32), extra)
    extra = jnp.where(lane >= LANE_ONE, -CODE_SIZE * (CODES + 2.0 * invalid), extra)
    extra = jnp.where(lane > LANE_ONE, jnp.where((lane >= LANE_LSE) & (lane < LANE_LSE + 3), 1.0, 0.0), extra)
    return extra


def query_extra(ids):
    lane = lane_of((ids.shape[0], 128))
    var = ids[:, VAR : VAR + 1]
    seg = ids[:, SEG : SEG + 1]
    bit = jnp.right_shift(seg, jnp.clip(lane - LANE_CODE, 0, CODES - 1)) & 1
    extra = jnp.where((var == lane - LANE_HIGH) | (var == lane - LANE_LOW) & (lane >= LANE_LOW), 1.0, 0.0)
    extra = jnp.where(lane >= LANE_CODE, (2 * bit - 1).astype(f32), extra)
    return jnp.where(lane >= LANE_ONE, jnp.where(lane == LANE_ONE, 1.0, 0.0), extra)


def part(ref, index, rows):
    block = ref[:, index * rows : (index + 1) * rows, :]
    return block.reshape(block.shape[0] * rows, block.shape[2])


def core_at(slot, cores):
    if cores == 1:
        return 0
    own = lax.axis_index("core")
    return own if slot == 0 else 1 - own


def fill_weights(full_ref, w_refs):
    parts, _, cores, rows, _ = full_ref.shape
    for slot in range(cores):
        for index in range(parts):
            full_ref[index, :, core_at(slot, cores)] = w_refs[slot][:, index * rows : (index + 1) * rows, :]


def weight(full_ref, index):
    width = full_ref.shape[4]
    return full_ref[index].reshape(width, width)


def put_grads(out_refs, acc_ref, first):
    _, cores, rows, _ = acc_ref.shape
    for slot in range(cores):
        out_refs[slot][:, first : first + rows, :] = acc_ref[:, core_at(slot, cores)].astype(bf16)


def project_kernel(
    own_first, own_last, cores,
    x_ref, gain_ref, cos_ref, sin_ref, gq_ref, gk_ref, ids_ref, diff_ref, *refs,
):
    w_refs = refs[:cores]
    n1_ref, q0_ref, k0_ref, q_ref, k_ref, v_ref, full_ref = refs[cores:]
    step = pl.program_id(0)

    @pl.when(step == 0)
    def _():
        fill_weights(full_ref, w_refs)

    x = x_ref[...].astype(f32)
    factor = lax.rsqrt(jnp.mean(x * x, axis=-1, keepdims=True) + EPS)
    n1 = (x * factor * gain_ref[...]).astype(bf16)
    n1_ref[...] = n1
    ones = head_ones()
    cosine = cos_ref[...]
    sine = sin_ref[...]
    kaug = key_extra(ids_ref[...])
    own_lane = lane_of(kaug.shape) < 64
    pairs = x.shape[1] // 128

    k0 = mm(n1, weight(full_ref, 1))
    k0_ref[...] = k0
    value = mm(n1, weight(full_ref, 2))
    vaug = jnp.where(lane_of(kaug.shape) < 67, 1.0, 0.0)
    for pair in range(pairs):
        cols = slice(pair * 128, pair * 128 + 128)
        raw = k0[:, cols]
        normed = raw * lax.rsqrt(head_mean(raw * raw, ones) + EPS) * gk_ref[...]
        turned = normed * cosine + swap_halves(normed) * sine
        k_ref[2 * pair] = jnp.where(own_lane, turned, kaug).astype(bf16)
        k_ref[2 * pair + 1] = jnp.where(own_lane, pltpu.roll(turned, 64, 1), kaug).astype(bf16)
        val = value[:, cols]
        v_ref[2 * pair] = jnp.where(own_lane, val, vaug).astype(bf16)
        v_ref[2 * pair + 1] = jnp.where(own_lane, pltpu.roll(val, 64, 1), vaug).astype(bf16)

    @pl.when((step >= own_first) & (step < own_last))
    def _():
        q0 = mm(n1, weight(full_ref, 0))
        q0_ref[...] = q0
        qaug = query_extra(ids_ref[...])
        for pair in range(pairs):
            raw = q0[:, pair * 128 : pair * 128 + 128]
            normed = raw * lax.rsqrt(head_mean(raw * raw, ones) + EPS) * gq_ref[...]
            turned = (normed * cosine + swap_halves(normed) * sine) * (0.125 * LOG2E)
            first = qaug * diff_ref[2 * pair : 2 * pair + 1, :]
            second = qaug * diff_ref[2 * pair + 1 : 2 * pair + 2, :]
            q_ref[2 * pair] = jnp.where(own_lane, turned, first).astype(bf16)
            q_ref[2 * pair + 1] = jnp.where(own_lane, pltpu.roll(turned, 64, 1), second).astype(bf16)


def full_weights(w, rows):
    chips, total, width = w[0].shape
    return pltpu.VMEM((total // rows, chips, len(w), rows, width), bf16)


def project(x_ext, gain, w, w_rows, cosine, sine, gq, gk, ids, diff, tok, heads):
    ext, width = x_ext.shape
    own_first = HALF // ROWS
    own_last = own_first + tok // ROWS
    row = lambda i: (i, 0)
    own = lambda i: (jnp.clip(i - own_first, 0, own_last - own_first - 1), 0)
    head_row = lambda i: (0, i, 0)
    head_own = lambda i: (0, own(i)[0], 0)
    return pl.pallas_call(
        functools.partial(project_kernel, own_first, own_last, len(w)),
        name="project",
        grid=(ext // ROWS,),
        in_specs=[
            pl.BlockSpec((ROWS, width), row),
            whole((1, width)),
            pl.BlockSpec((ROWS, 128), row),
            pl.BlockSpec((ROWS, 128), row),
            whole((1, 128)),
            whole((1, 128)),
            pl.BlockSpec((ROWS, ids.shape[1]), row),
            whole(diff.shape),
        ]
        + [whole(each.shape) for each in w],
        out_specs=[
            pl.BlockSpec((ROWS, width), row),
            pl.BlockSpec((ROWS, width), own),
            pl.BlockSpec((ROWS, width), row),
            pl.BlockSpec((heads, ROWS, 128), head_own),
            pl.BlockSpec((heads, ROWS, 128), head_row),
            pl.BlockSpec((heads, ROWS, 128), head_row),
        ],
        out_shape=[
            shape_of((ext, width), bf16),
            shape_of((tok, width), f32),
            shape_of((ext, width), f32),
            shape_of((heads, tok, 128), bf16),
            shape_of((heads, ext, 128), bf16),
            shape_of((heads, ext, 128), bf16),
        ],
        scratch_shapes=[full_weights(w, w_rows)],
        compiler_params=params(),
        cost_estimate=cost(27),
    )(x_ext, gain, cosine, sine, gq, gk, ids, diff, *w)


def fill_masks(ids_ref, diag_ref, edge_ref, key_axis):
    shape = (ROWS, ROWS)
    key = lax.broadcasted_iota(jnp.int32, shape, key_axis)
    query = lax.broadcasted_iota(jnp.int32, shape, 1 - key_axis)
    edge_ref[0] = jnp.where(key > query, 0.0, -OUTSIDE)
    edge_ref[1] = jnp.where(key < query, 0.0, -OUTSIDE)
    for i in range(diag_ref.shape[0] // ROWS):
        rows = slice(i * ROWS, i * ROWS + ROWS)
        diag_ref[rows, :] = jnp.where(key == query, 2.0 * CODE_SIZE * (1.0 - flag(ids_ref, rows)), 0.0)


def attend_kernel(q_ref, k_ref, v_ref, ids_ref, o_ref, qb_ref, diag_ref, edge_ref):
    @pl.when(pl.program_id(0) == 0)
    def _():
        fill_masks(ids_ref, diag_ref, edge_ref, 1)

    tiles = 1 + 2 * HALF // ROWS
    tok = q_ref.shape[1]

    def block(i, carry):
        first_row = pl.multiple_of(i * ROWS, ROWS)
        outs = []
        for head in range(2):
            query = q_ref[head, pl.ds(first_row, ROWS), :]
            total = jnp.zeros((ROWS, 128), f32)
            for j in range(tiles):
                keys = pl.ds(first_row + j * ROWS, ROWS)
                score = mm_nt(query, k_ref[head, keys, :])
                if j == 0:
                    score = score + edge_ref[0]
                elif j == tiles - 1:
                    score = score + edge_ref[1]
                elif j == tiles // 2:
                    score = score + diag_ref[pl.ds(first_row, ROWS), :]
                total = total + mm(jnp.exp2(score).astype(bf16), v_ref[head, keys, :])
            weight = total[:, 64:65]
            outs.append(total / weight)
            lse = jnp.log2(weight)
            high = lse.astype(bf16).astype(f32)
            middle = (lse - high).astype(bf16).astype(f32)
            low = lse - high - middle
            lane = lane_of((ROWS, 128))
            updated = jnp.where(lane == LANE_LSE, -high, query.astype(f32))
            updated = jnp.where(lane == LANE_LSE + 1, -middle, updated)
            updated = jnp.where(lane == LANE_LSE + 2, -low, updated)
            qb_ref[head, pl.ds(first_row, ROWS), :] = updated.astype(bf16)
        lane = lane_of((ROWS, 128))
        joined = jnp.where(lane < 64, outs[0], pltpu.roll(outs[1], 64, 1))
        o_ref[pl.ds(first_row, ROWS), :] = joined.astype(bf16)
        return carry

    lax.fori_loop(0, tok // ROWS, block, 0)


def attend(q, k, v, ids):
    heads, tok, _ = q.shape
    ext = k.shape[1]
    pair = lambda p: (p, 0, 0)
    return pl.pallas_call(
        attend_kernel,
        name="attend",
        grid=(heads // 2,),
        in_specs=[
            pl.BlockSpec((2, tok, 128), pair),
            pl.BlockSpec((2, ext, 128), pair),
            pl.BlockSpec((2, ext, 128), pair),
            whole(ids.shape),
        ],
        out_specs=[
            pl.BlockSpec((tok, 128), lambda p: (0, p)),
            pl.BlockSpec((2, tok, 128), pair),
        ],
        out_shape=[shape_of((tok, heads * 64), bf16), shape_of((heads, tok, 128), bf16)],
        scratch_shapes=[pltpu.VMEM((tok, ROWS), f32), pltpu.VMEM((2, ROWS, ROWS), f32)],
        compiler_params=params(),
        cost_estimate=cost(36),
    )(q, k, v, ids)


def attend_back_kernel(
    q_ref, k_ref, v_ref, o_ref, do_ref, ids_ref,
    dq_ref, dk_ref, dv_ref, bias_ref,
    diag_ref, edge_ref, kt_ref, dkey_ref, dval_ref, dout_ref, dqt_ref,
):
    @pl.when(pl.program_id(0) == 0)
    def _():
        fill_masks(ids_ref, diag_ref, edge_ref, 0)

    tiles = 1 + 2 * HALF // ROWS
    tok = q_ref.shape[1]
    ext = k_ref.shape[1]
    blocks = tok // ROWS

    def one_head(head, carry):
        for i in range(blocks):
            rows = slice(i * ROWS, i * ROWS + ROWS)
            lane = lane_of((ROWS, 128))
            dout = do_ref[rows, :].astype(f32)
            shift = head * 64
            dout = pltpu.roll(dout, shift, 1)
            product = pltpu.roll(o_ref[rows, :].astype(f32), shift, 1) * dout
            delta = jnp.sum(jnp.where(lane < 64, product, 0.0), axis=-1, keepdims=True)
            high = delta.astype(bf16).astype(f32)
            middle = (delta - high).astype(bf16).astype(f32)
            low = delta - high - middle
            aug = jnp.where(lane == 64, -high, jnp.where(lane == 65, -middle, jnp.where(lane == 66, -low, 0.0)))
            dout_ref[rows, :] = jnp.where(lane < 64, dout, aug).astype(bf16)
        for t in range(ext // ROWS):
            rows = slice(t * ROWS, t * ROWS + ROWS)
            kt_ref[:, rows] = k_ref[head, rows, :].T
            dkey_ref[rows, :] = jnp.zeros((ROWS, 128), f32)
            dval_ref[rows, :] = jnp.zeros((ROWS, 128), f32)

        for i in range(blocks):
            rows = slice(i * ROWS, i * ROWS + ROWS)
            query = q_ref[head, rows, :]
            dout = dout_ref[rows, :]
            dqt = jnp.zeros((128, ROWS), f32)
            for j in range(tiles):
                keys = slice((i + j) * ROWS, (i + j + 1) * ROWS)
                score = mm_nt(k_ref[head, keys, :], query)
                if j == 0:
                    score = score + edge_ref[0]
                elif j == tiles - 1:
                    score = score + edge_ref[1]
                elif j == tiles // 2:
                    score = score + diag_ref[rows, :]
                weight = jnp.exp2(score)
                dscore = (weight * mm_nt(v_ref[head, keys, :], dout)).astype(bf16)
                dval_ref[keys, :] += mm(weight.astype(bf16), dout)
                dkey_ref[keys, :] += mm(dscore, query)
                dqt = dqt + mm(kt_ref[:, keys], dscore)
            dqt_ref[:, rows] = dqt

        dquery = dqt_ref[...].T
        base = query_extra(ids_ref[...])
        same = jnp.sum(dquery * base, axis=0, keepdims=True)
        every = jnp.sum(dquery, axis=0, keepdims=True)
        bias_ref[pl.ds(2 * head, 1), :] = same
        bias_ref[pl.ds(2 * head + 1, 1), :] = every

        @pl.when(head == 0)
        def _():
            dq_ref[...] = (dquery * 0.125).astype(bf16)
            dk_ref[...] = (dkey_ref[...] * (1.0 / LOG2E)).astype(bf16)
            dv_ref[...] = dval_ref[...].astype(bf16)

        @pl.when(head == 1)
        def _():
            def join(ref, rows, values):
                lane = lane_of(values.shape)
                kept = ref[rows, :].astype(f32)
                ref[rows, :] = jnp.where(lane < 64, kept, pltpu.roll(values, 64, 1)).astype(bf16)

            join(dq_ref, slice(0, tok), dquery * 0.125)
            for t in range(ext // ROWS):
                rows = slice(t * ROWS, t * ROWS + ROWS)
                join(dk_ref, rows, dkey_ref[rows, :] * (1.0 / LOG2E))
                join(dv_ref, rows, dval_ref[rows, :])

        return carry

    lax.fori_loop(0, 2, one_head, 0)


def attend_back(q, k, v, o, do, ids):
    heads, tok, _ = q.shape
    ext = k.shape[1]
    pair = lambda p: (p, 0, 0)
    cols = lambda p: (0, p)
    return pl.pallas_call(
        attend_back_kernel,
        name="attend_back",
        grid=(heads // 2,),
        in_specs=[
            pl.BlockSpec((2, tok, 128), pair),
            pl.BlockSpec((2, ext, 128), pair),
            pl.BlockSpec((2, ext, 128), pair),
            pl.BlockSpec((tok, 128), cols),
            pl.BlockSpec((tok, 128), cols),
            whole(ids.shape),
        ],
        out_specs=[
            pl.BlockSpec((tok, 128), cols),
            pl.BlockSpec((ext, 128), cols),
            pl.BlockSpec((ext, 128), cols),
            pl.BlockSpec((8, 128), lambda p: (p, 0)),
        ],
        out_shape=[
            shape_of((tok, heads * 64), bf16),
            shape_of((ext, heads * 64), bf16),
            shape_of((ext, heads * 64), bf16),
            shape_of((heads // 2 * 8, 128), f32),
        ],
        scratch_shapes=[
            pltpu.VMEM((tok, ROWS), f32),
            pltpu.VMEM((2, ROWS, ROWS), f32),
            pltpu.VMEM((128, ext), bf16),
            pltpu.VMEM((ext, 128), f32),
            pltpu.VMEM((ext, 128), f32),
            pltpu.VMEM((tok, 128), bf16),
            pltpu.VMEM((128, tok), f32),
        ],
        compiler_params=params(),
        cost_estimate=cost(71),
    )(q, k, v, o, do, ids)


def branch_kernel(o_ref, x_ref, w_ref, gain_ref, ids_ref, h_ref, n2_ref, sum_ref):
    branch = mm(o_ref[...], part(w_ref, 0, w_ref.shape[1]))
    h = x_ref[...].astype(f32) + branch
    h_ref[...] = h
    factor = lax.rsqrt(jnp.mean(h * h, axis=-1, keepdims=True) + EPS)
    n2_ref[...] = (h * factor * gain_ref[...]).astype(bf16)

    @pl.when(pl.program_id(0) == 0)
    def _():
        sum_ref[...] = jnp.zeros_like(sum_ref)

    sum_ref[...] += fold_rows(branch * branch * flag(ids_ref))


def branch_forward(o, x, w, w_spec, gain, ids):
    tok, width = x.shape
    row = lambda i: (i, 0)
    return pl.pallas_call(
        branch_kernel,
        name="branch",
        grid=(tok // ROWS,),
        in_specs=[
            pl.BlockSpec((ROWS, width), row),
            pl.BlockSpec((ROWS, width), row),
            w_spec,
            whole((1, width)),
            pl.BlockSpec((ROWS, ids.shape[1]), row),
        ],
        out_specs=[
            pl.BlockSpec((ROWS, width), row),
            pl.BlockSpec((ROWS, width), row),
            pl.BlockSpec((8, width), lambda i: (0, 0)),
        ],
        out_shape=[
            shape_of((tok, width), f32),
            shape_of((tok, width), bf16),
            shape_of((8, width), f32),
        ],
        compiler_params=params(),
        cost_estimate=cost(7),
    )(o, x, w, gain, ids)


def ffn_grads_kernel(
    places, n2_ref, dy_ref, wg_ref, wu_ref, wd_ref,
    hidden_ref, dgate_ref, dup_ref, out_ref,
    n2t_ref, gate_stage, up_stage, down_stage, sems,
):
    j = pl.program_id(0)
    last = pl.num_programs(0) - 1
    slot = lax.rem(j, 2)

    def copies(which, at):
        stages = (gate_stage, up_stage, down_stage)
        return [
            pltpu.make_async_copy(stage.at[at], out_ref.at[place], sems.at[index, at])
            for index, (stage, place) in enumerate(zip(stages, places(which)))
        ]

    @pl.when(j == 0)
    def _():
        n2t_ref[...] = n2_ref[...].T

    width = n2_ref.shape[1]
    n2 = n2_ref[...]
    dy = dy_ref[...]
    wd = wd_ref[...].reshape(FF_TILE, width)
    gate = mm(n2, wg_ref[...].reshape(width, FF_TILE))
    up = mm(n2, wu_ref[...].reshape(width, FF_TILE))
    dhid = mm_nt(dy, wd)
    sig = 1.0 / (1.0 + jnp.exp(-gate))
    act = gate * sig
    hidden = (act * up).astype(bf16)
    dgate = (dhid * up * sig * (1.0 + gate * (1.0 - sig))).astype(bf16)
    dup = (dhid * act).astype(bf16)
    hidden_ref[...] = hidden
    dgate_ref[...] = dgate
    dup_ref[...] = dup

    @pl.when(j >= 2)
    def _():
        for copy in copies(j - 2, slot):
            copy.wait()

    n2t = n2t_ref[...]
    gate_stage[slot] = mm(n2t, dgate).astype(bf16).reshape(gate_stage.shape[1:])
    up_stage[slot] = mm(n2t, dup).astype(bf16).reshape(up_stage.shape[1:])
    down_stage[slot] = mm_tn(hidden, dy).astype(bf16).reshape(down_stage.shape[1:])
    for copy in copies(j, slot):
        copy.start()

    @pl.when(j == last)
    def _():
        for copy in copies(j - 1, 1 - slot):
            copy.wait()
        for copy in copies(j, slot):
            copy.wait()


def ffn_sums_kernel(hidden_ref, dgate_ref, dup_ref, wg_ref, wu_ref, wd_ref, f_ref, dn2_ref):
    width = f_ref.shape[1]
    wg = wg_ref[...].reshape(width, FF_TILE)
    wu = wu_ref[...].reshape(width, FF_TILE)
    wd = wd_ref[...].reshape(FF_TILE, width)

    @pl.when(pl.program_id(0) == 0)
    def _():
        f_ref[...] = jnp.zeros_like(f_ref)
        dn2_ref[...] = jnp.zeros_like(dn2_ref)

    f_ref[...] += mm(hidden_ref[...], wd)
    dn2_ref[...] += mm_nt(dgate_ref[...], wg) + mm_nt(dup_ref[...], wu)


def ffn_blocks(width, devices, rows, blocks):
    parts = width // FF_TILE
    down_rows = blocks * rows
    if devices > 1:
        down_block = (FF_TILE // down_rows, down_rows, width)
        down_map = lambda j: (j, 0, 0)
    else:
        down_block = (1, FF_TILE, width)
        down_map = lambda j: (0, j, 0)
    side_block = (devices, rows, FF_TILE)
    specs = [
        pl.BlockSpec(side_block, lambda j: (0, blocks + j // parts, j % parts)),
        pl.BlockSpec(side_block, lambda j: (0, 2 * blocks + j // parts, j % parts)),
        pl.BlockSpec(down_block, down_map),
    ]
    return specs, side_block, down_block


def ffn_grads(n2, dy, w, devices, rows, blocks):
    tok, width = n2.shape
    ff = blocks * width
    parts = width // FF_TILE
    down_rows = blocks * rows
    w_specs, side_block, down_block = ffn_blocks(width, devices, rows, blocks)

    def places(j):
        cols = pl.ds(pl.multiple_of(lax.rem(j, parts) * FF_TILE, FF_TILE), FF_TILE)
        first = pl.multiple_of(down_rows + (j // parts) * rows, rows)
        second = pl.multiple_of(2 * down_rows + (j // parts) * rows, rows)
        if devices > 1:
            down_at = (pl.ds(j * down_block[0], down_block[0]), pl.ds(0, down_rows))
        else:
            down_at = (slice(None), pl.ds(pl.multiple_of(j * FF_TILE, FF_TILE), FF_TILE))
        return (slice(None), pl.ds(first, rows), cols), (slice(None), pl.ds(second, rows), cols), down_at

    tile = pl.BlockSpec((tok, FF_TILE), lambda j: (0, j))
    return pl.pallas_call(
        functools.partial(ffn_grads_kernel, places),
        name="ffn_grads",
        grid=(ff // FF_TILE,),
        in_specs=[whole((tok, width)), whole((tok, width))] + w_specs,
        out_specs=[tile, tile, tile, pl.BlockSpec(memory_space=pl.ANY)],
        out_shape=[shape_of((tok, ff), bf16)] * 3 + [shape_of((devices, 3 * down_rows, width), bf16)],
        scratch_shapes=[
            pltpu.VMEM((width, tok), bf16),
            pltpu.VMEM((2,) + side_block, bf16),
            pltpu.VMEM((2,) + side_block, bf16),
            pltpu.VMEM((2,) + down_block, bf16),
            pltpu.SemaphoreType.DMA((3, 2)),
        ],
        compiler_params=params(60),
        cost_estimate=cost(50),
    )(n2, dy, w, w, w)


def ffn_sums(hidden, dgate, dup, w, devices, rows, blocks):
    tok, ff = hidden.shape
    width = ff // blocks
    w_specs, _, _ = ffn_blocks(width, devices, rows, blocks)
    tile = pl.BlockSpec((tok, FF_TILE), lambda j: (0, j))
    return pl.pallas_call(
        ffn_sums_kernel,
        name="ffn_sums",
        grid=(ff // FF_TILE,),
        in_specs=[tile, tile, tile] + w_specs,
        out_specs=[whole((tok, width)), whole((tok, width))],
        out_shape=[shape_of((tok, width), f32)] * 2,
        compiler_params=params(60),
        cost_estimate=cost(25),
    )(hidden, dgate, dup, w, w, w)


def pair_grads_kernel(
    places, n2_ref, n2_other_ref, dy_ref, dy_other_ref, wg_ref, wu_ref, wd_ref,
    hidden_ref, dgate_ref, dup_ref, wgc_ref, wuc_ref, wdc_ref, out_ref,
    n2t_ref, gate_stage, up_stage, down_stage, sems,
):
    j = pl.program_id(0)
    last = pl.num_programs(0) - 1
    slot = lax.rem(j, 2)
    core = lax.axis_index("core")
    width = n2_ref.shape[1]
    token_sets = ((n2_ref, dy_ref), (n2_other_ref, dy_other_ref))

    def copies(which, at):
        stages = (gate_stage, up_stage, down_stage)
        return [
            pltpu.make_async_copy(stage.at[at], out_ref.at[place], sems.at[index, at])
            for index, (stage, place) in enumerate(zip(stages, places(which)))
        ]

    @pl.when(j == 0)
    def _():
        n2t_ref[0] = n2_ref[...].T
        n2t_ref[1] = n2_other_ref[...].T

    for chunk in range(FF_TILE // 128):
        cols = slice(chunk * 128, chunk * 128 + 128)
        at = pl.ds(pl.multiple_of(core * 128 + chunk * 256, 128), 128)
        wgc_ref[:, cols] = wg_ref[:, :, at].reshape(width, 128)
        wuc_ref[:, cols] = wu_ref[:, :, at].reshape(width, 128)
        wdc_ref[cols, :] = wd_ref[2 * chunk + core]
    wd = wdc_ref[...]
    for index, (n2_at, dy_at) in enumerate(token_sets):
        n2 = n2_at[...]
        gate = mm(n2, wgc_ref[...])
        up = mm(n2, wuc_ref[...])
        dhid = mm_nt(dy_at[...], wd)
        sig = 1.0 / (1.0 + jnp.exp(-gate))
        act = gate * sig
        hidden_ref[index] = (act * up).astype(bf16)
        dgate_ref[index] = (dhid * up * sig * (1.0 + gate * (1.0 - sig))).astype(bf16)
        dup_ref[index] = (dhid * act).astype(bf16)

    @pl.when(j >= 2)
    def _():
        for copy in copies(j - 2, slot):
            copy.wait()

    def both(left, right):
        return (left(0, right[0]) + left(1, right[1])).astype(bf16)

    side = lambda index, grad: mm(n2t_ref[index], grad)
    down = lambda index, hidden: mm_tn(hidden, token_sets[index][1][...])
    gate_stage[slot] = both(side, dgate_ref).reshape(gate_stage.shape[1:])
    up_stage[slot] = both(side, dup_ref).reshape(up_stage.shape[1:])
    down_stage[slot] = both(down, hidden_ref).reshape(down_stage.shape[1:])
    for copy in copies(j, slot):
        copy.start()

    @pl.when(j == last)
    def _():
        for copy in copies(j - 1, 1 - slot):
            copy.wait()
        for copy in copies(j, slot):
            copy.wait()


def pair_grads(n2, n2_other, dy, dy_other, w, rows, blocks):
    tok, width = n2.shape
    devices = w.shape[0]
    chips = devices // 2
    ff = blocks * width // 2
    parts = width // FF_TILE
    down_rows = blocks * rows
    down_chips = FF_TILE // down_rows

    def places(j):
        cols = pl.ds(pl.multiple_of(lax.rem(j, parts) * FF_TILE, FF_TILE), FF_TILE)
        first = pl.multiple_of(down_rows + (j // parts) * 2 * rows, rows)
        second = pl.multiple_of(2 * down_rows + (j // parts) * 2 * rows, rows)
        return (
            (slice(None), pl.ds(first, 2 * rows), cols),
            (slice(None), pl.ds(second, 2 * rows), cols),
            (pl.ds(j * down_chips, down_chips), pl.ds(0, down_rows)),
        )

    tile = pl.BlockSpec((2, tok, FF_TILE), lambda j: (0, 0, j))
    side = pl.BlockSpec((width, FF_TILE), lambda j: (0, j))
    side_stage = pltpu.VMEM((2, chips, 2 * rows, FF_TILE), bf16)
    return pl.pallas_call(
        functools.partial(pair_grads_kernel, places),
        name="pair_grads",
        grid=(ff // FF_TILE,),
        in_specs=[whole((tok, width))] * 4
        + [
            pl.BlockSpec((devices, rows, width), lambda j: (0, blocks + j, 0)),
            pl.BlockSpec((devices, rows, width), lambda j: (0, 2 * blocks + j, 0)),
            pl.BlockSpec((2 * down_chips, down_rows, width), lambda j: (j, 0, 0)),
        ],
        out_specs=[tile, tile, tile, side, side, pl.BlockSpec((FF_TILE, width), lambda j: (j, 0))]
        + [pl.BlockSpec(memory_space=pl.ANY)],
        out_shape=[shape_of((2, tok, ff), bf16)] * 3
        + [shape_of((width, ff), bf16)] * 2
        + [shape_of((ff, width), bf16), shape_of((chips, 3 * down_rows, width), bf16)],
        scratch_shapes=[
            pltpu.VMEM((2, width, tok), bf16),
            side_stage,
            side_stage,
            pltpu.VMEM((2, down_chips, down_rows, width), bf16),
            pltpu.SemaphoreType.DMA((3, 2)),
        ],
        compiler_params=params(62),
        cost_estimate=cost(53),
    )(n2, n2_other, dy, dy_other, w, w, w)


def pair_sums_kernel(sent, hidden_ref, dgate_ref, dup_ref, wg_ref, wu_ref, wd_ref, *refs):
    f_ref, dn2_ref = refs[-2:]

    @pl.when(pl.program_id(0) == 0)
    def _():
        f_ref[...] = jnp.zeros_like(f_ref)
        dn2_ref[...] = jnp.zeros_like(dn2_ref)

    f_ref[...] += mm(hidden_ref[0], wd_ref[...])
    dn2_ref[...] += mm_nt(dgate_ref[0], wg_ref[...]) + mm_nt(dup_ref[0], wu_ref[...])

    if sent:

        @pl.when(pl.program_id(0) == pl.num_programs(0) - 1)
        def _():
            refs[0][0] = f_ref[...].astype(bf16)
            refs[0][1] = dn2_ref[...].astype(bf16)


def pair_sums(sent, hidden, dgate, dup, wg, wu, wd):
    _, tok, ff = hidden.shape
    width = wd.shape[1]
    tile = pl.BlockSpec((1, tok, FF_TILE), lambda j: (int(sent), 0, j))
    side = pl.BlockSpec((width, FF_TILE), lambda j: (0, j))
    down = pl.BlockSpec((FF_TILE, width), lambda j: (j, 0))
    if sent:
        out = dict(
            out_specs=whole((2, tok, width)),
            out_shape=shape_of((2, tok, width), bf16),
            scratch_shapes=[pltpu.VMEM((tok, width), f32)] * 2,
        )
    else:
        out = dict(out_specs=[whole((tok, width))] * 2, out_shape=[shape_of((tok, width), f32)] * 2)
    return pl.pallas_call(
        functools.partial(pair_sums_kernel, sent),
        name="pair_sums_sent" if sent else "pair_sums_own",
        grid=(ff // FF_TILE,),
        in_specs=[tile, tile, tile, side, side, down],
        compiler_params=params(60),
        cost_estimate=cost(14),
        **out,
    )(hidden, dgate, dup, wg, wu, wd)


def residual_back_kernel(
    paired, h_ref, f_ref, dn2_ref, dy_ref, o_ref, w_ref, gain_ref, ids_ref, *refs,
):
    got_ref, refs = refs[0], refs[paired:]
    out_ref, dh_ref, do_ref, sum_ref = refs[:4]
    dw_refs, acc_ref = refs[4:-1], refs[-1]
    step = pl.program_id(0)
    h = h_ref[...]
    f = f_ref[...]
    dn2 = dn2_ref[...]
    if paired:
        f = f + got_ref[0].astype(f32)
        dn2 = dn2 + got_ref[1].astype(f32)
    y = h + f
    out_ref[...] = y.astype(bf16)
    valid = flag(ids_ref)
    factor = lax.rsqrt(jnp.mean(h * h, axis=-1, keepdims=True) + EPS)
    unit = h * factor
    dunit = dn2 * gain_ref[...]
    inner = jnp.mean(dunit * unit, axis=-1, keepdims=True)
    dh = dy_ref[...].astype(f32) + factor * (dunit - unit * inner)
    dh_ref[...] = dh
    da = dh.astype(bf16)
    do_ref[...] = mm_nt(da, part(w_ref, 0, w_ref.shape[1])).astype(bf16)

    @pl.when(step == 0)
    def _():
        sum_ref[...] = jnp.zeros_like(sum_ref)
        acc_ref[...] = jnp.zeros_like(acc_ref)

    sum_ref[0] += fold_rows(y * y * valid)
    sum_ref[1] += fold_rows(f * f * valid)
    sum_ref[2] += fold_rows(dn2 * unit)
    acc_ref[...] += mm_tn(o_ref[...], da).reshape(acc_ref.shape)

    @pl.when(step == pl.num_programs(0) - 1)
    def _():
        put_grads(dw_refs, acc_ref, 0)


def residual_back(h, f, dn2, dy, o, w, w_spec, gain, ids, grad_shape, got):
    chips, cores, rows_each, _ = grad_shape
    tok, width = h.shape
    row = lambda i: (i, 0)
    rows = pl.BlockSpec((ROWS, width), row)
    return pl.pallas_call(
        functools.partial(residual_back_kernel, len(got)),
        name="residual_back",
        grid=(tok // ROWS,),
        in_specs=[
            rows, rows, rows, rows, rows, w_spec, whole((1, width)),
            pl.BlockSpec((ROWS, ids.shape[1]), row),
        ]
        + [pl.BlockSpec((2, ROWS, width), lambda i: (0, i, 0))] * len(got),
        out_specs=[
            rows,
            rows,
            rows,
            pl.BlockSpec((3, 8, width), lambda i: (0, 0, 0)),
        ]
        + [whole((chips, rows_each, width))] * cores,
        out_shape=[
            shape_of((tok, width), bf16),
            shape_of((tok, width), f32),
            shape_of((tok, width), bf16),
            shape_of((3, 8, width), f32),
        ]
        + [shape_of((chips, rows_each, width), bf16)] * cores,
        scratch_shapes=[pltpu.VMEM(grad_shape, f32)],
        compiler_params=params(),
        cost_estimate=cost(13),
    )(h, f, dn2, dy, o, w, gain, ids, *got)


def project_back_kernel(
    own, cores,
    dk_ref, dv_ref, k0_ref, n1_ref, x_ref, cos_ref, sin_ref, gk_ref, *refs,
):
    step = pl.program_id(0)
    w_refs, refs = refs[:cores], refs[cores:]
    if own:
        dq_ref, q0_ref, gq_ref, firstk_ref, firstv_ref, dn1_ref, gain_ref, rows_ref = refs[:8]
        dw_refs, (accq_ref, acck_ref, accv_ref, low_ref, full_ref) = refs[8 : 8 + cores], refs[8 + cores :]
    else:
        dn1_ref, gain_ref, rows_ref, acck_ref, accv_ref, low_ref, full_ref = refs

    @pl.when(step == 0)
    def _():
        fill_weights(full_ref, w_refs)
        acck_ref[...] = jnp.zeros_like(acck_ref)
        accv_ref[...] = jnp.zeros_like(accv_ref)
        gain_ref[...] = jnp.zeros_like(gain_ref)
        rows_ref[...] = jnp.zeros_like(rows_ref)
        if own:
            accq_ref[...] = jnp.zeros_like(accq_ref)

    ones = head_ones()
    cosine = cos_ref[...]
    sine = sin_ref[...]
    n1 = n1_ref[...]
    n1t = n1.T
    pairs = n1.shape[1] // 128

    def through_norm(grad_ref, raw_ref, gain, index):
        for pair in range(pairs):
            cols = slice(pair * 128, pair * 128 + 128)
            grad = grad_ref[:, cols].astype(f32)
            grad = grad * cosine - swap_halves(grad) * sine
            raw = raw_ref[:, cols]
            factor = lax.rsqrt(head_mean(raw * raw, ones) + EPS)
            unit = raw * factor
            gain_ref[index, :, cols] += fold_rows(grad * unit)
            dunit = grad * gain
            inner = head_mean(dunit * unit, ones)
            low_ref[:, cols] = (factor * (dunit - unit * inner)).astype(bf16)
        return low_ref[...]

    dk0 = through_norm(dk_ref, k0_ref, gk_ref[...], 0)
    dv = dv_ref[...]
    acck_ref[...] += mm(n1t, dk0).reshape(acck_ref.shape)
    accv_ref[...] += mm(n1t, dv).reshape(accv_ref.shape)
    dn1 = mm_nt(dk0, weight(full_ref, 1)) + mm_nt(dv, weight(full_ref, 2))
    if own:
        dq0 = through_norm(dq_ref, q0_ref, gq_ref[...], 1)
        accq_ref[...] += mm(n1t, dq0).reshape(accq_ref.shape)
        dn1 = dn1 + mm_nt(dq0, weight(full_ref, 0))
    dn1_ref[...] = dn1.astype(dn1_ref.dtype)
    x = x_ref[...].astype(f32)
    unit = x * lax.rsqrt(jnp.mean(x * x, axis=-1, keepdims=True) + EPS)
    rows_ref[...] += fold_rows(dn1 * unit)

    if own:

        @pl.when(step == pl.num_programs(0) - 1)
        def _():
            acck_ref[...] += firstk_ref[...]
            accv_ref[...] += firstv_ref[...]
            for index, ref in enumerate((accq_ref, acck_ref, accv_ref)):
                put_grads(dw_refs, ref, index * ref.shape[2])


def project_back(own, dq, dk, dv, q0, k0, n1, x_ext, cosine, sine, gq, gk, w, w_rows, first_sums=None):
    ext, width = n1.shape
    tok = ext - 2 * HALF
    first = HALF // ROWS
    tiles = tok // ROWS
    cores = len(w)
    acc_shape = (w[0].shape[0], cores, w_rows, width)
    if own:
        place = lambda i: (i + first, 0)
        steps, out_type = tiles, f32
    else:
        place = lambda i: (jnp.where(i < first, i, i + tiles), 0)
        steps, out_type = 2 * first, bf16
    wide = pl.BlockSpec((ROWS, width), place)
    narrow = pl.BlockSpec((ROWS, 128), place)
    local_row = pl.BlockSpec((ROWS, width), lambda i: (i, 0))
    acc = pltpu.VMEM(acc_shape, f32)
    in_specs = [wide, wide, wide, wide, wide, narrow, narrow, whole((1, 128))] + [whole(each.shape) for each in w]
    args = [dk, dv, k0, n1, x_ext, cosine, sine, gk, *w]
    out_specs = [local_row, whole((2, 8, width)), whole((8, width))]
    out_shape = [
        shape_of((steps * ROWS, width), out_type),
        shape_of((2, 8, width), f32),
        shape_of((8, width), f32),
    ]
    scratch = [pltpu.VMEM((ROWS, width), bf16), full_weights(w, w_rows)]
    if own:
        in_specs += [local_row, local_row, whole((1, 128)), whole(acc_shape), whole(acc_shape)]
        args += [dq, q0, gq, *first_sums]
        out_specs += [whole(each.shape) for each in w]
        out_shape += [shape_of(each.shape, bf16) for each in w]
        scratch = [acc] * 3 + scratch
    else:
        out_specs += [whole(acc_shape)] * 2
        out_shape += [shape_of(acc_shape, f32)] * 2
    return pl.pallas_call(
        functools.partial(project_back_kernel, own, cores),
        name="project_back_own" if own else "project_back_halo",
        grid=(steps,),
        in_specs=in_specs,
        out_specs=out_specs,
        out_shape=out_shape,
        scratch_shapes=scratch,
        compiler_params=params(60),
        cost_estimate=cost(25 if own else 21),
    )(*args)


def assemble_kernel(rows, blocks, grads_ref, got_ref, down_ref, gate_ref, up_ref):
    core = lax.axis_index("core")
    width = grads_ref.shape[1]
    down_rows = blocks * rows
    down_ref[...] = grads_ref[0:down_rows, :].astype(f32)
    for index, out_ref in enumerate((gate_ref, up_ref)):
        for block in range(blocks // 2):
            first = down_rows + (index * (blocks // 2) + block) * 2 * rows
            mine = grads_ref[pl.ds(pl.multiple_of(first + core * rows, rows), rows), :].astype(f32)
            other = got_ref[index, block].astype(f32)
            for chunk in range(width // 128):
                at = block * 2 * width + chunk * 256
                cols = slice(chunk * 128, chunk * 128 + 128)
                out_ref[:, pl.ds(pl.multiple_of(at + core * 128, 128), 128)] = mine[:, cols]
                out_ref[:, pl.ds(pl.multiple_of(at + (1 - core) * 128, 128), 128)] = other[:, cols]


def assemble(grads, got, rows, blocks):
    width = grads.shape[1]
    return pl.pallas_call(
        functools.partial(assemble_kernel, rows, blocks),
        name="assemble",
        out_shape=[
            shape_of((blocks * rows, width), f32),
            shape_of((rows, blocks * width), f32),
            shape_of((rows, blocks * width), f32),
        ],
        compiler_params=params(16),
        cost_estimate=cost(2),
    )(grads, got)


def pack_kernel(copies_spread, blocks, rows, wq, wk, wv, wo, wg, wu, wd, attn_out, rest_out, sems):
    width = wq.shape[1]
    jobs = [(wd, rest_out.at[pl.ds(0, blocks * rows)])]
    for index, side in enumerate((wg, wu)):
        for part_at in range(blocks):
            at = (blocks * (1 + index) + part_at) * rows
            jobs.append((side.at[:, pl.ds(part_at * width, width)], rest_out.at[pl.ds(at, rows)]))
    jobs.append((wo, rest_out.at[pl.ds(3 * blocks * rows, rows)]))
    for copy in range(copies_spread):
        for index, each in enumerate((wq, wk, wv)):
            jobs.append((each, attn_out.at[copy, pl.ds(index * rows, rows)]))
    found = [pltpu.make_async_copy(source, target, sems.at[i]) for i, (source, target) in enumerate(jobs)]
    for copy in found:
        copy.start()
    for copy in found:
        copy.wait()


def pack(weights, copies_spread, blocks):
    rows, width = weights[0].shape
    total = (3 * blocks + 1) * rows
    return pl.pallas_call(
        functools.partial(pack_kernel, copies_spread, blocks, rows),
        name="pack",
        in_specs=[pl.BlockSpec(memory_space=pl.ANY)] * 7,
        out_specs=[pl.BlockSpec(memory_space=pl.ANY)] * 2,
        out_shape=[shape_of((copies_spread, 3 * rows, width), bf16), shape_of((total, width), bf16)],
        scratch_shapes=[pltpu.SemaphoreType.DMA((2 + 2 * blocks + 3 * copies_spread,))],
        compiler_params=params(4),
    )(*weights)


def local(
    inputs, seg_ids, var_ids, time_ids, valid_mask,
    w_query, w_key, w_value, w_out, w_gate, w_up, w_down,
    gain_attn, gain_ffn, gain_query, gain_key, variate_bias, out_grad,
):
    axes = ("head", "chip", "core")
    head_count, chip_count, core_count = (lax.axis_size(axis) for axis in axes)
    blk_count = chip_count * core_count
    devices = head_count * blk_count
    chips = head_count * chip_count
    tok, width = inputs.shape[1:]
    heads = variate_bias.shape[1]
    head_dim = gain_query.shape[0]
    rows = w_query.shape[0]
    blocks = w_gate.shape[1] // width
    ext = tok + 2 * HALF
    blk = lax.axis_index("chip") * core_count + lax.axis_index("core")
    place = blk * head_count + lax.axis_index("head")
    fast = rows % 16 == 0
    k_cores, k_devices, k_rows = (core_count, devices, rows) if fast else (1, 1, width)
    k_chips = k_devices // k_cores

    def flat(p):
        return (p % head_count) * blk_count + p // head_count

    onward = [(flat(p), flat(p + 1)) for p in range(devices - 1)]
    back = [(b, a) for a, b in onward]

    def exchange(values, axis):
        return lax.all_to_all(values, axis, split_axis=0, concat_axis=0, tiled=True)

    def swap_cores(values):
        return lax.ppermute(values, "core", [(0, 1), (1, 0)])

    def spread_to_all(full, parts):
        full = exchange(jnp.broadcast_to(full[None], (head_count,) + full.shape), "head")
        full = full.reshape(chips, parts * rows, width)
        other = swap_cores(full)
        if fast:
            return [full, other]
        swapped = lax.axis_index("core") == 1
        both = jnp.stack([jnp.where(swapped, other, full), jnp.where(swapped, full, other)])
        pieces = both.reshape(core_count, chips, parts, rows, width).transpose(2, 1, 0, 3, 4)
        return [pieces.reshape(1, parts * width, width)]

    def total(values):
        return jnp.sum(values.astype(f32), axis=0)

    def reduce_cores(grads, parts):
        if not fast:
            pieces = grads[0].reshape(parts, chips, core_count, rows, width).transpose(2, 1, 0, 3, 4)
            core = lax.axis_index("core")
            grads = [lax.dynamic_index_in_dim(pieces, at, 0, False) for at in (core, 1 - core)]
        mine, other = (each.reshape(head_count, chip_count, parts * rows, width) for each in grads)
        return (mine.astype(f32) + swap_cores(other).astype(f32)).astype(bf16)

    def reduce_heads(grads):
        return total(exchange(grads, "head")).astype(bf16)

    def reduce_chips(grads):
        return total(exchange(grads, "chip"))

    def gather_rest(shard):
        full = lax.all_gather(shard, axes, axis=0, tiled=False)
        if fast:
            return full
        parts = shard.shape[0] // rows
        down = full[:, : blocks * rows].reshape(1, blocks * width, width)
        rest = full[:, blocks * rows :].reshape(devices, parts - blocks, rows, width)
        rest = rest.transpose(1, 0, 2, 3).reshape(1, (parts - blocks) * width, width)
        return jnp.concatenate([down, rest], axis=1)

    def scatter_pair(grads):
        pieces = grads[blocks * rows :].reshape(2, blocks // 2, 2, rows, width)
        other = lax.dynamic_index_in_dim(pieces, 1 - lax.axis_index("core"), 2, False)
        return assemble(grads, swap_cores(other), rows, blocks)

    def scatter_stage(grads, axis):
        return lax.psum_scatter(grads.reshape(-1, width), axis, scatter_dimension=0, tiled=True)

    def scatter_rest(grads):
        if not fast:
            down = grads[0, : blocks * width].reshape(devices, blocks * rows, width)
            rest = grads[0, blocks * width :].reshape(2 * blocks, devices, rows, width).transpose(1, 0, 2, 3)
            grads = jnp.concatenate([down, rest.reshape(devices, -1, width)], axis=1)
        grads = grads.reshape(devices * 3 * blocks * rows, width)
        return lax.psum_scatter(grads, axes, scatter_dimension=0, tiled=True).astype(f32)

    def columns(shard):
        return [shard[:, i * width : (i + 1) * width] for i in range(blocks)]

    def sides(owned):
        return jnp.concatenate([owned[i * rows : (i + 1) * rows] for i in range(blocks)], axis=1)

    if fast:
        attn_part, rest_part = pack((w_query, w_key, w_value, w_out, w_gate, w_up, w_down), chip_count, blocks)
    else:
        attn_part = jnp.concatenate([w_query, w_key, w_value], axis=0)
        attn_part = jnp.broadcast_to(attn_part[None], (chip_count,) + attn_part.shape)
        rest_part = jnp.concatenate([w_down] + columns(w_gate) + columns(w_up) + [w_out], axis=0)
    rest_w = gather_rest(rest_part)
    x = inputs[0]
    attn_w = exchange(attn_part, "chip")
    ids = jnp.stack([seg_ids, var_ids, valid_mask, time_ids]).reshape(4, -1)
    ids = jnp.pad(ids, ((0, 0), (HALF, HALF)))
    ids = lax.dynamic_slice_in_dim(ids, place * tok, ext, 1).T
    own = slice(HALF, HALF + tok)
    quarter = jnp.arange(128) % (head_dim // 2)
    frequency = 10000.0 ** (-quarter.astype(f32) * 2.0 / head_dim)
    angles = ids[:, 3:].astype(f32) * frequency[None, :]
    cosine = jnp.cos(angles)
    sine = jnp.sin(angles) * jnp.where(jnp.arange(128) % head_dim < head_dim // 2, -1.0, 1.0)
    diff = (variate_bias[0] - variate_bias[1]) * LOG2E
    diff_high = lax.reduce_precision(diff, 8, 7)
    diff_low = diff - diff_high
    lane = jnp.arange(128)[None, :]
    diff_rows = jnp.where(lane < LANE_LOW, diff_high[:, None], jnp.where(lane < LANE_CODE, diff_low[:, None], 1.0))
    gq = jnp.tile(gain_query, 2)[None]
    gk = jnp.tile(gain_key, 2)[None]

    before = lax.ppermute(x[tok - HALF :], axes, onward)
    after = lax.ppermute(x[:HALF], axes, back)
    attn_w, before, after, ids, cosine, sine = lax.optimization_barrier((attn_w, before, after, ids, cosine, sine))
    attn_w = spread_to_all(attn_w, 3)
    x_ext = jnp.concatenate([before, x, after], axis=0)

    own_ids = ids[own]

    n1, q0, k0, q, k, v = project(
        x_ext, gain_attn[None], attn_w, k_rows, cosine, sine, gq, gk, ids, diff_rows, tok, heads
    )
    o, qb = attend(q, k, v, own_ids)

    out_spec = pl.BlockSpec((k_devices, k_rows, width), lambda i: (0, 3 * blocks, 0), pipeline_mode=pl.Buffered(1))
    h, n2, branch_sum = branch_forward(o, x, rest_w, out_spec, gain_ffn[None], own_ids)
    dy = out_grad[0]
    if fast:
        *middle, ff_grads = pair_grads(n2, swap_cores(n2), dy, swap_cores(dy), rest_w, rows, blocks)
        ff_grads = scatter_stage(ff_grads, "head")
        got = [swap_cores(pair_sums(True, *middle))]
        f, dn2 = pair_sums(False, *middle)
    else:
        hidden, dgate, dup, ff_grads = ffn_grads(n2, dy, rest_w, k_devices, k_rows, blocks)
        ff_owned = scatter_rest(ff_grads)
        down_owned = ff_owned[: blocks * rows]
        gate_owned = sides(ff_owned[blocks * rows : 2 * blocks * rows])
        up_owned = sides(ff_owned[2 * blocks * rows :])
        got = []
        f, dn2 = ffn_sums(hidden, dgate, dup, rest_w, k_devices, k_rows, blocks)
    layer_out, dh, do, sums, *out_grads = residual_back(
        h, f, dn2, dy, o, rest_w, out_spec, gain_ffn[None], own_ids, (k_chips, k_cores, k_rows, width), got
    )
    early = reduce_cores(out_grads, 1)
    do, early = lax.optimization_barrier((do, early))
    early = reduce_heads(early)
    dq, dk, dv, bias_rows = attend_back(qb, k, v, o, do, own_ids)
    dq, early = lax.optimization_barrier((dq, early))
    early_owned = reduce_chips(early)
    turn = (cosine, sine, gq, gk, attn_w, k_rows)
    dn1_halo, gain_halo, rows_halo, *first_sums = project_back(False, dq, dk, dv, q0, k0, n1, x_ext, *turn)
    from_left = lax.ppermute(dn1_halo[HALF:], axes, onward)
    from_right = lax.ppermute(dn1_halo[:HALF], axes, back)
    if fast:
        dq, ff_grads = lax.optimization_barrier((dq, ff_grads))
        down_owned, gate_owned, up_owned = scatter_pair(scatter_stage(ff_grads, "chip"))
    dn1_own, gain_own, rows_own, *attn_grads = project_back(
        True, dq, dk, dv, q0, k0, n1, x_ext, *turn, first_sums
    )
    attn_grads, early_owned, from_left, from_right = lax.optimization_barrier(
        (attn_grads, early_owned, from_left, from_right)
    )
    attn_sums = reduce_cores(attn_grads, 3)
    attn_sums, gain_halo = lax.optimization_barrier((attn_sums, gain_halo))
    attn_owned = reduce_chips(reduce_heads(attn_sums))

    dn1 = (
        dn1_own
        + jnp.pad(from_left.astype(f32), ((0, tok - HALF), (0, 0)))
        + jnp.pad(from_right.astype(f32), ((tok - HALF, 0), (0, 0)))
    )
    x_float = x.astype(f32)
    factor = lax.rsqrt(jnp.mean(x_float * x_float, axis=-1, keepdims=True) + EPS)
    unit = x_float * factor
    dunit = dn1 * gain_attn
    inner = jnp.mean(dunit * unit, axis=-1, keepdims=True)
    grad_inputs = (dh + factor * (dunit - unit * inner)).astype(bf16)
    grad_gain_attn = (rows_own + rows_halo).sum(0)

    bias_rows = bias_rows.reshape(heads // 2, 8, 128)[:, :4].reshape(heads, 2, 128)[:, :, 64 : 64 + VARS].sum(-1)
    bias_grad = jnp.stack([bias_rows[:, 0], bias_rows[:, 1] - bias_rows[:, 0]])
    gain_heads = (gain_own + gain_halo)[::-1].sum(1).reshape(2, heads, head_dim).sum(1)
    squares = jnp.stack([sums[0].sum(), branch_sum.sum(), sums[1].sum()])
    small = jnp.concatenate(
        [grad_gain_attn, sums[2].sum(0), gain_heads.reshape(-1), bias_grad.reshape(-1), squares]
    )
    filled = -small.shape[0] % 1024
    small = jnp.pad(small, (0, filled)).reshape(-1, 128)
    for axis, count in (("core", core_count), ("head", head_count), ("chip", chip_count)):
        step = 1
        while step < count:
            small = small + lax.ppermute(small, axis, [(i, i ^ step) for i in range(count)])
            step *= 2
    small = small.reshape(-1)
    at = 2 * width
    valid_count = jnp.maximum(jnp.sum((valid_mask == 1).astype(f32)), 1.0)
    rms_values = jnp.sqrt(small[at + 2 * head_dim + 2 * heads :][:3] / (valid_count * width))

    return (
        layer_out[None],
        grad_inputs[None],
        attn_owned[:rows],
        attn_owned[rows : 2 * rows],
        attn_owned[2 * rows :],
        early_owned,
        gate_owned,
        up_owned,
        down_owned,
        small[:width],
        small[width : 2 * width],
        small[at : at + head_dim],
        small[at + head_dim : at + 2 * head_dim],
        small[at + 2 * head_dim : at + 2 * head_dim + 2 * heads].reshape(2, heads),
        rms_values,
    )


def solution(mesh):
    heads, blks = mesh.devices.shape
    cores = 2 if blks % 2 == 0 else 1
    mesh = Mesh(mesh.devices.reshape(heads, blks // cores, cores), ("head", "chip", "core"))
    tokens = P(("chip", "core"), "head", None)
    weights = P(("head", "chip", "core"), None)
    in_specs = (tokens,) + (P(),) * 4 + (weights,) * 7 + (P(),) * 5 + (tokens,)
    out_specs = (tokens,) * 2 + (weights,) * 7 + (P(),) * 6
    return jax.shard_map(local, mesh=mesh, in_specs=in_specs, out_specs=out_specs, check_vma=False)
```

```python
import functools

import jax
import jax.numpy as jnp
from jax import lax
from jax.experimental import pallas as pl
from jax.experimental.pallas import tpu as pltpu
from jax.sharding import Mesh
from jax.sharding import PartitionSpec as P

HALF = 512
ROWS = 256
FF_TILE = 512
VARS = 8
CODES = 8
CODE_SIZE = 64.0
OUTSIDE = 256.0
LOG2E = 1.4426950408889634
EPS = 1e-05
MIB = 1 << 20

LANE_HIGH = 64
LANE_LOW = 72
LANE_CODE = 80
LANE_ONE = 88
LANE_LSE = 90

SEG, VAR, VALID = 0, 1, 2

f32 = jnp.float32
bf16 = jnp.bfloat16
shape_of = jax.ShapeDtypeStruct


def mm(a, b):
    return lax.dot_general(a, b, (((1,), (0,)), ((), ())), preferred_element_type=f32)


def mm_nt(a, b):
    return lax.dot_general(a, b, (((1,), (1,)), ((), ())), preferred_element_type=f32)


def mm_tn(a, b):
    return lax.dot_general(a, b, (((0,), (0,)), ((), ())), preferred_element_type=f32)


def params(vmem=56):
    return pltpu.CompilerParams(vmem_limit_bytes=vmem * MIB)


def cost(us):
    return pl.CostEstimate(flops=int(us * 1e9), bytes_accessed=1 << 20, transcendentals=0)


def whole(shape):
    return pl.BlockSpec(shape, lambda *_: (0,) * len(shape), pipeline_mode=pl.Buffered(1))


def lane_of(shape):
    return lax.broadcasted_iota(jnp.int32, shape, len(shape) - 1)


def row_of(shape):
    return lax.broadcasted_iota(jnp.int32, shape, len(shape) - 2)


def head_ones(size=128):
    shape = (size, size)
    return jnp.where((row_of(shape) // 64) == (lane_of(shape) // 64), 1.0, 0.0).astype(bf16)


def head_mean(values, ones):
    high = values.astype(bf16)
    low = (values - high.astype(f32)).astype(bf16)
    return (mm(high, ones) + mm(low, ones)) * (1.0 / 64.0)


def swap_halves(values):
    first = (lane_of(values.shape) % 64) < 32
    return jnp.where(first, pltpu.roll(values, 96, 1), pltpu.roll(values, 32, 1))


def fold_rows(values):
    rows, width = values.shape
    return jnp.sum(values.reshape(rows // 8, 8, width), axis=0)


def flag(ids_ref, rows=slice(None)):
    return jnp.where(ids_ref[rows, VALID : VALID + 1] == 1, 1.0, 0.0)


def key_extra(ids):
    lane = lane_of((ids.shape[0], 128))
    var = ids[:, VAR : VAR + 1]
    seg = ids[:, SEG : SEG + 1]
    invalid = jnp.where(ids[:, VALID : VALID + 1] == 1, 0.0, 1.0)
    bit = jnp.right_shift(seg, jnp.clip(lane - LANE_CODE, 0, CODES - 1)) & 1
    extra = jnp.where((var == lane - LANE_HIGH) | (var == lane - LANE_LOW) & (lane >= LANE_LOW), 1.0, 0.0)
    extra = jnp.where(lane >= LANE_CODE, CODE_SIZE * (2 * bit - 1).astype(f32), extra)
    extra = jnp.where(lane >= LANE_ONE, -CODE_SIZE * (CODES + 2.0 * invalid), extra)
    extra = jnp.where(lane > LANE_ONE, jnp.where((lane >= LANE_LSE) & (lane < LANE_LSE + 3), 1.0, 0.0), extra)
    return extra


def query_extra(ids):
    lane = lane_of((ids.shape[0], 128))
    var = ids[:, VAR : VAR + 1]
    seg = ids[:, SEG : SEG + 1]
    bit = jnp.right_shift(seg, jnp.clip(lane - LANE_CODE, 0, CODES - 1)) & 1
    extra = jnp.where((var == lane - LANE_HIGH) | (var == lane - LANE_LOW) & (lane >= LANE_LOW), 1.0, 0.0)
    extra = jnp.where(lane >= LANE_CODE, (2 * bit - 1).astype(f32), extra)
    return jnp.where(lane >= LANE_ONE, jnp.where(lane == LANE_ONE, 1.0, 0.0), extra)


def part(ref, index, rows):
    block = ref[:, index * rows : (index + 1) * rows, :]
    return block.reshape(block.shape[0] * rows, block.shape[2])


def core_at(slot, cores):
    if cores == 1:
        return 0
    own = lax.axis_index("core")
    return own if slot == 0 else 1 - own


def fill_weights(full_ref, w_refs, half=0):
    parts, _, cores, rows, width = full_ref.shape
    cols = slice(half * width, (half + 1) * width)
    for slot in range(cores):
        for index in range(parts):
            full_ref[index, :, core_at(slot, cores)] = w_refs[slot][:, index * rows : (index + 1) * rows, cols]


def weight(full_ref, index):
    _, chips, cores, rows, width = full_ref.shape
    return full_ref[index].reshape(chips * cores * rows, width)


def put_grads(out_refs, acc_ref, first):
    _, cores, rows, _ = acc_ref.shape
    for slot in range(cores):
        out_refs[slot][:, first : first + rows, :] = acc_ref[:, core_at(slot, cores)].astype(bf16)


def project_kernel(
    own_first, own_last, cores,
    x_ref, gain_ref, cos_ref, sin_ref, gq_ref, gk_ref, ids_ref, diff_ref, *refs,
):
    w_refs = refs[:cores]
    n1_ref, q0_ref, qf_ref, k0_ref, kf_ref, q_ref, k_ref, v_ref, full_ref = refs[cores:]
    step = pl.program_id(0)

    @pl.when(step == 0)
    def _():
        fill_weights(full_ref, w_refs)

    x = x_ref[...].astype(f32)
    factor = lax.rsqrt(jnp.mean(x * x, axis=-1, keepdims=True) + EPS)
    n1 = (x * factor * gain_ref[...]).astype(bf16)
    n1_ref[...] = n1
    ones = head_ones()
    cosine = cos_ref[...]
    sine = sin_ref[...]
    kaug = key_extra(ids_ref[...])
    own_lane = lane_of(kaug.shape) < 64
    pairs = x.shape[1] // 128

    k0 = mm(n1, weight(full_ref, 1))
    k0_ref[...] = k0
    value = mm(n1, weight(full_ref, 2))
    vaug = jnp.where(lane_of(kaug.shape) < 67, 1.0, 0.0)
    for pair in range(pairs):
        cols = slice(pair * 128, pair * 128 + 128)
        raw = k0[:, cols]
        factor = lax.rsqrt(head_mean(raw * raw, ones) + EPS)
        kf_ref[:, cols] = factor
        normed = raw * factor * gk_ref[...]
        turned = normed * cosine + swap_halves(normed) * sine
        k_ref[2 * pair] = jnp.where(own_lane, turned, kaug).astype(bf16)
        k_ref[2 * pair + 1] = jnp.where(own_lane, pltpu.roll(turned, 64, 1), kaug).astype(bf16)
        val = value[:, cols]
        v_ref[2 * pair] = jnp.where(own_lane, val, vaug).astype(bf16)
        v_ref[2 * pair + 1] = jnp.where(own_lane, pltpu.roll(val, 64, 1), vaug).astype(bf16)

    @pl.when((step >= own_first) & (step < own_last))
    def _():
        q0 = mm(n1, weight(full_ref, 0))
        q0_ref[...] = q0
        qaug = query_extra(ids_ref[...])
        for pair in range(pairs):
            cols = slice(pair * 128, pair * 128 + 128)
            raw = q0[:, cols]
            factor = lax.rsqrt(head_mean(raw * raw, ones) + EPS)
            qf_ref[:, cols] = factor
            normed = raw * factor * gq_ref[...]
            turned = (normed * cosine + swap_halves(normed) * sine) * (0.125 * LOG2E)
            first = qaug * diff_ref[2 * pair : 2 * pair + 1, :]
            second = qaug * diff_ref[2 * pair + 1 : 2 * pair + 2, :]
            q_ref[2 * pair] = jnp.where(own_lane, turned, first).astype(bf16)
            q_ref[2 * pair + 1] = jnp.where(own_lane, pltpu.roll(turned, 64, 1), second).astype(bf16)


def full_weights(w, rows):
    chips, total, width = w[0].shape
    return pltpu.VMEM((total // rows, chips, len(w), rows, width), bf16)


def project(x_ext, gain, w, w_rows, cosine, sine, gq, gk, ids, diff, tok, heads):
    ext, width = x_ext.shape
    own_first = HALF // ROWS
    own_last = own_first + tok // ROWS
    row = lambda i: (i, 0)
    own = lambda i: (jnp.clip(i - own_first, 0, own_last - own_first - 1), 0)
    head_row = lambda i: (0, i, 0)
    head_own = lambda i: (0, own(i)[0], 0)
    return pl.pallas_call(
        functools.partial(project_kernel, own_first, own_last, len(w)),
        name="project",
        grid=(ext // ROWS,),
        in_specs=[
            pl.BlockSpec((ROWS, width), row),
            whole((1, width)),
            pl.BlockSpec((ROWS, 128), row),
            pl.BlockSpec((ROWS, 128), row),
            whole((1, 128)),
            whole((1, 128)),
            pl.BlockSpec((ROWS, ids.shape[1]), row),
            whole(diff.shape),
        ]
        + [whole(each.shape) for each in w],
        out_specs=[
            pl.BlockSpec((ROWS, width), row),
            pl.BlockSpec((ROWS, width), own),
            pl.BlockSpec((ROWS, width), own),
            pl.BlockSpec((ROWS, width), row),
            pl.BlockSpec((ROWS, width), row),
            pl.BlockSpec((heads, ROWS, 128), head_own),
            pl.BlockSpec((heads, ROWS, 128), head_row),
            pl.BlockSpec((heads, ROWS, 128), head_row),
        ],
        out_shape=[
            shape_of((ext, width), bf16),
            shape_of((tok, width), f32),
            shape_of((tok, width), f32),
            shape_of((ext, width), f32),
            shape_of((ext, width), f32),
            shape_of((heads, tok, 128), bf16),
            shape_of((heads, ext, 128), bf16),
            shape_of((heads, ext, 128), bf16),
        ],
        scratch_shapes=[full_weights(w, w_rows)],
        compiler_params=params(),
        cost_estimate=cost(27),
    )(x_ext, gain, cosine, sine, gq, gk, ids, diff, *w)


def fill_masks(ids_ref, diag_ref, edge_ref, key_axis):
    shape = (ROWS, ROWS)
    key = lax.broadcasted_iota(jnp.int32, shape, key_axis)
    query = lax.broadcasted_iota(jnp.int32, shape, 1 - key_axis)
    edge_ref[0] = jnp.where(key > query, 0.0, -OUTSIDE)
    edge_ref[1] = jnp.where(key < query, 0.0, -OUTSIDE)
    for i in range(diag_ref.shape[0] // ROWS):
        rows = slice(i * ROWS, i * ROWS + ROWS)
        diag_ref[rows, :] = jnp.where(key == query, 2.0 * CODE_SIZE * (1.0 - flag(ids_ref, rows)), 0.0)


def attend_kernel(q_ref, k_ref, v_ref, ids_ref, o_ref, qb_ref, diag_ref, edge_ref):
    @pl.when(pl.program_id(0) == 0)
    def _():
        fill_masks(ids_ref, diag_ref, edge_ref, 1)

    tiles = 1 + 2 * HALF // ROWS
    tok = q_ref.shape[1]

    def block(i, carry):
        first_row = pl.multiple_of(i * ROWS, ROWS)
        outs = []
        for head in range(2):
            query = q_ref[head, pl.ds(first_row, ROWS), :]
            total = jnp.zeros((ROWS, 128), f32)
            for j in range(tiles):
                keys = pl.ds(first_row + j * ROWS, ROWS)
                score = mm_nt(query, k_ref[head, keys, :])
                if j == 0:
                    score = score + edge_ref[0]
                elif j == tiles - 1:
                    score = score + edge_ref[1]
                elif j == tiles // 2:
                    score = score + diag_ref[pl.ds(first_row, ROWS), :]
                total = total + mm(jnp.exp2(score).astype(bf16), v_ref[head, keys, :])
            weight = total[:, 64:65]
            outs.append(total / weight)
            lse = jnp.log2(weight)
            high = lse.astype(bf16).astype(f32)
            middle = (lse - high).astype(bf16).astype(f32)
            low = lse - high - middle
            lane = lane_of((ROWS, 128))
            updated = jnp.where(lane == LANE_LSE, -high, query.astype(f32))
            updated = jnp.where(lane == LANE_LSE + 1, -middle, updated)
            updated = jnp.where(lane == LANE_LSE + 2, -low, updated)
            qb_ref[head, pl.ds(first_row, ROWS), :] = updated.astype(bf16)
        lane = lane_of((ROWS, 128))
        joined = jnp.where(lane < 64, outs[0], pltpu.roll(outs[1], 64, 1))
        o_ref[pl.ds(first_row, ROWS), :] = joined.astype(bf16)
        return carry

    lax.fori_loop(0, tok // ROWS, block, 0)


def attend(q, k, v, ids):
    heads, tok, _ = q.shape
    ext = k.shape[1]
    pair = lambda p: (p, 0, 0)
    return pl.pallas_call(
        attend_kernel,
        name="attend",
        grid=(heads // 2,),
        in_specs=[
            pl.BlockSpec((2, tok, 128), pair),
            pl.BlockSpec((2, ext, 128), pair),
            pl.BlockSpec((2, ext, 128), pair),
            whole(ids.shape),
        ],
        out_specs=[
            pl.BlockSpec((tok, 128), lambda p: (0, p)),
            pl.BlockSpec((2, tok, 128), pair),
        ],
        out_shape=[shape_of((tok, heads * 64), bf16), shape_of((heads, tok, 128), bf16)],
        scratch_shapes=[pltpu.VMEM((tok, ROWS), f32), pltpu.VMEM((2, ROWS, ROWS), f32)],
        compiler_params=params(),
        cost_estimate=cost(36),
    )(q, k, v, ids)


def attend_back_kernel(
    q_ref, k_ref, v_ref, o_ref, do_ref, ids_ref,
    dq_ref, dk_ref, dv_ref, bias_ref,
    diag_ref, edge_ref, kt_ref, dkey_ref, dval_ref, dout_ref, dqt_ref,
):
    @pl.when(pl.program_id(0) == 0)
    def _():
        fill_masks(ids_ref, diag_ref, edge_ref, 0)

    span = 2 * HALF // ROWS
    tok = q_ref.shape[1]
    ext = k_ref.shape[1]
    blocks = tok // ROWS

    def one_head(head, carry):
        shift = head * 64

        def put(ref, rows, values):
            mine = (lane_of(values.shape) // 64) == head
            kept = ref[rows, :].astype(f32)
            ref[rows, :] = jnp.where(mine, pltpu.roll(values, shift, 1), kept).astype(bf16)

        for i in range(blocks):
            rows = slice(i * ROWS, i * ROWS + ROWS)
            lane = lane_of((ROWS, 128))
            dout = pltpu.roll(do_ref[rows, :].astype(f32), shift, 1)
            product = pltpu.roll(o_ref[rows, :].astype(f32), shift, 1) * dout
            delta = jnp.sum(jnp.where(lane < 64, product, 0.0), axis=-1, keepdims=True)
            high = delta.astype(bf16).astype(f32)
            middle = (delta - high).astype(bf16).astype(f32)
            low = delta - high - middle
            aug = jnp.where(lane == 64, -high, jnp.where(lane == 65, -middle, jnp.where(lane == 66, -low, 0.0)))
            dout_ref[rows, :] = jnp.where(lane < 64, dout, aug).astype(bf16)

        for t in range(ext // ROWS):
            rows = slice(t * ROWS, t * ROWS + ROWS)
            kt_ref[:, rows] = k_ref[head, rows, :].T

        for i in range(blocks):
            rows = slice(i * ROWS, i * ROWS + ROWS)
            query = q_ref[head, rows, :]
            dout = dout_ref[rows, :]
            dqt = jnp.zeros((128, ROWS), f32)
            for j in range(span + 1):
                keys = slice((i + j) * ROWS, (i + j + 1) * ROWS)
                score = mm_nt(k_ref[head, keys, :], query)
                if j == 0:
                    score = score + edge_ref[0]
                elif j == span:
                    score = score + edge_ref[1]
                elif 2 * j == span:
                    score = score + diag_ref[rows, :]
                weight = jnp.exp2(score)
                dscore = (weight * mm_nt(v_ref[head, keys, :], dout)).astype(bf16)
                dval = mm(weight.astype(bf16), dout)
                dkey = mm(dscore, query)
                if i == 0 or j == span:
                    dval_ref[keys, :] = dval
                    dkey_ref[keys, :] = dkey
                else:
                    dval_ref[keys, :] += dval
                    dkey_ref[keys, :] += dkey
                dqt = dqt + mm(kt_ref[:, keys], dscore)
            dqt_ref[:, rows] = dqt
        for t in range(ext // ROWS):
            rows = slice(t * ROWS, t * ROWS + ROWS)
            put(dk_ref, rows, dkey_ref[rows, :] * (1.0 / LOG2E))
            put(dv_ref, rows, dval_ref[rows, :])

        dquery = dqt_ref[...].T
        base = query_extra(ids_ref[...])
        bias_ref[pl.ds(2 * head, 1), :] = jnp.sum(dquery * base, axis=0, keepdims=True)
        bias_ref[pl.ds(2 * head + 1, 1), :] = jnp.sum(dquery, axis=0, keepdims=True)
        put(dq_ref, slice(0, tok), dquery * 0.125)
        return carry

    lax.fori_loop(0, 2, one_head, 0)


def attend_back(half, q, k, v, o, do, ids):
    heads, tok, _ = q.shape
    ext = k.shape[1]
    pairs = heads // 4
    pair = lambda p: (p + half * pairs, 0, 0)
    cols = lambda p: (0, p + half * pairs)
    out = lambda p: (0, p)
    return pl.pallas_call(
        attend_back_kernel,
        name="attend_back",
        grid=(pairs,),
        in_specs=[
            pl.BlockSpec((2, tok, 128), pair),
            pl.BlockSpec((2, ext, 128), pair),
            pl.BlockSpec((2, ext, 128), pair),
            pl.BlockSpec((tok, 128), cols),
            pl.BlockSpec((tok, 128), cols),
            whole(ids.shape),
        ],
        out_specs=[
            pl.BlockSpec((tok, 128), out),
            pl.BlockSpec((ext, 128), out),
            pl.BlockSpec((ext, 128), out),
            pl.BlockSpec((8, 128), lambda p: (p, 0)),
        ],
        out_shape=[
            shape_of((tok, pairs * 128), bf16),
            shape_of((ext, pairs * 128), bf16),
            shape_of((ext, pairs * 128), bf16),
            shape_of((pairs * 8, 128), f32),
        ],
        scratch_shapes=[
            pltpu.VMEM((tok, ROWS), f32),
            pltpu.VMEM((2, ROWS, ROWS), f32),
            pltpu.VMEM((128, ext), bf16),
            pltpu.VMEM((ext, 128), f32),
            pltpu.VMEM((ext, 128), f32),
            pltpu.VMEM((tok, 128), bf16),
            pltpu.VMEM((128, tok), f32),
        ],
        compiler_params=params(),
        cost_estimate=cost(36),
    )(q, k, v, o, do, ids)


def branch_kernel(o_ref, x_ref, w_ref, gain_ref, ids_ref, h_ref, n2_ref, sum_ref):
    branch = mm(o_ref[...], part(w_ref, 0, w_ref.shape[1]))
    h = x_ref[...].astype(f32) + branch
    h_ref[...] = h
    factor = lax.rsqrt(jnp.mean(h * h, axis=-1, keepdims=True) + EPS)
    n2_ref[...] = (h * factor * gain_ref[...]).astype(bf16)

    @pl.when(pl.program_id(0) == 0)
    def _():
        sum_ref[...] = jnp.zeros_like(sum_ref)

    sum_ref[...] += fold_rows(branch * branch * flag(ids_ref))


def branch_forward(o, x, w, w_spec, gain, ids):
    tok, width = x.shape
    row = lambda i: (i, 0)
    return pl.pallas_call(
        branch_kernel,
        name="branch",
        grid=(tok // ROWS,),
        in_specs=[
            pl.BlockSpec((ROWS, width), row),
            pl.BlockSpec((ROWS, width), row),
            w_spec,
            whole((1, width)),
            pl.BlockSpec((ROWS, ids.shape[1]), row),
        ],
        out_specs=[
            pl.BlockSpec((ROWS, width), row),
            pl.BlockSpec((ROWS, width), row),
            pl.BlockSpec((8, width), lambda i: (0, 0)),
        ],
        out_shape=[
            shape_of((tok, width), f32),
            shape_of((tok, width), bf16),
            shape_of((8, width), f32),
        ],
        compiler_params=params(),
        cost_estimate=cost(7),
    )(o, x, w, gain, ids)


def ffn_grads_kernel(
    places, n2_ref, dy_ref, wg_ref, wu_ref, wd_ref,
    hidden_ref, dgate_ref, dup_ref, out_ref,
    n2t_ref, gate_stage, up_stage, down_stage, sems,
):
    j = pl.program_id(0)
    last = pl.num_programs(0) - 1
    slot = lax.rem(j, 2)

    def copies(which, at):
        stages = (gate_stage, up_stage, down_stage)
        return [
            pltpu.make_async_copy(stage.at[at], out_ref.at[place], sems.at[index, at])
            for index, (stage, place) in enumerate(zip(stages, places(which)))
        ]

    @pl.when(j == 0)
    def _():
        n2t_ref[...] = n2_ref[...].T

    width = n2_ref.shape[1]
    n2 = n2_ref[...]
    dy = dy_ref[...]
    wd = wd_ref[...].reshape(FF_TILE, width)
    gate = mm(n2, wg_ref[...].reshape(width, FF_TILE))
    up = mm(n2, wu_ref[...].reshape(width, FF_TILE))
    dhid = mm_nt(dy, wd)
    sig = 1.0 / (1.0 + jnp.exp(-gate))
    act = gate * sig
    hidden = (act * up).astype(bf16)
    dgate = (dhid * up * sig * (1.0 + gate * (1.0 - sig))).astype(bf16)
    dup = (dhid * act).astype(bf16)
    hidden_ref[...] = hidden
    dgate_ref[...] = dgate
    dup_ref[...] = dup

    @pl.when(j >= 2)
    def _():
        for copy in copies(j - 2, slot):
            copy.wait()

    n2t = n2t_ref[...]
    gate_stage[slot] = mm(n2t, dgate).astype(bf16).reshape(gate_stage.shape[1:])
    up_stage[slot] = mm(n2t, dup).astype(bf16).reshape(up_stage.shape[1:])
    down_stage[slot] = mm_tn(hidden, dy).astype(bf16).reshape(down_stage.shape[1:])
    for copy in copies(j, slot):
        copy.start()

    @pl.when(j == last)
    def _():
        for copy in copies(j - 1, 1 - slot):
            copy.wait()
        for copy in copies(j, slot):
            copy.wait()


def ffn_sums_kernel(hidden_ref, dgate_ref, dup_ref, wg_ref, wu_ref, wd_ref, f_ref, dn2_ref):
    width = f_ref.shape[1]
    wg = wg_ref[...].reshape(width, FF_TILE)
    wu = wu_ref[...].reshape(width, FF_TILE)
    wd = wd_ref[...].reshape(FF_TILE, width)

    @pl.when(pl.program_id(0) == 0)
    def _():
        f_ref[...] = jnp.zeros_like(f_ref)
        dn2_ref[...] = jnp.zeros_like(dn2_ref)

    f_ref[...] += mm(hidden_ref[...], wd)
    dn2_ref[...] += mm_nt(dgate_ref[...], wg) + mm_nt(dup_ref[...], wu)


def ffn_blocks(width, devices, rows, blocks):
    parts = width // FF_TILE
    down_rows = blocks * rows
    if devices > 1:
        down_block = (FF_TILE // down_rows, down_rows, width)
        down_map = lambda j: (j, 0, 0)
    else:
        down_block = (1, FF_TILE, width)
        down_map = lambda j: (0, j, 0)
    side_block = (devices, rows, FF_TILE)
    specs = [
        pl.BlockSpec(side_block, lambda j: (0, blocks + j // parts, j % parts)),
        pl.BlockSpec(side_block, lambda j: (0, 2 * blocks + j // parts, j % parts)),
        pl.BlockSpec(down_block, down_map),
    ]
    return specs, side_block, down_block


def ffn_grads(n2, dy, w, devices, rows, blocks):
    tok, width = n2.shape
    ff = blocks * width
    parts = width // FF_TILE
    down_rows = blocks * rows
    w_specs, side_block, down_block = ffn_blocks(width, devices, rows, blocks)

    def places(j):
        cols = pl.ds(pl.multiple_of(lax.rem(j, parts) * FF_TILE, FF_TILE), FF_TILE)
        first = pl.multiple_of(down_rows + (j // parts) * rows, rows)
        second = pl.multiple_of(2 * down_rows + (j // parts) * rows, rows)
        if devices > 1:
            down_at = (pl.ds(j * down_block[0], down_block[0]), pl.ds(0, down_rows))
        else:
            down_at = (slice(None), pl.ds(pl.multiple_of(j * FF_TILE, FF_TILE), FF_TILE))
        return (slice(None), pl.ds(first, rows), cols), (slice(None), pl.ds(second, rows), cols), down_at

    tile = pl.BlockSpec((tok, FF_TILE), lambda j: (0, j))
    return pl.pallas_call(
        functools.partial(ffn_grads_kernel, places),
        name="ffn_grads",
        grid=(ff // FF_TILE,),
        in_specs=[whole((tok, width)), whole((tok, width))] + w_specs,
        out_specs=[tile, tile, tile, pl.BlockSpec(memory_space=pl.ANY)],
        out_shape=[shape_of((tok, ff), bf16)] * 3 + [shape_of((devices, 3 * down_rows, width), bf16)],
        scratch_shapes=[
            pltpu.VMEM((width, tok), bf16),
            pltpu.VMEM((2,) + side_block, bf16),
            pltpu.VMEM((2,) + side_block, bf16),
            pltpu.VMEM((2,) + down_block, bf16),
            pltpu.SemaphoreType.DMA((3, 2)),
        ],
        compiler_params=params(60),
        cost_estimate=cost(50),
    )(n2, dy, w, w, w)


def ffn_sums(hidden, dgate, dup, w, devices, rows, blocks):
    tok, ff = hidden.shape
    width = ff // blocks
    w_specs, _, _ = ffn_blocks(width, devices, rows, blocks)
    tile = pl.BlockSpec((tok, FF_TILE), lambda j: (0, j))
    return pl.pallas_call(
        ffn_sums_kernel,
        name="ffn_sums",
        grid=(ff // FF_TILE,),
        in_specs=[tile, tile, tile] + w_specs,
        out_specs=[whole((tok, width)), whole((tok, width))],
        out_shape=[shape_of((tok, width), f32)] * 2,
        compiler_params=params(60),
        cost_estimate=cost(25),
    )(hidden, dgate, dup, w, w, w)


def pair_grads_kernel(
    places, n2_ref, n2_other_ref, dy_ref, dy_other_ref, wg_ref, wu_ref, wd_ref,
    hidden_ref, dgate_ref, dup_ref, wgc_ref, wuc_ref, wdc_ref, out_ref,
    n2t_ref, gate_stage, up_stage, down_stage, sems,
):
    j = pl.program_id(0)
    last = pl.num_programs(0) - 1
    slot = lax.rem(j, 2)
    core = lax.axis_index("core")
    width = n2_ref.shape[1]
    token_sets = ((n2_ref, dy_ref), (n2_other_ref, dy_other_ref))

    def copies(which, at):
        stages = (gate_stage, up_stage, down_stage)
        return [
            pltpu.make_async_copy(stage.at[at], out_ref.at[place], sems.at[index, at])
            for index, (stage, place) in enumerate(zip(stages, places(which)))
        ]

    @pl.when(j == 0)
    def _():
        n2t_ref[0] = n2_ref[...].T
        n2t_ref[1] = n2_other_ref[...].T

    for chunk in range(FF_TILE // 128):
        cols = slice(chunk * 128, chunk * 128 + 128)
        at = pl.ds(pl.multiple_of(core * 128 + chunk * 256, 128), 128)
        wgc_ref[:, cols] = wg_ref[:, :, at].reshape(width, 128)
        wuc_ref[:, cols] = wu_ref[:, :, at].reshape(width, 128)
        wdc_ref[cols, :] = wd_ref[2 * chunk + core]
    wd = wdc_ref[...]
    for index, (n2_at, dy_at) in enumerate(token_sets):
        n2 = n2_at[...]
        gate = mm(n2, wgc_ref[...])
        up = mm(n2, wuc_ref[...])
        dhid = mm_nt(dy_at[...], wd)
        sig = 1.0 / (1.0 + jnp.exp(-gate))
        act = gate * sig
        hidden_ref[index] = (act * up).astype(bf16)
        dgate_ref[index] = (dhid * up * sig * (1.0 + gate * (1.0 - sig))).astype(bf16)
        dup_ref[index] = (dhid * act).astype(bf16)

    @pl.when(j >= 2)
    def _():
        for copy in copies(j - 2, slot):
            copy.wait()

    def both(left, right):
        return (left(0, right[0]) + left(1, right[1])).astype(bf16)

    side = lambda index, grad: mm(n2t_ref[index], grad)
    down = lambda index, hidden: mm_tn(hidden, token_sets[index][1][...])
    gate_stage[slot] = both(side, dgate_ref).reshape(gate_stage.shape[1:])
    up_stage[slot] = both(side, dup_ref).reshape(up_stage.shape[1:])
    down_stage[slot] = both(down, hidden_ref).reshape(down_stage.shape[1:])
    for copy in copies(j, slot):
        copy.start()

    @pl.when(j == last)
    def _():
        for copy in copies(j - 1, 1 - slot):
            copy.wait()
        for copy in copies(j, slot):
            copy.wait()


def pair_grads(n2, n2_other, dy, dy_other, w, rows, blocks):
    tok, width = n2.shape
    devices = w.shape[0]
    chips = devices // 2
    ff = blocks * width // 2
    parts = width // FF_TILE
    down_rows = blocks * rows
    down_chips = FF_TILE // down_rows

    def places(j):
        cols = pl.ds(pl.multiple_of(lax.rem(j, parts) * FF_TILE, FF_TILE), FF_TILE)
        first = pl.multiple_of(down_rows + (j // parts) * 2 * rows, rows)
        second = pl.multiple_of(2 * down_rows + (j // parts) * 2 * rows, rows)
        return (
            (slice(None), pl.ds(first, 2 * rows), cols),
            (slice(None), pl.ds(second, 2 * rows), cols),
            (pl.ds(j * down_chips, down_chips), pl.ds(0, down_rows)),
        )

    tile = pl.BlockSpec((2, tok, FF_TILE), lambda j: (0, 0, j))
    side = pl.BlockSpec((width, FF_TILE), lambda j: (0, j))
    side_stage = pltpu.VMEM((2, chips, 2 * rows, FF_TILE), bf16)
    return pl.pallas_call(
        functools.partial(pair_grads_kernel, places),
        name="pair_grads",
        grid=(ff // FF_TILE,),
        in_specs=[whole((tok, width))] * 4
        + [
            pl.BlockSpec((devices, rows, width), lambda j: (0, blocks + j, 0)),
            pl.BlockSpec((devices, rows, width), lambda j: (0, 2 * blocks + j, 0)),
            pl.BlockSpec((2 * down_chips, down_rows, width), lambda j: (j, 0, 0)),
        ],
        out_specs=[tile, tile, tile, side, side, pl.BlockSpec((FF_TILE, width), lambda j: (j, 0))]
        + [pl.BlockSpec(memory_space=pl.ANY)],
        out_shape=[shape_of((2, tok, ff), bf16)] * 3
        + [shape_of((width, ff), bf16)] * 2
        + [shape_of((ff, width), bf16), shape_of((chips, 3 * down_rows, width), bf16)],
        scratch_shapes=[
            pltpu.VMEM((2, width, tok), bf16),
            side_stage,
            side_stage,
            pltpu.VMEM((2, down_chips, down_rows, width), bf16),
            pltpu.SemaphoreType.DMA((3, 2)),
        ],
        compiler_params=params(62),
        cost_estimate=cost(53),
    )(n2, n2_other, dy, dy_other, w, w, w)


def pair_sums_kernel(sent, hidden_ref, dgate_ref, dup_ref, wg_ref, wu_ref, wd_ref, *refs):
    f_ref, dn2_ref = refs[-2:]

    @pl.when(pl.program_id(0) == 0)
    def _():
        f_ref[...] = jnp.zeros_like(f_ref)
        dn2_ref[...] = jnp.zeros_like(dn2_ref)

    f_ref[...] += mm(hidden_ref[0], wd_ref[...])
    dn2_ref[...] += mm_nt(dgate_ref[0], wg_ref[...]) + mm_nt(dup_ref[0], wu_ref[...])

    if sent:

        @pl.when(pl.program_id(0) == pl.num_programs(0) - 1)
        def _():
            refs[0][0] = f_ref[...].astype(bf16)
            refs[0][1] = dn2_ref[...].astype(bf16)


def pair_sums(sent, hidden, dgate, dup, wg, wu, wd):
    _, tok, ff = hidden.shape
    width = wd.shape[1]
    tile = pl.BlockSpec((1, tok, FF_TILE), lambda j: (int(sent), 0, j))
    side = pl.BlockSpec((width, FF_TILE), lambda j: (0, j))
    down = pl.BlockSpec((FF_TILE, width), lambda j: (j, 0))
    if sent:
        out = dict(
            out_specs=whole((2, tok, width)),
            out_shape=shape_of((2, tok, width), bf16),
            scratch_shapes=[pltpu.VMEM((tok, width), f32)] * 2,
        )
    else:
        out = dict(out_specs=[whole((tok, width))] * 2, out_shape=[shape_of((tok, width), f32)] * 2)
    return pl.pallas_call(
        functools.partial(pair_sums_kernel, sent),
        name="pair_sums_sent" if sent else "pair_sums_own",
        grid=(ff // FF_TILE,),
        in_specs=[tile, tile, tile, side, side, down],
        compiler_params=params(60),
        cost_estimate=cost(14),
        **out,
    )(hidden, dgate, dup, wg, wu, wd)


def residual_back_kernel(
    paired, h_ref, f_ref, dn2_ref, dy_ref, o_ref, w_ref, gain_ref, ids_ref, *refs,
):
    got_ref, refs = refs[0], refs[paired:]
    out_ref, dh_ref, do_ref, sum_ref = refs[:4]
    dw_refs, acc_ref = refs[4:-1], refs[-1]
    step = pl.program_id(0)
    h = h_ref[...]
    f = f_ref[...]
    dn2 = dn2_ref[...]
    if paired:
        f = f + got_ref[0].astype(f32)
        dn2 = dn2 + got_ref[1].astype(f32)
    y = h + f
    out_ref[...] = y.astype(bf16)
    valid = flag(ids_ref)
    factor = lax.rsqrt(jnp.mean(h * h, axis=-1, keepdims=True) + EPS)
    unit = h * factor
    dunit = dn2 * gain_ref[...]
    inner = jnp.mean(dunit * unit, axis=-1, keepdims=True)
    dh = dy_ref[...].astype(f32) + factor * (dunit - unit * inner)
    dh_ref[...] = dh
    da = dh.astype(bf16)
    do_ref[...] = mm_nt(da, part(w_ref, 0, w_ref.shape[1])).astype(bf16)

    @pl.when(step == 0)
    def _():
        sum_ref[...] = jnp.zeros_like(sum_ref)
        acc_ref[...] = jnp.zeros_like(acc_ref)

    sum_ref[0] += fold_rows(y * y * valid)
    sum_ref[1] += fold_rows(f * f * valid)
    sum_ref[2] += fold_rows(dn2 * unit)
    acc_ref[...] += mm_tn(o_ref[...], da).reshape(acc_ref.shape)

    @pl.when(step == pl.num_programs(0) - 1)
    def _():
        put_grads(dw_refs, acc_ref, 0)


def residual_back(h, f, dn2, dy, o, w, w_spec, gain, ids, grad_shape, got):
    chips, cores, rows_each, _ = grad_shape
    tok, width = h.shape
    row = lambda i: (i, 0)
    rows = pl.BlockSpec((ROWS, width), row)
    return pl.pallas_call(
        functools.partial(residual_back_kernel, len(got)),
        name="residual_back",
        grid=(tok // ROWS,),
        in_specs=[
            rows, rows, rows, rows, rows, w_spec, whole((1, width)),
            pl.BlockSpec((ROWS, ids.shape[1]), row),
        ]
        + [pl.BlockSpec((2, ROWS, width), lambda i: (0, i, 0))] * len(got),
        out_specs=[
            rows,
            rows,
            rows,
            pl.BlockSpec((3, 8, width), lambda i: (0, 0, 0)),
        ]
        + [whole((chips, rows_each, width))] * cores,
        out_shape=[
            shape_of((tok, width), bf16),
            shape_of((tok, width), f32),
            shape_of((tok, width), bf16),
            shape_of((3, 8, width), f32),
        ]
        + [shape_of((chips, rows_each, width), bf16)] * cores,
        scratch_shapes=[pltpu.VMEM(grad_shape, f32)],
        compiler_params=params(),
        cost_estimate=cost(13),
    )(h, f, dn2, dy, o, w, gain, ids, *got)


def project_back_kernel(
    half, cores, own_first, own_last,
    dk_ref, dv_ref, k0_ref, kf_ref, n1_ref, x_ref, cos_ref, sin_ref, gk_ref,
    dq_ref, q0_ref, qf_ref, gq_ref, *refs,
):
    step = pl.program_id(0)
    w_refs, refs = refs[:cores], refs[cores:]
    if half:
        before_ref, own_ref, left_ref, right_ref, gain_ref, rows_ref, *refs = refs
    else:
        dn1_ref, gain_ref, *refs = refs
    dw_refs, (accq_ref, acck_ref, accv_ref, low_ref, full_ref) = refs[:cores], refs[cores:]

    @pl.when(step == 0)
    def _():
        fill_weights(full_ref, w_refs, half)
        accq_ref[...] = jnp.zeros_like(accq_ref)
        acck_ref[...] = jnp.zeros_like(acck_ref)
        accv_ref[...] = jnp.zeros_like(accv_ref)
        gain_ref[...] = jnp.zeros_like(gain_ref)
        if half:
            rows_ref[...] = jnp.zeros_like(rows_ref)

    ones = head_ones(256)
    cosine = cos_ref[...]
    sine = sin_ref[...]
    n1t = n1_ref[...].T

    def through_norm(grad_ref, raw_ref, factor_ref, gain, index):
        for chunk in range(low_ref.shape[1] // 256):
            units, dunits = [], []
            for pair in range(2):
                at = chunk * 256 + pair * 128
                cols = slice(at, at + 128)
                grad = grad_ref[:, cols].astype(f32)
                grad = grad * cosine - swap_halves(grad) * sine
                unit = raw_ref[:, cols] * factor_ref[:, cols]
                gain_ref[index, :, cols] += fold_rows(grad * unit)
                units.append(unit)
                dunits.append(grad * gain)
            cols = slice(chunk * 256, chunk * 256 + 256)
            unit = jnp.concatenate(units, axis=1)
            dunit = jnp.concatenate(dunits, axis=1)
            inner = head_mean(dunit * unit, ones)
            low_ref[:, cols] = (factor_ref[:, cols] * (dunit - unit * inner)).astype(bf16)
        return low_ref[...]

    dk0 = through_norm(dk_ref, k0_ref, kf_ref, gk_ref[...], 0)
    dv = dv_ref[...]
    acck_ref[...] += mm(n1t, dk0).reshape(acck_ref.shape)
    accv_ref[...] += mm(n1t, dv).reshape(accv_ref.shape)
    dn1 = mm_nt(dk0, weight(full_ref, 1)) + mm_nt(dv, weight(full_ref, 2))
    own = (step >= own_first) & (step < own_last)

    def query_part():
        dq0 = through_norm(dq_ref, q0_ref, qf_ref, gq_ref[...], 1)
        accq_ref[...] += mm(n1t, dq0).reshape(accq_ref.shape)
        return mm_nt(dq0, weight(full_ref, 0))

    if half:
        dn1 = dn1 + before_ref[...]
        x = x_ref[...].astype(f32)
        unit = x * lax.rsqrt(jnp.mean(x * x, axis=-1, keepdims=True) + EPS)

        @pl.when(own)
        def _():
            full = dn1 + query_part()
            own_ref[...] = full
            rows_ref[...] += fold_rows(full * unit)

        @pl.when(jnp.logical_not(own))
        def _():
            rows_ref[...] += fold_rows(dn1 * unit)

        @pl.when(step < own_first)
        def _():
            left_ref[...] = dn1.astype(bf16)

        @pl.when(step >= own_last)
        def _():
            right_ref[...] = dn1.astype(bf16)

    else:
        dn1_ref[...] = dn1

        @pl.when(own)
        def _():
            dn1_ref[...] += query_part()

    @pl.when(step == pl.num_programs(0) - 1)
    def _():
        for index, ref in enumerate((accq_ref, acck_ref, accv_ref)):
            put_grads(dw_refs, ref, index * ref.shape[2])


def project_back(half, dq, dk, dv, q0, qf, k0, kf, n1, x_ext, cosine, sine, gq, gk, w, w_rows, before=()):
    ext, width = n1.shape
    tok = q0.shape[0]
    cores = len(w)
    part_width = width // 2
    own_first = HALF // ROWS
    own_last = own_first + tok // ROWS
    w_shape = (w[0].shape[0], w[0].shape[1], part_width)
    acc = pltpu.VMEM((w[0].shape[0], cores, w_rows, part_width), f32)
    row = lambda i: (i, 0)
    own = lambda i: (jnp.clip(i - own_first, 0, own_last - own_first - 1), 0)
    left = lambda i: (jnp.minimum(i, own_first - 1), 0)
    right = lambda i: (jnp.maximum(i - own_last, 0), 0)
    part_row = lambda i: (i, half)
    part_own = lambda i: (own(i)[0], half)
    wide = pl.BlockSpec((ROWS, width), row)
    narrow = pl.BlockSpec((ROWS, 128), row)
    in_specs = [
        pl.BlockSpec((ROWS, part_width), row),
        pl.BlockSpec((ROWS, part_width), row),
        pl.BlockSpec((ROWS, part_width), part_row),
        pl.BlockSpec((ROWS, part_width), part_row),
        wide,
        wide,
        narrow,
        narrow,
        whole((1, 128)),
        pl.BlockSpec((ROWS, part_width), own),
        pl.BlockSpec((ROWS, part_width), part_own),
        pl.BlockSpec((ROWS, part_width), part_own),
        whole((1, 128)),
    ] + [whole(each.shape) for each in w]
    gains = whole((2, 8, part_width))
    if half:
        in_specs += [wide]
        out_specs = [pl.BlockSpec((ROWS, width), place) for place in (own, left, right)] + [gains, whole((8, width))]
        out_shape = [
            shape_of((tok, width), f32),
            shape_of((HALF, width), bf16),
            shape_of((HALF, width), bf16),
            shape_of((2, 8, part_width), f32),
            shape_of((8, width), f32),
        ]
    else:
        out_specs = [wide, gains]
        out_shape = [shape_of((ext, width), f32), shape_of((2, 8, part_width), f32)]
    return pl.pallas_call(
        functools.partial(project_back_kernel, half, cores, own_first, own_last),
        name="project_back",
        grid=(ext // ROWS,),
        in_specs=in_specs,
        out_specs=out_specs + [whole(w_shape)] * cores,
        out_shape=out_shape + [shape_of(w_shape, bf16)] * cores,
        scratch_shapes=[
            acc, acc, acc,
            pltpu.VMEM((ROWS, part_width), bf16),
            pltpu.VMEM((w[0].shape[1] // w_rows, w[0].shape[0], cores, w_rows, part_width), bf16),
        ],
        compiler_params=params(60),
        cost_estimate=cost(24),
    )(dk, dv, k0, kf, n1, x_ext, cosine, sine, gk, dq, q0, qf, gq, *w, *before)


def assemble_kernel(rows, blocks, grads_ref, got_ref, down_ref, gate_ref, up_ref):
    core = lax.axis_index("core")
    width = grads_ref.shape[1]
    down_rows = blocks * rows
    down_ref[...] = grads_ref[0:down_rows, :].astype(f32)
    for index, out_ref in enumerate((gate_ref, up_ref)):
        for block in range(blocks // 2):
            first = down_rows + (index * (blocks // 2) + block) * 2 * rows
            mine = grads_ref[pl.ds(pl.multiple_of(first + core * rows, rows), rows), :].astype(f32)
            other = got_ref[index, block].astype(f32)
            for chunk in range(width // 128):
                at = block * 2 * width + chunk * 256
                cols = slice(chunk * 128, chunk * 128 + 128)
                out_ref[:, pl.ds(pl.multiple_of(at + core * 128, 128), 128)] = mine[:, cols]
                out_ref[:, pl.ds(pl.multiple_of(at + (1 - core) * 128, 128), 128)] = other[:, cols]


def assemble(grads, got, rows, blocks):
    width = grads.shape[1]
    return pl.pallas_call(
        functools.partial(assemble_kernel, rows, blocks),
        name="assemble",
        out_shape=[
            shape_of((blocks * rows, width), f32),
            shape_of((rows, blocks * width), f32),
            shape_of((rows, blocks * width), f32),
        ],
        compiler_params=params(16),
        cost_estimate=cost(2),
    )(grads, got)


def pack_kernel(copies_spread, blocks, rows, wq, wk, wv, wo, wg, wu, wd, attn_out, rest_out, sems):
    width = wq.shape[1]
    jobs = [(wd, rest_out.at[pl.ds(0, blocks * rows)])]
    for index, side in enumerate((wg, wu)):
        for part_at in range(blocks):
            at = (blocks * (1 + index) + part_at) * rows
            jobs.append((side.at[:, pl.ds(part_at * width, width)], rest_out.at[pl.ds(at, rows)]))
    jobs.append((wo, rest_out.at[pl.ds(3 * blocks * rows, rows)]))
    for copy in range(copies_spread):
        for index, each in enumerate((wq, wk, wv)):
            jobs.append((each, attn_out.at[copy, pl.ds(index * rows, rows)]))
    found = [pltpu.make_async_copy(source, target, sems.at[i]) for i, (source, target) in enumerate(jobs)]
    for copy in found:
        copy.start()
    for copy in found:
        copy.wait()


def pack(weights, copies_spread, blocks):
    rows, width = weights[0].shape
    total = (3 * blocks + 1) * rows
    return pl.pallas_call(
        functools.partial(pack_kernel, copies_spread, blocks, rows),
        name="pack",
        in_specs=[pl.BlockSpec(memory_space=pl.ANY)] * 7,
        out_specs=[pl.BlockSpec(memory_space=pl.ANY)] * 2,
        out_shape=[shape_of((copies_spread, 3 * rows, width), bf16), shape_of((total, width), bf16)],
        scratch_shapes=[pltpu.SemaphoreType.DMA((2 + 2 * blocks + 3 * copies_spread,))],
        compiler_params=params(4),
    )(*weights)


def local(
    inputs, seg_ids, var_ids, time_ids, valid_mask,
    w_query, w_key, w_value, w_out, w_gate, w_up, w_down,
    gain_attn, gain_ffn, gain_query, gain_key, variate_bias, out_grad,
):
    axes = ("head", "chip", "core")
    head_count, chip_count, core_count = (lax.axis_size(axis) for axis in axes)
    blk_count = chip_count * core_count
    devices = head_count * blk_count
    chips = head_count * chip_count
    tok, width = inputs.shape[1:]
    heads = variate_bias.shape[1]
    head_dim = gain_query.shape[0]
    rows = w_query.shape[0]
    blocks = w_gate.shape[1] // width
    ext = tok + 2 * HALF
    blk = lax.axis_index("chip") * core_count + lax.axis_index("core")
    place = blk * head_count + lax.axis_index("head")
    fast = rows % 16 == 0
    k_cores, k_devices, k_rows = (core_count, devices, rows) if fast else (1, 1, width)
    k_chips = k_devices // k_cores

    def flat(p):
        return (p % head_count) * blk_count + p // head_count

    onward = [(flat(p), flat(p + 1)) for p in range(devices - 1)]
    back = [(b, a) for a, b in onward]

    def exchange(values, axis):
        return lax.all_to_all(values, axis, split_axis=0, concat_axis=0, tiled=True)

    def swap_cores(values):
        return lax.ppermute(values, "core", [(0, 1), (1, 0)])

    def spread_to_all(full, parts):
        full = exchange(jnp.broadcast_to(full[None], (head_count,) + full.shape), "head")
        full = full.reshape(chips, parts * rows, width)
        other = swap_cores(full)
        if fast:
            return [full, other]
        swapped = lax.axis_index("core") == 1
        both = jnp.stack([jnp.where(swapped, other, full), jnp.where(swapped, full, other)])
        pieces = both.reshape(core_count, chips, parts, rows, width).transpose(2, 1, 0, 3, 4)
        return [pieces.reshape(1, parts * width, width)]

    def total(values):
        return jnp.sum(values.astype(f32), axis=0)

    def reduce_cores(grads, parts):
        wide = grads[0].shape[-1]
        if not fast:
            pieces = grads[0].reshape(parts, chips, core_count, rows, wide).transpose(2, 1, 0, 3, 4)
            core = lax.axis_index("core")
            grads = [lax.dynamic_index_in_dim(pieces, at, 0, False) for at in (core, 1 - core)]
        mine, other = (each.reshape(head_count, chip_count, parts * rows, wide) for each in grads)
        return (mine.astype(f32) + swap_cores(other).astype(f32)).astype(bf16)

    def reduce_heads(grads):
        return total(exchange(grads, "head")).astype(bf16)

    def reduce_chips(grads):
        return total(exchange(grads, "chip"))

    def gather_rest(shard):
        full = lax.all_gather(shard, axes, axis=0, tiled=False)
        if fast:
            return full
        parts = shard.shape[0] // rows
        down = full[:, : blocks * rows].reshape(1, blocks * width, width)
        rest = full[:, blocks * rows :].reshape(devices, parts - blocks, rows, width)
        rest = rest.transpose(1, 0, 2, 3).reshape(1, (parts - blocks) * width, width)
        return jnp.concatenate([down, rest], axis=1)

    def scatter_pair(grads):
        pieces = grads[blocks * rows :].reshape(2, blocks // 2, 2, rows, width)
        other = lax.dynamic_index_in_dim(pieces, 1 - lax.axis_index("core"), 2, False)
        return assemble(grads, swap_cores(other), rows, blocks)

    def scatter_stage(grads, axis):
        return lax.psum_scatter(grads.reshape(-1, width), axis, scatter_dimension=0, tiled=True)

    def scatter_rest(grads):
        if not fast:
            down = grads[0, : blocks * width].reshape(devices, blocks * rows, width)
            rest = grads[0, blocks * width :].reshape(2 * blocks, devices, rows, width).transpose(1, 0, 2, 3)
            grads = jnp.concatenate([down, rest.reshape(devices, -1, width)], axis=1)
        grads = grads.reshape(devices * 3 * blocks * rows, width)
        return lax.psum_scatter(grads, axes, scatter_dimension=0, tiled=True).astype(f32)

    def columns(shard):
        return [shard[:, i * width : (i + 1) * width] for i in range(blocks)]

    def sides(owned):
        return jnp.concatenate([owned[i * rows : (i + 1) * rows] for i in range(blocks)], axis=1)

    if fast:
        attn_part, rest_part = pack((w_query, w_key, w_value, w_out, w_gate, w_up, w_down), chip_count, blocks)
    else:
        attn_part = jnp.concatenate([w_query, w_key, w_value], axis=0)
        attn_part = jnp.broadcast_to(attn_part[None], (chip_count,) + attn_part.shape)
        rest_part = jnp.concatenate([w_down] + columns(w_gate) + columns(w_up) + [w_out], axis=0)
    rest_w = gather_rest(rest_part)
    x = inputs[0]
    attn_w = exchange(attn_part, "chip")
    ids = jnp.stack([seg_ids, var_ids, valid_mask, time_ids]).reshape(4, -1)
    ids = jnp.pad(ids, ((0, 0), (HALF, HALF)))
    ids = lax.dynamic_slice_in_dim(ids, place * tok, ext, 1).T
    own = slice(HALF, HALF + tok)
    quarter = jnp.arange(128) % (head_dim // 2)
    frequency = 10000.0 ** (-quarter.astype(f32) * 2.0 / head_dim)
    angles = ids[:, 3:].astype(f32) * frequency[None, :]
    cosine = jnp.cos(angles)
    sine = jnp.sin(angles) * jnp.where(jnp.arange(128) % head_dim < head_dim // 2, -1.0, 1.0)
    diff = (variate_bias[0] - variate_bias[1]) * LOG2E
    diff_high = lax.reduce_precision(diff, 8, 7)
    diff_low = diff - diff_high
    lane = jnp.arange(128)[None, :]
    diff_rows = jnp.where(lane < LANE_LOW, diff_high[:, None], jnp.where(lane < LANE_CODE, diff_low[:, None], 1.0))
    gq = jnp.tile(gain_query, 2)[None]
    gk = jnp.tile(gain_key, 2)[None]

    before = lax.ppermute(x[tok - HALF :], axes, onward)
    after = lax.ppermute(x[:HALF], axes, back)
    attn_w, before, after, ids, cosine, sine = lax.optimization_barrier((attn_w, before, after, ids, cosine, sine))
    attn_w = spread_to_all(attn_w, 3)
    x_ext = jnp.concatenate([before, x, after], axis=0)

    own_ids = ids[own]

    n1, q0, qf, k0, kf, q, k, v = project(
        x_ext, gain_attn[None], attn_w, k_rows, cosine, sine, gq, gk, ids, diff_rows, tok, heads
    )
    o, qb = attend(q, k, v, own_ids)

    out_spec = pl.BlockSpec((k_devices, k_rows, width), lambda i: (0, 3 * blocks, 0), pipeline_mode=pl.Buffered(1))
    h, n2, branch_sum = branch_forward(o, x, rest_w, out_spec, gain_ffn[None], own_ids)
    dy = out_grad[0]
    if fast:
        *middle, ff_grads = pair_grads(n2, swap_cores(n2), dy, swap_cores(dy), rest_w, rows, blocks)
        ff_grads = scatter_stage(ff_grads, "head")
        got = [swap_cores(pair_sums(True, *middle))]
        f, dn2 = pair_sums(False, *middle)
    else:
        hidden, dgate, dup, ff_grads = ffn_grads(n2, dy, rest_w, k_devices, k_rows, blocks)
        ff_owned = scatter_rest(ff_grads)
        down_owned = ff_owned[: blocks * rows]
        gate_owned = sides(ff_owned[blocks * rows : 2 * blocks * rows])
        up_owned = sides(ff_owned[2 * blocks * rows :])
        got = []
        f, dn2 = ffn_sums(hidden, dgate, dup, rest_w, k_devices, k_rows, blocks)
    layer_out, dh, do, sums, *out_grads = residual_back(
        h, f, dn2, dy, o, rest_w, out_spec, gain_ffn[None], own_ids, (k_chips, k_cores, k_rows, width), got
    )
    early = reduce_cores(out_grads, 1)
    do, early = lax.optimization_barrier((do, early))
    early = reduce_heads(early)
    norms = (q0, qf, k0, kf, n1, x_ext, cosine, sine, gq, gk, attn_w, k_rows)
    dq, dk, dv, bias_first = attend_back(0, qb, k, v, o, do, own_ids)
    dq, early = lax.optimization_barrier((dq, early))
    early_owned = reduce_chips(early)
    dn1_first, gain_first, *grads = project_back(0, dq, dk, dv, *norms)
    grads, early_owned = lax.optimization_barrier((grads, early_owned))
    first_sums = reduce_cores(grads, 3)
    if fast:
        do, first_sums, ff_grads = lax.optimization_barrier((do, first_sums, ff_grads))
        down_owned, gate_owned, up_owned = scatter_pair(scatter_stage(ff_grads, "chip"))
    else:
        do, first_sums = lax.optimization_barrier((do, first_sums))
    first_sums = reduce_heads(first_sums)
    dq, dk, dv, bias_second = attend_back(1, qb, k, v, o, do, own_ids)
    dq, first_sums = lax.optimization_barrier((dq, first_sums))
    first_owned = reduce_chips(first_sums)
    dn1_own, left, right, gain_second, attn_rows, *grads = project_back(1, dq, dk, dv, *norms, (dn1_first,))
    grads, first_owned = lax.optimization_barrier((grads, first_owned))
    second_sums = reduce_cores(grads, 3)
    grad_gain_attn = attn_rows.sum(0)
    bias_rows = jnp.concatenate([bias_first, bias_second], axis=0)
    bias_rows = bias_rows.reshape(heads // 2, 8, 128)[:, :4].reshape(heads, 2, 128)[:, :, 64 : 64 + VARS].sum(-1)
    bias_grad = jnp.stack([bias_rows[:, 0], bias_rows[:, 1] - bias_rows[:, 0]])
    gain_heads = (gain_first + gain_second)[::-1].sum(1).reshape(2, heads // 2, head_dim).sum(1)
    squares = jnp.stack([sums[0].sum(), branch_sum.sum(), sums[1].sum()])
    small = jnp.concatenate(
        [grad_gain_attn, sums[2].sum(0), gain_heads.reshape(-1), bias_grad.reshape(-1), squares]
    )
    filled = -small.shape[0] % 1024
    small = jnp.pad(small, (0, filled)).reshape(-1, 128)
    def doubled(values, axis, count):
        step = 1
        while step < count:
            values = values + lax.ppermute(values, axis, [(i, i ^ step) for i in range(count)])
            step *= 2
        return values

    small = doubled(doubled(small, "core", core_count), "chip", chip_count)
    second_sums, small = lax.optimization_barrier((second_sums, small))
    from_left = lax.ppermute(right, axes, onward)
    from_right = lax.ppermute(left, axes, back)
    second_sums = reduce_heads(second_sums)
    second_sums, from_left, from_right, small = lax.optimization_barrier(
        (second_sums, from_left, from_right, small)
    )
    attn_owned = jnp.concatenate([first_owned, reduce_chips(second_sums)], axis=1)

    dn1 = (
        dn1_own
        + jnp.pad(from_left.astype(f32), ((0, tok - HALF), (0, 0)))
        + jnp.pad(from_right.astype(f32), ((tok - HALF, 0), (0, 0)))
    )
    x_float = x.astype(f32)
    factor = lax.rsqrt(jnp.mean(x_float * x_float, axis=-1, keepdims=True) + EPS)
    unit = x_float * factor
    dunit = dn1 * gain_attn
    inner = jnp.mean(dunit * unit, axis=-1, keepdims=True)
    grad_inputs = (dh + factor * (dunit - unit * inner)).astype(bf16)

    small = doubled(small, "head", head_count).reshape(-1)
    at = 2 * width
    valid_count = jnp.maximum(jnp.sum((valid_mask == 1).astype(f32)), 1.0)
    rms_values = jnp.sqrt(small[at + 2 * head_dim + 2 * heads :][:3] / (valid_count * width))

    return (
        layer_out[None],
        grad_inputs[None],
        attn_owned[:rows],
        attn_owned[rows : 2 * rows],
        attn_owned[2 * rows :],
        early_owned,
        gate_owned,
        up_owned,
        down_owned,
        small[:width],
        small[width : 2 * width],
        small[at : at + head_dim],
        small[at + head_dim : at + 2 * head_dim],
        small[at + 2 * head_dim : at + 2 * head_dim + 2 * heads].reshape(2, heads),
        rms_values,
    )


def solution(mesh):
    heads, blks = mesh.devices.shape
    cores = 2 if blks % 2 == 0 else 1
    mesh = Mesh(mesh.devices.reshape(heads, blks // cores, cores), ("head", "chip", "core"))
    tokens = P(("chip", "core"), "head", None)
    weights = P(("head", "chip", "core"), None)
    in_specs = (tokens,) + (P(),) * 4 + (weights,) * 7 + (P(),) * 5 + (tokens,)
    out_specs = (tokens,) * 2 + (weights,) * 7 + (P(),) * 6
    return jax.shard_map(local, mesh=mesh, in_specs=in_specs, out_specs=out_specs, check_vma=False)
```

```python
import functools

import jax
import jax.numpy as jnp
from jax import lax
from jax.experimental import pallas as pl
from jax.experimental.pallas import tpu as pltpu
from jax.sharding import Mesh
from jax.sharding import PartitionSpec as P

HALF = 512
ROWS = 256
SIDE_ROWS = 384
FF_TILE = 512
VARS = 8
CODES = 8
CODE_SIZE = 64.0
OUTSIDE = 256.0
LOG2E = 1.4426950408889634
EPS = 1e-05
MIB = 1 << 20

LANE_HIGH = 64
LANE_LOW = 72
LANE_CODE = 80
LANE_ONE = 88
LANE_LSE = 90

SEG, VAR, VALID = 0, 1, 2

f32 = jnp.float32
bf16 = jnp.bfloat16
shape_of = jax.ShapeDtypeStruct


def mm(a, b):
    return lax.dot_general(a, b, (((1,), (0,)), ((), ())), preferred_element_type=f32)


def mm_nt(a, b):
    return lax.dot_general(a, b, (((1,), (1,)), ((), ())), preferred_element_type=f32)


def mm_tn(a, b):
    return lax.dot_general(a, b, (((0,), (0,)), ((), ())), preferred_element_type=f32)


def params(vmem=56):
    return pltpu.CompilerParams(vmem_limit_bytes=vmem * MIB)


def cost(us):
    return pl.CostEstimate(flops=int(us * 1e9), bytes_accessed=1 << 20, transcendentals=0)


def whole(shape):
    return pl.BlockSpec(shape, lambda *_: (0,) * len(shape), pipeline_mode=pl.Buffered(1))


def lane_of(shape):
    return lax.broadcasted_iota(jnp.int32, shape, len(shape) - 1)


def row_of(shape):
    return lax.broadcasted_iota(jnp.int32, shape, len(shape) - 2)


def head_ones(size=128):
    shape = (size, size)
    return jnp.where((row_of(shape) // 64) == (lane_of(shape) // 64), 1.0, 0.0).astype(bf16)


def head_mean(values, ones):
    high = values.astype(bf16)
    low = (values - high.astype(f32)).astype(bf16)
    return (mm(high, ones) + mm(low, ones)) * (1.0 / 64.0)


def swap_halves(values):
    first = (lane_of(values.shape) % 64) < 32
    return jnp.where(first, pltpu.roll(values, 96, 1), pltpu.roll(values, 32, 1))


def fold_rows(values):
    rows, width = values.shape
    return jnp.sum(values.reshape(rows // 8, 8, width), axis=0)


def flag(ids_ref, rows=slice(None)):
    return jnp.where(ids_ref[rows, VALID : VALID + 1] == 1, 1.0, 0.0)


def key_extra(ids):
    lane = lane_of((ids.shape[0], 128))
    var = ids[:, VAR : VAR + 1]
    seg = ids[:, SEG : SEG + 1]
    invalid = jnp.where(ids[:, VALID : VALID + 1] == 1, 0.0, 1.0)
    bit = jnp.right_shift(seg, jnp.clip(lane - LANE_CODE, 0, CODES - 1)) & 1
    extra = jnp.where((var == lane - LANE_HIGH) | (var == lane - LANE_LOW) & (lane >= LANE_LOW), 1.0, 0.0)
    extra = jnp.where(lane >= LANE_CODE, CODE_SIZE * (2 * bit - 1).astype(f32), extra)
    extra = jnp.where(lane >= LANE_ONE, -CODE_SIZE * (CODES + 2.0 * invalid), extra)
    extra = jnp.where(lane > LANE_ONE, jnp.where((lane >= LANE_LSE) & (lane < LANE_LSE + 3), 1.0, 0.0), extra)
    return extra


def query_extra(ids):
    lane = lane_of((ids.shape[0], 128))
    var = ids[:, VAR : VAR + 1]
    seg = ids[:, SEG : SEG + 1]
    bit = jnp.right_shift(seg, jnp.clip(lane - LANE_CODE, 0, CODES - 1)) & 1
    extra = jnp.where((var == lane - LANE_HIGH) | (var == lane - LANE_LOW) & (lane >= LANE_LOW), 1.0, 0.0)
    extra = jnp.where(lane >= LANE_CODE, (2 * bit - 1).astype(f32), extra)
    return jnp.where(lane >= LANE_ONE, jnp.where(lane == LANE_ONE, 1.0, 0.0), extra)


def part(ref, index, rows):
    block = ref[:, index * rows : (index + 1) * rows, :]
    return block.reshape(block.shape[0] * rows, block.shape[2])


def core_at(slot, cores):
    if cores == 1:
        return 0
    own = lax.axis_index("core")
    return own if slot == 0 else 1 - own


def fill_weights(full_ref, w_refs, half=0):
    parts, _, cores, rows, width = full_ref.shape
    cols = slice(half * width, (half + 1) * width)
    for slot in range(cores):
        for index in range(parts):
            full_ref[index, :, core_at(slot, cores)] = w_refs[slot][:, index * rows : (index + 1) * rows, cols]


def weight(full_ref, index):
    _, chips, cores, rows, width = full_ref.shape
    return full_ref[index].reshape(chips * cores * rows, width)


def put_grads(out_refs, acc_ref, first):
    _, cores, rows, _ = acc_ref.shape
    for slot in range(cores):
        out_refs[slot][:, first : first + rows, :] = acc_ref[:, core_at(slot, cores)].astype(bf16)


def project_kernel(
    own_first, own_last, cores,
    x_ref, gain_ref, cos_ref, sin_ref, gq_ref, gk_ref, ids_ref, diff_ref, *refs,
):
    w_refs = refs[:cores]
    n1_ref, q0_ref, qf_ref, k0_ref, kf_ref, q_ref, k_ref, v_ref, full_ref = refs[cores:]
    step = pl.program_id(0)

    @pl.when(step == 0)
    def _():
        fill_weights(full_ref, w_refs)

    x = x_ref[...].astype(f32)
    factor = lax.rsqrt(jnp.mean(x * x, axis=-1, keepdims=True) + EPS)
    n1 = (x * factor * gain_ref[...]).astype(bf16)
    n1_ref[...] = n1
    ones = head_ones()
    cosine = cos_ref[...]
    sine = sin_ref[...]
    kaug = key_extra(ids_ref[...])
    own_lane = lane_of(kaug.shape) < 64
    pairs = x.shape[1] // 128

    k0 = mm(n1, weight(full_ref, 1))
    k0_ref[...] = k0
    value = mm(n1, weight(full_ref, 2))
    vaug = jnp.where(lane_of(kaug.shape) < 67, 1.0, 0.0)
    for pair in range(pairs):
        cols = slice(pair * 128, pair * 128 + 128)
        raw = k0[:, cols]
        factor = lax.rsqrt(head_mean(raw * raw, ones) + EPS)
        kf_ref[:, cols] = factor
        normed = raw * factor * gk_ref[...]
        turned = normed * cosine + swap_halves(normed) * sine
        k_ref[2 * pair] = jnp.where(own_lane, turned, kaug).astype(bf16)
        k_ref[2 * pair + 1] = jnp.where(own_lane, pltpu.roll(turned, 64, 1), kaug).astype(bf16)
        val = value[:, cols]
        v_ref[2 * pair] = jnp.where(own_lane, val, vaug).astype(bf16)
        v_ref[2 * pair + 1] = jnp.where(own_lane, pltpu.roll(val, 64, 1), vaug).astype(bf16)

    @pl.when((step >= own_first) & (step < own_last))
    def _():
        q0 = mm(n1, weight(full_ref, 0))
        q0_ref[...] = q0
        qaug = query_extra(ids_ref[...])
        for pair in range(pairs):
            cols = slice(pair * 128, pair * 128 + 128)
            raw = q0[:, cols]
            factor = lax.rsqrt(head_mean(raw * raw, ones) + EPS)
            qf_ref[:, cols] = factor
            normed = raw * factor * gq_ref[...]
            turned = (normed * cosine + swap_halves(normed) * sine) * (0.125 * LOG2E)
            first = qaug * diff_ref[2 * pair : 2 * pair + 1, :]
            second = qaug * diff_ref[2 * pair + 1 : 2 * pair + 2, :]
            q_ref[2 * pair] = jnp.where(own_lane, turned, first).astype(bf16)
            q_ref[2 * pair + 1] = jnp.where(own_lane, pltpu.roll(turned, 64, 1), second).astype(bf16)


def full_weights(w, rows):
    chips, total, width = w[0].shape
    return pltpu.VMEM((total // rows, chips, len(w), rows, width), bf16)


def project(x_ext, gain, w, w_rows, cosine, sine, gq, gk, ids, diff, tok, heads):
    ext, width = x_ext.shape
    own_first = HALF // ROWS
    own_last = own_first + tok // ROWS
    row = lambda i: (i, 0)
    own = lambda i: (jnp.clip(i - own_first, 0, own_last - own_first - 1), 0)
    head_row = lambda i: (0, i, 0)
    head_own = lambda i: (0, own(i)[0], 0)
    return pl.pallas_call(
        functools.partial(project_kernel, own_first, own_last, len(w)),
        name="project",
        grid=(ext // ROWS,),
        in_specs=[
            pl.BlockSpec((ROWS, width), row),
            whole((1, width)),
            pl.BlockSpec((ROWS, 128), row),
            pl.BlockSpec((ROWS, 128), row),
            whole((1, 128)),
            whole((1, 128)),
            pl.BlockSpec((ROWS, ids.shape[1]), row),
            whole(diff.shape),
        ]
        + [whole(each.shape) for each in w],
        out_specs=[
            pl.BlockSpec((ROWS, width), row),
            pl.BlockSpec((ROWS, width), own),
            pl.BlockSpec((ROWS, width), own),
            pl.BlockSpec((ROWS, width), row),
            pl.BlockSpec((ROWS, width), row),
            pl.BlockSpec((heads, ROWS, 128), head_own),
            pl.BlockSpec((heads, ROWS, 128), head_row),
            pl.BlockSpec((heads, ROWS, 128), head_row),
        ],
        out_shape=[
            shape_of((ext, width), bf16),
            shape_of((tok, width), f32),
            shape_of((tok, width), f32),
            shape_of((ext, width), f32),
            shape_of((ext, width), f32),
            shape_of((heads, tok, 128), bf16),
            shape_of((heads, ext, 128), bf16),
            shape_of((heads, ext, 128), bf16),
        ],
        scratch_shapes=[full_weights(w, w_rows)],
        compiler_params=params(),
        cost_estimate=cost(27),
    )(x_ext, gain, cosine, sine, gq, gk, ids, diff, *w)


def fill_masks(ids_ref, diag_ref, edge_ref, key_axis):
    shape = (ROWS, ROWS)
    key = lax.broadcasted_iota(jnp.int32, shape, key_axis)
    query = lax.broadcasted_iota(jnp.int32, shape, 1 - key_axis)
    edge_ref[0] = jnp.where(key > query, 0.0, -OUTSIDE)
    edge_ref[1] = jnp.where(key < query, 0.0, -OUTSIDE)
    for i in range(diag_ref.shape[0] // ROWS):
        rows = slice(i * ROWS, i * ROWS + ROWS)
        diag_ref[rows, :] = jnp.where(key == query, 2.0 * CODE_SIZE * (1.0 - flag(ids_ref, rows)), 0.0)


def attend_kernel(q_ref, k_ref, v_ref, ids_ref, o_ref, qb_ref, diag_ref, edge_ref):
    @pl.when(pl.program_id(0) == 0)
    def _():
        fill_masks(ids_ref, diag_ref, edge_ref, 1)

    tiles = 1 + 2 * HALF // ROWS
    tok = q_ref.shape[1]

    def block(i, carry):
        first_row = pl.multiple_of(i * ROWS, ROWS)
        outs = []
        for head in range(2):
            query = q_ref[head, pl.ds(first_row, ROWS), :]
            total = jnp.zeros((ROWS, 128), f32)
            for j in range(tiles):
                keys = pl.ds(first_row + j * ROWS, ROWS)
                score = mm_nt(query, k_ref[head, keys, :])
                if j == 0:
                    score = score + edge_ref[0]
                elif j == tiles - 1:
                    score = score + edge_ref[1]
                elif j == tiles // 2:
                    score = score + diag_ref[pl.ds(first_row, ROWS), :]
                total = total + mm(jnp.exp2(score).astype(bf16), v_ref[head, keys, :])
            weight = total[:, 64:65]
            outs.append(total / weight)
            lse = jnp.log2(weight)
            high = lse.astype(bf16).astype(f32)
            middle = (lse - high).astype(bf16).astype(f32)
            low = lse - high - middle
            lane = lane_of((ROWS, 128))
            updated = jnp.where(lane == LANE_LSE, -high, query.astype(f32))
            updated = jnp.where(lane == LANE_LSE + 1, -middle, updated)
            updated = jnp.where(lane == LANE_LSE + 2, -low, updated)
            qb_ref[head, pl.ds(first_row, ROWS), :] = updated.astype(bf16)
        lane = lane_of((ROWS, 128))
        joined = jnp.where(lane < 64, outs[0], pltpu.roll(outs[1], 64, 1))
        o_ref[pl.ds(first_row, ROWS), :] = joined.astype(bf16)
        return carry

    lax.fori_loop(0, tok // ROWS, block, 0)


def attend(q, k, v, ids):
    heads, tok, _ = q.shape
    ext = k.shape[1]
    pair = lambda p: (p, 0, 0)
    return pl.pallas_call(
        attend_kernel,
        name="attend",
        grid=(heads // 2,),
        in_specs=[
            pl.BlockSpec((2, tok, 128), pair),
            pl.BlockSpec((2, ext, 128), pair),
            pl.BlockSpec((2, ext, 128), pair),
            whole(ids.shape),
        ],
        out_specs=[
            pl.BlockSpec((tok, 128), lambda p: (0, p)),
            pl.BlockSpec((2, tok, 128), pair),
        ],
        out_shape=[shape_of((tok, heads * 64), bf16), shape_of((heads, tok, 128), bf16)],
        scratch_shapes=[pltpu.VMEM((tok, ROWS), f32), pltpu.VMEM((2, ROWS, ROWS), f32)],
        compiler_params=params(),
        cost_estimate=cost(36),
    )(q, k, v, ids)


def attend_back_kernel(
    tiles, final, q_ref, k_ref, v_ref, o_ref, do_ref, ids_ref, *refs,
):
    sums_ref, refs = refs[0], refs[final:]
    dq_ref, dk_ref, dv_ref, bias_ref, diag_ref, edge_ref, kt_ref, dkey_ref, dval_ref, dout_ref, dqt_ref = refs

    @pl.when(pl.program_id(0) == 0)
    def _():
        fill_masks(ids_ref, diag_ref, edge_ref, 0)

    span = 2 * HALF // ROWS
    tok = q_ref.shape[1]
    blocks = tok // ROWS

    def one_head(head):
        shift = head * 64

        def put(ref, rows, values, added=None):
            turned = pltpu.roll(values, shift, 1) if head else values
            if added is not None:
                turned = turned + added
            if head:
                turned = jnp.where(lane_of(values.shape) < 64, ref[rows, :].astype(f32), turned)
            ref[rows, :] = turned.astype(ref.dtype)

        for i in range(blocks):
            rows = slice(i * ROWS, i * ROWS + ROWS)
            lane = lane_of((ROWS, 128))
            dout = do_ref[rows, :].astype(f32)
            product = o_ref[rows, :].astype(f32) * dout
            if head:
                dout = pltpu.roll(dout, shift, 1)
                product = pltpu.roll(product, shift, 1)
            delta = jnp.sum(jnp.where(lane < 64, product, 0.0), axis=-1, keepdims=True)
            high = delta.astype(bf16).astype(f32)
            middle = (delta - high).astype(bf16).astype(f32)
            low = delta - high - middle
            aug = jnp.where(lane == 64, -high, jnp.where(lane == 65, -middle, jnp.where(lane == 66, -low, 0.0)))
            dout_ref[rows, :] = jnp.where(lane < 64, dout, aug).astype(bf16)

        for at, t in enumerate(tiles):
            kt_ref[:, at * ROWS : (at + 1) * ROWS] = k_ref[head, t * ROWS : (t + 1) * ROWS, :].T

        for i in range(blocks):
            rows = slice(i * ROWS, i * ROWS + ROWS)
            query = q_ref[head, rows, :]
            dout = dout_ref[rows, :]
            group = [(at, t) for at, t in enumerate(tiles) if 0 <= t - i <= span]
            stack = lambda ref: jnp.concatenate([ref[head, t * ROWS : (t + 1) * ROWS, :] for _, t in group], axis=0)
            scores = mm_nt(stack(k_ref), query)
            dweights = mm_nt(stack(v_ref), dout)
            weights, dscores = [], []
            for index, (_, t) in enumerate(group):
                piece = slice(index * ROWS, (index + 1) * ROWS)
                score = scores[piece, :]
                if t == i:
                    score = score + edge_ref[0]
                elif t == i + span:
                    score = score + edge_ref[1]
                elif 2 * (t - i) == span:
                    score = score + diag_ref[rows, :]
                weight = jnp.exp2(score)
                weights.append(weight.astype(bf16))
                dscores.append((weight * dweights[piece, :]).astype(bf16))
            dvals = mm(jnp.concatenate(weights, axis=0), dout)
            dscore = jnp.concatenate(dscores, axis=0)
            dkeys = mm(dscore, query)
            for index, (at, t) in enumerate(group):
                piece = slice(index * ROWS, (index + 1) * ROWS)
                local = slice(at * ROWS, (at + 1) * ROWS)
                if i == max(0, t - span):
                    dval_ref[local, :] = dvals[piece, :]
                    dkey_ref[local, :] = dkeys[piece, :]
                else:
                    dval_ref[local, :] += dvals[piece, :]
                    dkey_ref[local, :] += dkeys[piece, :]
            dqt = mm(kt_ref[:, group[0][0] * ROWS : (group[-1][0] + 1) * ROWS], dscore)
            dqt_ref[:, rows] = dqt
        for at in range(len(tiles)):
            rows = slice(at * ROWS, at * ROWS + ROWS)
            put(dk_ref, rows, dkey_ref[rows, :] * (1.0 / LOG2E))
            put(dv_ref, rows, dval_ref[rows, :])

        dquery = dqt_ref[...].T
        base = query_extra(ids_ref[...])
        bias_ref[2 * head : 2 * head + 1, :] = jnp.sum(dquery * base, axis=0, keepdims=True)
        bias_ref[2 * head + 1 : 2 * head + 2, :] = jnp.sum(dquery, axis=0, keepdims=True)
        put(dq_ref, slice(0, tok), dquery * 0.125, sums_ref[...] if final else None)

    one_head(0)
    one_head(1)


def attend_back(tiles, first_pair, pairs, q, k, v, o, do, ids, sums=()):
    heads, tok, _ = q.shape
    ext = k.shape[1]
    rows = len(tiles) * ROWS
    pair = lambda p: (p + first_pair, 0, 0)
    cols = pl.BlockSpec((tok, 128), lambda p: (0, p + first_pair))
    out = lambda p: (0, p)
    return pl.pallas_call(
        functools.partial(attend_back_kernel, tiles, len(sums)),
        name="attend_back",
        grid=(pairs,),
        in_specs=[
            pl.BlockSpec((2, tok, 128), pair),
            pl.BlockSpec((2, ext, 128), pair),
            pl.BlockSpec((2, ext, 128), pair),
            cols,
            cols,
            whole(ids.shape),
        ]
        + [cols] * len(sums),
        out_specs=[
            pl.BlockSpec((tok, 128), out),
            pl.BlockSpec((rows, 128), out),
            pl.BlockSpec((rows, 128), out),
            pl.BlockSpec((8, 128), lambda p: (p, 0)),
        ],
        out_shape=[
            shape_of((tok, pairs * 128), bf16 if sums else f32),
            shape_of((rows, pairs * 128), bf16),
            shape_of((rows, pairs * 128), bf16),
            shape_of((pairs * 8, 128), f32),
        ],
        scratch_shapes=[
            pltpu.VMEM((tok, ROWS), f32),
            pltpu.VMEM((2, ROWS, ROWS), f32),
            pltpu.VMEM((128, rows), bf16),
            pltpu.VMEM((rows, 128), f32),
            pltpu.VMEM((rows, 128), f32),
            pltpu.VMEM((tok, 128), bf16),
            pltpu.VMEM((128, tok), f32),
        ],
        compiler_params=params(),
        cost_estimate=cost(40 if sums else 30),
    )(q, k, v, o, do, ids, *sums)


def branch_kernel(o_ref, x_ref, w_ref, gain_ref, ids_ref, h_ref, n2_ref, sum_ref):
    branch = mm(o_ref[...], part(w_ref, 0, w_ref.shape[1]))
    h = x_ref[...].astype(f32) + branch
    h_ref[...] = h
    factor = lax.rsqrt(jnp.mean(h * h, axis=-1, keepdims=True) + EPS)
    n2_ref[...] = (h * factor * gain_ref[...]).astype(bf16)

    @pl.when(pl.program_id(0) == 0)
    def _():
        sum_ref[...] = jnp.zeros_like(sum_ref)

    sum_ref[...] += fold_rows(branch * branch * flag(ids_ref))


def branch_forward(o, x, w, w_spec, gain, ids):
    tok, width = x.shape
    row = lambda i: (i, 0)
    return pl.pallas_call(
        branch_kernel,
        name="branch",
        grid=(tok // SIDE_ROWS,),
        in_specs=[
            pl.BlockSpec((SIDE_ROWS, width), row),
            pl.BlockSpec((SIDE_ROWS, width), row),
            w_spec,
            whole((1, width)),
            pl.BlockSpec((SIDE_ROWS, ids.shape[1]), row),
        ],
        out_specs=[
            pl.BlockSpec((SIDE_ROWS, width), row),
            pl.BlockSpec((SIDE_ROWS, width), row),
            pl.BlockSpec((8, width), lambda i: (0, 0)),
        ],
        out_shape=[
            shape_of((tok, width), f32),
            shape_of((tok, width), bf16),
            shape_of((8, width), f32),
        ],
        compiler_params=params(),
        cost_estimate=cost(7),
    )(o, x, w, gain, ids)


def ffn_grads_kernel(
    places, n2_ref, dy_ref, wg_ref, wu_ref, wd_ref,
    hidden_ref, dgate_ref, dup_ref, out_ref,
    n2t_ref, gate_stage, up_stage, down_stage, sems,
):
    j = pl.program_id(0)
    last = pl.num_programs(0) - 1
    slot = lax.rem(j, 2)

    def copies(which, at):
        stages = (gate_stage, up_stage, down_stage)
        return [
            pltpu.make_async_copy(stage.at[at], out_ref.at[place], sems.at[index, at])
            for index, (stage, place) in enumerate(zip(stages, places(which)))
        ]

    @pl.when(j == 0)
    def _():
        n2t_ref[...] = n2_ref[...].T

    width = n2_ref.shape[1]
    n2 = n2_ref[...]
    dy = dy_ref[...]
    wd = wd_ref[...].reshape(FF_TILE, width)
    gate = mm(n2, wg_ref[...].reshape(width, FF_TILE))
    up = mm(n2, wu_ref[...].reshape(width, FF_TILE))
    dhid = mm_nt(dy, wd)
    sig = 1.0 / (1.0 + jnp.exp(-gate))
    act = gate * sig
    hidden = (act * up).astype(bf16)
    dgate = (dhid * up * sig * (1.0 + gate * (1.0 - sig))).astype(bf16)
    dup = (dhid * act).astype(bf16)
    hidden_ref[...] = hidden
    dgate_ref[...] = dgate
    dup_ref[...] = dup

    @pl.when(j >= 2)
    def _():
        for copy in copies(j - 2, slot):
            copy.wait()

    n2t = n2t_ref[...]
    gate_stage[slot] = mm(n2t, dgate).astype(bf16).reshape(gate_stage.shape[1:])
    up_stage[slot] = mm(n2t, dup).astype(bf16).reshape(up_stage.shape[1:])
    down_stage[slot] = mm_tn(hidden, dy).astype(bf16).reshape(down_stage.shape[1:])
    for copy in copies(j, slot):
        copy.start()

    @pl.when(j == last)
    def _():
        for copy in copies(j - 1, 1 - slot):
            copy.wait()
        for copy in copies(j, slot):
            copy.wait()


def ffn_sums_kernel(hidden_ref, dgate_ref, dup_ref, wg_ref, wu_ref, wd_ref, f_ref, dn2_ref):
    width = f_ref.shape[1]
    wg = wg_ref[...].reshape(width, FF_TILE)
    wu = wu_ref[...].reshape(width, FF_TILE)
    wd = wd_ref[...].reshape(FF_TILE, width)

    @pl.when(pl.program_id(0) == 0)
    def _():
        f_ref[...] = jnp.zeros_like(f_ref)
        dn2_ref[...] = jnp.zeros_like(dn2_ref)

    f_ref[...] += mm(hidden_ref[...], wd)
    dn2_ref[...] += mm_nt(dgate_ref[...], wg) + mm_nt(dup_ref[...], wu)


def ffn_blocks(width, devices, rows, blocks):
    parts = width // FF_TILE
    down_rows = blocks * rows
    if devices > 1:
        down_block = (FF_TILE // down_rows, down_rows, width)
        down_map = lambda j: (j, 0, 0)
    else:
        down_block = (1, FF_TILE, width)
        down_map = lambda j: (0, j, 0)
    side_block = (devices, rows, FF_TILE)
    specs = [
        pl.BlockSpec(side_block, lambda j: (0, blocks + j // parts, j % parts)),
        pl.BlockSpec(side_block, lambda j: (0, 2 * blocks + j // parts, j % parts)),
        pl.BlockSpec(down_block, down_map),
    ]
    return specs, side_block, down_block


def ffn_grads(n2, dy, w, devices, rows, blocks):
    tok, width = n2.shape
    ff = blocks * width
    parts = width // FF_TILE
    down_rows = blocks * rows
    w_specs, side_block, down_block = ffn_blocks(width, devices, rows, blocks)

    def places(j):
        cols = pl.ds(pl.multiple_of(lax.rem(j, parts) * FF_TILE, FF_TILE), FF_TILE)
        first = pl.multiple_of(down_rows + (j // parts) * rows, rows)
        second = pl.multiple_of(2 * down_rows + (j // parts) * rows, rows)
        if devices > 1:
            down_at = (pl.ds(j * down_block[0], down_block[0]), pl.ds(0, down_rows))
        else:
            down_at = (slice(None), pl.ds(pl.multiple_of(j * FF_TILE, FF_TILE), FF_TILE))
        return (slice(None), pl.ds(first, rows), cols), (slice(None), pl.ds(second, rows), cols), down_at

    tile = pl.BlockSpec((tok, FF_TILE), lambda j: (0, j))
    return pl.pallas_call(
        functools.partial(ffn_grads_kernel, places),
        name="ffn_grads",
        grid=(ff // FF_TILE,),
        in_specs=[whole((tok, width)), whole((tok, width))] + w_specs,
        out_specs=[tile, tile, tile, pl.BlockSpec(memory_space=pl.ANY)],
        out_shape=[shape_of((tok, ff), bf16)] * 3 + [shape_of((devices, 3 * down_rows, width), bf16)],
        scratch_shapes=[
            pltpu.VMEM((width, tok), bf16),
            pltpu.VMEM((2,) + side_block, bf16),
            pltpu.VMEM((2,) + side_block, bf16),
            pltpu.VMEM((2,) + down_block, bf16),
            pltpu.SemaphoreType.DMA((3, 2)),
        ],
        compiler_params=params(60),
        cost_estimate=cost(50),
    )(n2, dy, w, w, w)


def ffn_sums(hidden, dgate, dup, w, devices, rows, blocks):
    tok, ff = hidden.shape
    width = ff // blocks
    w_specs, _, _ = ffn_blocks(width, devices, rows, blocks)
    tile = pl.BlockSpec((tok, FF_TILE), lambda j: (0, j))
    return pl.pallas_call(
        ffn_sums_kernel,
        name="ffn_sums",
        grid=(ff // FF_TILE,),
        in_specs=[tile, tile, tile] + w_specs,
        out_specs=[whole((tok, width)), whole((tok, width))],
        out_shape=[shape_of((tok, width), f32)] * 2,
        compiler_params=params(60),
        cost_estimate=cost(25),
    )(hidden, dgate, dup, w, w, w)


def pair_grads_kernel(
    places, n2_ref, n2_other_ref, dy_ref, dy_other_ref, wg_ref, wu_ref, wd_ref,
    hidden_ref, dgate_ref, dup_ref, wgc_ref, wuc_ref, wdc_ref, out_ref,
    n2t_ref, gate_stage, up_stage, down_stage, sems,
):
    j = pl.program_id(0)
    last = pl.num_programs(0) - 1
    slot = lax.rem(j, 2)
    core = lax.axis_index("core")
    width = n2_ref.shape[1]
    token_sets = ((n2_ref, dy_ref), (n2_other_ref, dy_other_ref))

    def copies(which, at):
        stages = (gate_stage, up_stage, down_stage)
        return [
            pltpu.make_async_copy(stage.at[at], out_ref.at[place], sems.at[index, at])
            for index, (stage, place) in enumerate(zip(stages, places(which)))
        ]

    @pl.when(j == 0)
    def _():
        n2t_ref[0] = n2_ref[...].T
        n2t_ref[1] = n2_other_ref[...].T

    for chunk in range(FF_TILE // 128):
        cols = slice(chunk * 128, chunk * 128 + 128)
        at = pl.ds(pl.multiple_of(core * 128 + chunk * 256, 128), 128)
        wgc_ref[:, cols] = wg_ref[:, :, at].reshape(width, 128)
        wuc_ref[:, cols] = wu_ref[:, :, at].reshape(width, 128)
        wdc_ref[cols, :] = wd_ref[2 * chunk + core]
    wd = wdc_ref[...]
    for index, (n2_at, dy_at) in enumerate(token_sets):
        n2 = n2_at[...]
        gate = mm(n2, wgc_ref[...])
        up = mm(n2, wuc_ref[...])
        dhid = mm_nt(dy_at[...], wd)
        sig = 1.0 / (1.0 + jnp.exp(-gate))
        act = gate * sig
        hidden_ref[index] = (act * up).astype(bf16)
        dgate_ref[index] = (dhid * up * sig * (1.0 + gate * (1.0 - sig))).astype(bf16)
        dup_ref[index] = (dhid * act).astype(bf16)

    @pl.when(j >= 2)
    def _():
        for copy in copies(j - 2, slot):
            copy.wait()

    def both(left, right):
        return (left(0, right[0]) + left(1, right[1])).astype(bf16)

    side = lambda index, grad: mm(n2t_ref[index], grad)
    down = lambda index, hidden: mm_tn(hidden, token_sets[index][1][...])
    gate_stage[slot] = both(side, dgate_ref).reshape(gate_stage.shape[1:])
    up_stage[slot] = both(side, dup_ref).reshape(up_stage.shape[1:])
    down_stage[slot] = both(down, hidden_ref).reshape(down_stage.shape[1:])
    for copy in copies(j, slot):
        copy.start()

    @pl.when(j == last)
    def _():
        for copy in copies(j - 1, 1 - slot):
            copy.wait()
        for copy in copies(j, slot):
            copy.wait()


def pair_grads(n2, n2_other, dy, dy_other, w, rows, blocks):
    tok, width = n2.shape
    devices = w.shape[0]
    chips = devices // 2
    ff = blocks * width // 2
    parts = width // FF_TILE
    down_rows = blocks * rows
    down_chips = FF_TILE // down_rows

    def places(j):
        cols = pl.ds(pl.multiple_of(lax.rem(j, parts) * FF_TILE, FF_TILE), FF_TILE)
        first = pl.multiple_of(down_rows + (j // parts) * 2 * rows, rows)
        second = pl.multiple_of(2 * down_rows + (j // parts) * 2 * rows, rows)
        return (
            (slice(None), pl.ds(first, 2 * rows), cols),
            (slice(None), pl.ds(second, 2 * rows), cols),
            (pl.ds(j * down_chips, down_chips), pl.ds(0, down_rows)),
        )

    tile = pl.BlockSpec((2, tok, FF_TILE), lambda j: (0, 0, j))
    side = pl.BlockSpec((width, FF_TILE), lambda j: (0, j))
    side_stage = pltpu.VMEM((2, chips, 2 * rows, FF_TILE), bf16)
    return pl.pallas_call(
        functools.partial(pair_grads_kernel, places),
        name="pair_grads",
        grid=(ff // FF_TILE,),
        in_specs=[whole((tok, width))] * 4
        + [
            pl.BlockSpec((devices, rows, width), lambda j: (0, blocks + j, 0)),
            pl.BlockSpec((devices, rows, width), lambda j: (0, 2 * blocks + j, 0)),
            pl.BlockSpec((2 * down_chips, down_rows, width), lambda j: (j, 0, 0)),
        ],
        out_specs=[tile, tile, tile, side, side, pl.BlockSpec((FF_TILE, width), lambda j: (j, 0))]
        + [pl.BlockSpec(memory_space=pl.ANY)],
        out_shape=[shape_of((2, tok, ff), bf16)] * 3
        + [shape_of((width, ff), bf16)] * 2
        + [shape_of((ff, width), bf16), shape_of((chips, 3 * down_rows, width), bf16)],
        scratch_shapes=[
            pltpu.VMEM((2, width, tok), bf16),
            side_stage,
            side_stage,
            pltpu.VMEM((2, down_chips, down_rows, width), bf16),
            pltpu.SemaphoreType.DMA((3, 2)),
        ],
        compiler_params=params(62),
        cost_estimate=cost(53),
    )(n2, n2_other, dy, dy_other, w, w, w)


def pair_sums_kernel(sent, hidden_ref, dgate_ref, dup_ref, wg_ref, wu_ref, wd_ref, *refs):
    f_ref, dn2_ref = refs[-2:]

    @pl.when(pl.program_id(0) == 0)
    def _():
        f_ref[...] = jnp.zeros_like(f_ref)
        dn2_ref[...] = jnp.zeros_like(dn2_ref)

    f_ref[...] += mm(hidden_ref[0], wd_ref[...])
    dn2_ref[...] += mm_nt(dgate_ref[0], wg_ref[...]) + mm_nt(dup_ref[0], wu_ref[...])

    if sent:

        @pl.when(pl.program_id(0) == pl.num_programs(0) - 1)
        def _():
            refs[0][0] = f_ref[...].astype(bf16)
            refs[0][1] = dn2_ref[...].astype(bf16)


def pair_sums(sent, hidden, dgate, dup, wg, wu, wd):
    _, tok, ff = hidden.shape
    width = wd.shape[1]
    tile = pl.BlockSpec((1, tok, FF_TILE), lambda j: (int(sent), 0, j))
    side = pl.BlockSpec((width, FF_TILE), lambda j: (0, j))
    down = pl.BlockSpec((FF_TILE, width), lambda j: (j, 0))
    if sent:
        out = dict(
            out_specs=whole((2, tok, width)),
            out_shape=shape_of((2, tok, width), bf16),
            scratch_shapes=[pltpu.VMEM((tok, width), f32)] * 2,
        )
    else:
        out = dict(out_specs=[whole((tok, width))] * 2, out_shape=[shape_of((tok, width), f32)] * 2)
    return pl.pallas_call(
        functools.partial(pair_sums_kernel, sent),
        name="pair_sums_sent" if sent else "pair_sums_own",
        grid=(ff // FF_TILE,),
        in_specs=[tile, tile, tile, side, side, down],
        compiler_params=params(60),
        cost_estimate=cost(14),
        **out,
    )(hidden, dgate, dup, wg, wu, wd)


def residual_back_kernel(
    paired, h_ref, f_ref, dn2_ref, dy_ref, o_ref, w_ref, gain_ref, ids_ref, *refs,
):
    got_ref, refs = refs[0], refs[paired:]
    out_ref, dh_ref, do_ref, sum_ref = refs[:4]
    dw_refs, acc_ref = refs[4:-1], refs[-1]
    step = pl.program_id(0)
    h = h_ref[...]
    f = f_ref[...]
    dn2 = dn2_ref[...]
    if paired:
        f = f + got_ref[0].astype(f32)
        dn2 = dn2 + got_ref[1].astype(f32)
    y = h + f
    out_ref[...] = y.astype(bf16)
    valid = flag(ids_ref)
    factor = lax.rsqrt(jnp.mean(h * h, axis=-1, keepdims=True) + EPS)
    unit = h * factor
    dunit = dn2 * gain_ref[...]
    inner = jnp.mean(dunit * unit, axis=-1, keepdims=True)
    dh = dy_ref[...].astype(f32) + factor * (dunit - unit * inner)
    dh_ref[...] = dh
    da = dh.astype(bf16)
    do_ref[...] = mm_nt(da, part(w_ref, 0, w_ref.shape[1])).astype(bf16)

    @pl.when(step == 0)
    def _():
        sum_ref[...] = jnp.zeros_like(sum_ref)
        acc_ref[...] = jnp.zeros_like(acc_ref)

    sum_ref[0] += fold_rows(y * y * valid)
    sum_ref[1] += fold_rows(f * f * valid)
    sum_ref[2] += fold_rows(dn2 * unit)
    acc_ref[...] += mm_tn(o_ref[...], da).reshape(acc_ref.shape)

    @pl.when(step == pl.num_programs(0) - 1)
    def _():
        put_grads(dw_refs, acc_ref, 0)


def residual_back(h, f, dn2, dy, o, w, w_spec, gain, ids, grad_shape, got):
    chips, cores, rows_each, _ = grad_shape
    tok, width = h.shape
    row = lambda i: (i, 0)
    rows = pl.BlockSpec((SIDE_ROWS, width), row)
    return pl.pallas_call(
        functools.partial(residual_back_kernel, len(got)),
        name="residual_back",
        grid=(tok // SIDE_ROWS,),
        in_specs=[
            rows, rows, rows, rows, rows, w_spec, whole((1, width)),
            pl.BlockSpec((SIDE_ROWS, ids.shape[1]), row),
        ]
        + [pl.BlockSpec((2, SIDE_ROWS, width), lambda i: (0, i, 0))] * len(got),
        out_specs=[
            rows,
            rows,
            rows,
            pl.BlockSpec((3, 8, width), lambda i: (0, 0, 0)),
        ]
        + [whole((chips, rows_each, width))] * cores,
        out_shape=[
            shape_of((tok, width), bf16),
            shape_of((tok, width), f32),
            shape_of((tok, width), bf16),
            shape_of((3, 8, width), f32),
        ]
        + [shape_of((chips, rows_each, width), bf16)] * cores,
        scratch_shapes=[pltpu.VMEM(grad_shape, f32)],
        compiler_params=params(),
        cost_estimate=cost(13),
    )(h, f, dn2, dy, o, w, gain, ids, *got)


def through_norm(grad_ref, raw_ref, factor_ref, gain, gain_ref, index, low_ref, cosine, sine):
    ones = head_ones(256)
    for chunk in range(low_ref.shape[1] // 256):
        units, dunits = [], []
        for pair in range(2):
            at = chunk * 256 + pair * 128
            cols = slice(at, at + 128)
            grad = grad_ref[:, cols].astype(f32)
            grad = grad * cosine - swap_halves(grad) * sine
            unit = raw_ref[:, cols] * factor_ref[:, cols]
            gain_ref[index, :, cols] += fold_rows(grad * unit)
            units.append(unit)
            dunits.append(grad * gain)
        cols = slice(chunk * 256, chunk * 256 + 256)
        unit = jnp.concatenate(units, axis=1)
        dunit = jnp.concatenate(dunits, axis=1)
        inner = head_mean(dunit * unit, ones)
        low_ref[:, cols] = (factor_ref[:, cols] * (dunit - unit * inner)).astype(bf16)
    return low_ref[...]


def unit_rows(x_ref):
    x = x_ref[...].astype(f32)
    return x * lax.rsqrt(jnp.mean(x * x, axis=-1, keepdims=True) + EPS)


def halo_back_kernel(
    cores, sides,
    dk_ref, dv_ref, k0_ref, kf_ref, n1_ref, x_ref, cos_ref, sin_ref, gk_ref, *refs,
):
    step = pl.program_id(0)
    left_ref, right_ref, gain_ref, rows_ref, acck_ref, accv_ref, low_ref, full_ref = refs[cores:]

    @pl.when(step == 0)
    def _():
        fill_weights(full_ref, refs[:cores])
        for ref in (acck_ref, accv_ref, gain_ref, rows_ref):
            ref[...] = jnp.zeros_like(ref)

    n1t = n1_ref[...].T
    dk0 = through_norm(dk_ref, k0_ref, kf_ref, gk_ref[...], gain_ref, 0, low_ref, cos_ref[...], sin_ref[...])
    dv = dv_ref[...]
    acck_ref[...] += mm(n1t, dk0).reshape(acck_ref.shape)
    accv_ref[...] += mm(n1t, dv).reshape(accv_ref.shape)
    dn1 = mm_nt(dk0, weight(full_ref, 1)) + mm_nt(dv, weight(full_ref, 2))
    rows_ref[...] += fold_rows(dn1 * unit_rows(x_ref))

    @pl.when(step < sides)
    def _():
        left_ref[...] = dn1.astype(bf16)

    @pl.when(step >= sides)
    def _():
        right_ref[...] = dn1.astype(bf16)


def halo_back(dk, dv, k0, kf, n1, x_ext, cosine, sine, gk, w, w_rows):
    ext, width = n1.shape
    cores = len(w)
    sides = HALF // ROWS
    tiles = ext // ROWS - 2 * sides
    acc_shape = (w[0].shape[0], cores, w_rows, width)
    place = lambda i: (jnp.where(i < sides, i, i + tiles), 0)
    wide = pl.BlockSpec((ROWS, width), place)
    narrow = pl.BlockSpec((ROWS, 128), place)
    local_row = pl.BlockSpec((ROWS, width), lambda i: (i, 0))
    return pl.pallas_call(
        functools.partial(halo_back_kernel, cores, sides),
        name="halo_back",
        grid=(2 * sides,),
        in_specs=[local_row, local_row, wide, wide, wide, wide, narrow, narrow, whole((1, 128))]
        + [whole(each.shape) for each in w],
        out_specs=[
            pl.BlockSpec((ROWS, width), lambda i: (jnp.minimum(i, sides - 1), 0)),
            pl.BlockSpec((ROWS, width), lambda i: (jnp.maximum(i - sides, 0), 0)),
            whole((1, 8, width)),
            whole((8, width)),
            whole(acc_shape),
            whole(acc_shape),
        ],
        out_shape=[
            shape_of((HALF, width), bf16),
            shape_of((HALF, width), bf16),
            shape_of((1, 8, width), f32),
            shape_of((8, width), f32),
            shape_of(acc_shape, f32),
            shape_of(acc_shape, f32),
        ],
        scratch_shapes=[pltpu.VMEM((ROWS, width), bf16), full_weights(w, w_rows)],
        compiler_params=params(60),
        cost_estimate=cost(21),
    )(dk, dv, k0, kf, n1, x_ext, cosine, sine, gk, *w)


def project_back_kernel(
    half, cores,
    dk_ref, dv_ref, k0_ref, kf_ref, n1_ref, x_ref, cos_ref, sin_ref, gk_ref,
    dq_ref, q0_ref, qf_ref, gq_ref, firstk_ref, firstv_ref, *refs,
):
    step = pl.program_id(0)
    w_refs, refs = refs[:cores], refs[cores:]
    if half:
        before_ref, dn1_ref, gain_ref, rows_ref, *refs = refs
    else:
        dn1_ref, gain_ref, *refs = refs
    dw_refs, (accq_ref, acck_ref, accv_ref, low_ref, full_ref) = refs[:cores], refs[cores:]

    @pl.when(step == 0)
    def _():
        fill_weights(full_ref, w_refs, half)
        accq_ref[...] = jnp.zeros_like(accq_ref)
        acck_ref[...] = firstk_ref[...]
        accv_ref[...] = firstv_ref[...]
        gain_ref[...] = jnp.zeros_like(gain_ref)
        if half:
            rows_ref[...] = jnp.zeros_like(rows_ref)

    turns = (cos_ref[...], sin_ref[...])
    n1t = n1_ref[...].T
    dv = dv_ref[...]
    accv_ref[...] += mm(n1t, dv).reshape(accv_ref.shape)
    dn1 = mm_nt(dv, weight(full_ref, 2))
    dk0 = through_norm(dk_ref, k0_ref, kf_ref, gk_ref[...], gain_ref, 0, low_ref, *turns)
    acck_ref[...] += mm(n1t, dk0).reshape(acck_ref.shape)
    dn1 = dn1 + mm_nt(dk0, weight(full_ref, 1))
    dq0 = through_norm(dq_ref, q0_ref, qf_ref, gq_ref[...], gain_ref, 1, low_ref, *turns)
    accq_ref[...] += mm(n1t, dq0).reshape(accq_ref.shape)
    dn1 = dn1 + mm_nt(dq0, weight(full_ref, 0))
    if half:
        dn1 = dn1 + before_ref[...]
        rows_ref[...] += fold_rows(dn1 * unit_rows(x_ref))
    dn1_ref[...] = dn1

    @pl.when(step == pl.num_programs(0) - 1)
    def _():
        for index, ref in enumerate((accq_ref, acck_ref, accv_ref)):
            put_grads(dw_refs, ref, index * ref.shape[2])


def project_back(
    half, dq, dk, dv, first_sums, q0, qf, k0, kf, n1, x_ext, cosine, sine, gq, gk, w, w_rows, before=()
):
    ext, width = n1.shape
    tok = q0.shape[0]
    cores = len(w)
    part_width = width // 2
    first = HALF // ROWS
    w_shape = (w[0].shape[0], w[0].shape[1], part_width)
    acc_shape = (w[0].shape[0], cores, w_rows, part_width)
    acc = pltpu.VMEM(acc_shape, f32)
    local_half = pl.BlockSpec((ROWS, part_width), lambda i: (i, half))
    place_half = pl.BlockSpec((ROWS, part_width), lambda i: (i + first, half))
    wide = pl.BlockSpec((ROWS, width), lambda i: (i + first, 0))
    narrow = pl.BlockSpec((ROWS, 128), lambda i: (i + first, 0))
    local_row = pl.BlockSpec((ROWS, width), lambda i: (i, 0))
    sums = pl.BlockSpec(acc_shape, lambda i: (0, 0, 0, half), pipeline_mode=pl.Buffered(1))
    return pl.pallas_call(
        functools.partial(project_back_kernel, half, cores),
        name="project_back",
        grid=(tok // ROWS,),
        in_specs=[
            local_half, local_half, place_half, place_half, wide, wide, narrow, narrow, whole((1, 128)),
            local_half, local_half, local_half, whole((1, 128)), sums, sums,
        ]
        + [whole(each.shape) for each in w]
        + [local_row] * half,
        out_specs=[local_row, whole((2, 8, part_width))] + [whole((8, width))] * half + [whole(w_shape)] * cores,
        out_shape=[shape_of((tok, width), f32), shape_of((2, 8, part_width), f32)]
        + [shape_of((8, width), f32)] * half
        + [shape_of(w_shape, bf16)] * cores,
        scratch_shapes=[
            acc, acc, acc,
            pltpu.VMEM((ROWS, part_width), bf16),
            pltpu.VMEM((w[0].shape[1] // w_rows, w[0].shape[0], cores, w_rows, part_width), bf16),
        ],
        compiler_params=params(60),
        cost_estimate=cost(15),
    )(dk, dv, k0, kf, n1, x_ext, cosine, sine, gk, dq, q0, qf, gq, *first_sums, *w, *before)


def assemble_kernel(rows, blocks, grads_ref, got_ref, down_ref, gate_ref, up_ref):
    core = lax.axis_index("core")
    width = grads_ref.shape[1]
    down_rows = blocks * rows
    down_ref[...] = grads_ref[0:down_rows, :].astype(f32)
    for index, out_ref in enumerate((gate_ref, up_ref)):
        for block in range(blocks // 2):
            first = down_rows + (index * (blocks // 2) + block) * 2 * rows
            mine = grads_ref[pl.ds(pl.multiple_of(first + core * rows, rows), rows), :].astype(f32)
            other = got_ref[index, block].astype(f32)
            for chunk in range(width // 128):
                at = block * 2 * width + chunk * 256
                cols = slice(chunk * 128, chunk * 128 + 128)
                out_ref[:, pl.ds(pl.multiple_of(at + core * 128, 128), 128)] = mine[:, cols]
                out_ref[:, pl.ds(pl.multiple_of(at + (1 - core) * 128, 128), 128)] = other[:, cols]


def assemble(grads, got, rows, blocks):
    width = grads.shape[1]
    return pl.pallas_call(
        functools.partial(assemble_kernel, rows, blocks),
        name="assemble",
        out_shape=[
            shape_of((blocks * rows, width), f32),
            shape_of((rows, blocks * width), f32),
            shape_of((rows, blocks * width), f32),
        ],
        compiler_params=params(16),
        cost_estimate=cost(2),
    )(grads, got)


def pack_kernel(copies_spread, blocks, rows, wq, wk, wv, wo, wg, wu, wd, attn_out, rest_out, sems):
    width = wq.shape[1]
    jobs = [(wd, rest_out.at[pl.ds(0, blocks * rows)])]
    for index, side in enumerate((wg, wu)):
        for part_at in range(blocks):
            at = (blocks * (1 + index) + part_at) * rows
            jobs.append((side.at[:, pl.ds(part_at * width, width)], rest_out.at[pl.ds(at, rows)]))
    jobs.append((wo, rest_out.at[pl.ds(3 * blocks * rows, rows)]))
    for copy in range(copies_spread):
        for index, each in enumerate((wq, wk, wv)):
            jobs.append((each, attn_out.at[copy, pl.ds(index * rows, rows)]))
    found = [pltpu.make_async_copy(source, target, sems.at[i]) for i, (source, target) in enumerate(jobs)]
    for copy in found:
        copy.start()
    for copy in found:
        copy.wait()


def pack(weights, copies_spread, blocks):
    rows, width = weights[0].shape
    total = (3 * blocks + 1) * rows
    return pl.pallas_call(
        functools.partial(pack_kernel, copies_spread, blocks, rows),
        name="pack",
        in_specs=[pl.BlockSpec(memory_space=pl.ANY)] * 7,
        out_specs=[pl.BlockSpec(memory_space=pl.ANY)] * 2,
        out_shape=[shape_of((copies_spread, 3 * rows, width), bf16), shape_of((total, width), bf16)],
        scratch_shapes=[pltpu.SemaphoreType.DMA((2 + 2 * blocks + 3 * copies_spread,))],
        compiler_params=params(4),
    )(*weights)


def local(
    inputs, seg_ids, var_ids, time_ids, valid_mask,
    w_query, w_key, w_value, w_out, w_gate, w_up, w_down,
    gain_attn, gain_ffn, gain_query, gain_key, variate_bias, out_grad,
):
    axes = ("head", "chip", "core")
    head_count, chip_count, core_count = (lax.axis_size(axis) for axis in axes)
    blk_count = chip_count * core_count
    devices = head_count * blk_count
    chips = head_count * chip_count
    tok, width = inputs.shape[1:]
    heads = variate_bias.shape[1]
    head_dim = gain_query.shape[0]
    rows = w_query.shape[0]
    blocks = w_gate.shape[1] // width
    ext = tok + 2 * HALF
    blk = lax.axis_index("chip") * core_count + lax.axis_index("core")
    place = blk * head_count + lax.axis_index("head")
    fast = rows % 16 == 0
    k_cores, k_devices, k_rows = (core_count, devices, rows) if fast else (1, 1, width)
    k_chips = k_devices // k_cores

    def flat(p):
        return (p % head_count) * blk_count + p // head_count

    onward = [(flat(p), flat(p + 1)) for p in range(devices - 1)]
    back = [(b, a) for a, b in onward]

    def exchange(values, axis):
        return lax.all_to_all(values, axis, split_axis=0, concat_axis=0, tiled=True)

    def swap_cores(values):
        return lax.ppermute(values, "core", [(0, 1), (1, 0)])

    def spread_to_all(full, parts):
        full = exchange(jnp.broadcast_to(full[None], (head_count,) + full.shape), "head")
        full = full.reshape(chips, parts * rows, width)
        other = swap_cores(full)
        if fast:
            return [full, other]
        swapped = lax.axis_index("core") == 1
        both = jnp.stack([jnp.where(swapped, other, full), jnp.where(swapped, full, other)])
        pieces = both.reshape(core_count, chips, parts, rows, width).transpose(2, 1, 0, 3, 4)
        return [pieces.reshape(1, parts * width, width)]

    def total(values):
        return jnp.sum(values.astype(f32), axis=0)

    def reduce_cores(grads, parts):
        wide = grads[0].shape[-1]
        if not fast:
            pieces = grads[0].reshape(parts, chips, core_count, rows, wide).transpose(2, 1, 0, 3, 4)
            core = lax.axis_index("core")
            grads = [lax.dynamic_index_in_dim(pieces, at, 0, False) for at in (core, 1 - core)]
        mine, other = (each.reshape(head_count, chip_count, parts * rows, wide) for each in grads)
        return (mine.astype(f32) + swap_cores(other).astype(f32)).astype(bf16)

    def reduce_heads(grads):
        return total(exchange(grads, "head")).astype(bf16)

    def reduce_chips(grads):
        return total(exchange(grads, "chip"))

    def gather_rest(shard):
        full = lax.all_gather(shard, axes, axis=0, tiled=False)
        if fast:
            return full
        parts = shard.shape[0] // rows
        down = full[:, : blocks * rows].reshape(1, blocks * width, width)
        rest = full[:, blocks * rows :].reshape(devices, parts - blocks, rows, width)
        rest = rest.transpose(1, 0, 2, 3).reshape(1, (parts - blocks) * width, width)
        return jnp.concatenate([down, rest], axis=1)

    def scatter_pair(grads):
        pieces = grads[blocks * rows :].reshape(2, blocks // 2, 2, rows, width)
        other = lax.dynamic_index_in_dim(pieces, 1 - lax.axis_index("core"), 2, False)
        return assemble(grads, swap_cores(other), rows, blocks)

    def scatter_stage(grads, axis):
        return lax.psum_scatter(grads.reshape(-1, width), axis, scatter_dimension=0, tiled=True)

    def scatter_rest(grads):
        if not fast:
            down = grads[0, : blocks * width].reshape(devices, blocks * rows, width)
            rest = grads[0, blocks * width :].reshape(2 * blocks, devices, rows, width).transpose(1, 0, 2, 3)
            grads = jnp.concatenate([down, rest.reshape(devices, -1, width)], axis=1)
        grads = grads.reshape(devices * 3 * blocks * rows, width)
        return lax.psum_scatter(grads, axes, scatter_dimension=0, tiled=True).astype(f32)

    def columns(shard):
        return [shard[:, i * width : (i + 1) * width] for i in range(blocks)]

    def sides(owned):
        return jnp.concatenate([owned[i * rows : (i + 1) * rows] for i in range(blocks)], axis=1)

    if fast:
        attn_part, rest_part = pack((w_query, w_key, w_value, w_out, w_gate, w_up, w_down), chip_count, blocks)
    else:
        attn_part = jnp.concatenate([w_query, w_key, w_value], axis=0)
        attn_part = jnp.broadcast_to(attn_part[None], (chip_count,) + attn_part.shape)
        rest_part = jnp.concatenate([w_down] + columns(w_gate) + columns(w_up) + [w_out], axis=0)
    rest_w = gather_rest(rest_part)
    x = inputs[0]
    attn_w = exchange(attn_part, "chip")
    ids = jnp.stack([seg_ids, var_ids, valid_mask, time_ids]).reshape(4, -1)
    ids = jnp.pad(ids, ((0, 0), (HALF, HALF)))
    ids = lax.dynamic_slice_in_dim(ids, place * tok, ext, 1).T
    own = slice(HALF, HALF + tok)
    quarter = jnp.arange(128) % (head_dim // 2)
    frequency = 10000.0 ** (-quarter.astype(f32) * 2.0 / head_dim)
    angles = ids[:, 3:].astype(f32) * frequency[None, :]
    cosine = jnp.cos(angles)
    sine = jnp.sin(angles) * jnp.where(jnp.arange(128) % head_dim < head_dim // 2, -1.0, 1.0)
    diff = (variate_bias[0] - variate_bias[1]) * LOG2E
    diff_high = lax.reduce_precision(diff, 8, 7)
    diff_low = diff - diff_high
    lane = jnp.arange(128)[None, :]
    diff_rows = jnp.where(lane < LANE_LOW, diff_high[:, None], jnp.where(lane < LANE_CODE, diff_low[:, None], 1.0))
    gq = jnp.tile(gain_query, 2)[None]
    gk = jnp.tile(gain_key, 2)[None]

    before = lax.ppermute(x[tok - HALF :], axes, onward)
    after = lax.ppermute(x[:HALF], axes, back)
    attn_w, before, after, ids, cosine, sine = lax.optimization_barrier((attn_w, before, after, ids, cosine, sine))
    attn_w = spread_to_all(attn_w, 3)
    x_ext = jnp.concatenate([before, x, after], axis=0)

    own_ids = ids[own]

    n1, q0, qf, k0, kf, q, k, v = project(
        x_ext, gain_attn[None], attn_w, k_rows, cosine, sine, gq, gk, ids, diff_rows, tok, heads
    )
    o, qb = attend(q, k, v, own_ids)

    out_spec = pl.BlockSpec((k_devices, k_rows, width), lambda i: (0, 3 * blocks, 0), pipeline_mode=pl.Buffered(1))
    h, n2, branch_sum = branch_forward(o, x, rest_w, out_spec, gain_ffn[None], own_ids)
    dy = out_grad[0]
    if fast:
        *middle, ff_grads = pair_grads(n2, swap_cores(n2), dy, swap_cores(dy), rest_w, rows, blocks)
        ff_grads = scatter_stage(ff_grads, "head")
        got = [swap_cores(pair_sums(True, *middle))]
        f, dn2 = pair_sums(False, *middle)
    else:
        hidden, dgate, dup, ff_grads = ffn_grads(n2, dy, rest_w, k_devices, k_rows, blocks)
        ff_owned = scatter_rest(ff_grads)
        down_owned = ff_owned[: blocks * rows]
        gate_owned = sides(ff_owned[blocks * rows : 2 * blocks * rows])
        up_owned = sides(ff_owned[2 * blocks * rows :])
        got = []
        f, dn2 = ffn_sums(hidden, dgate, dup, rest_w, k_devices, k_rows, blocks)
    layer_out, dh, do, sums, *out_grads = residual_back(
        h, f, dn2, dy, o, rest_w, out_spec, gain_ffn[None], own_ids, (k_chips, k_cores, k_rows, width), got
    )
    early = reduce_cores(out_grads, 1)
    do, early = lax.optimization_barrier((do, early))
    early = reduce_heads(early)
    norms = (q0, qf, k0, kf, n1, x_ext, cosine, sine, gq, gk, attn_w, k_rows)
    edge, count = HALF // ROWS, ext // ROWS
    halo_tiles = (*range(edge), *range(count - edge, count))
    own_tiles = tuple(range(edge, count - edge))
    pairs = heads // 2
    attention = (qb, k, v, o)
    dq_sums, dk, dv, bias_halo = attend_back(halo_tiles, 0, pairs, *attention, do, own_ids)
    dk, early = lax.optimization_barrier((dk, early))
    early_owned = reduce_chips(early)
    left, right, gain_halo, rows_halo, *first_sums = halo_back(
        dk, dv, k0, kf, n1, x_ext, cosine, sine, gk, attn_w, k_rows
    )
    from_left = lax.ppermute(right, axes, onward)
    from_right = lax.ppermute(left, axes, back)
    do, early_owned, left = lax.optimization_barrier((do, early_owned, left))
    dq, dk, dv, bias_own = attend_back(own_tiles, 0, pairs, *attention, do, own_ids, (dq_sums,))
    dq, from_left, from_right = lax.optimization_barrier((dq, from_left, from_right))
    if fast:
        dq, ff_grads = lax.optimization_barrier((dq, ff_grads))
        down_owned, gate_owned, up_owned = scatter_pair(scatter_stage(ff_grads, "chip"))
    dn1_first, gain_first, *grads = project_back(0, dq, dk, dv, first_sums, *norms)
    first_grads = reduce_cores(grads, 3)
    bias_rows = bias_halo + bias_own
    bias_rows = bias_rows.reshape(heads // 2, 8, 128)[:, :4].reshape(heads, 2, 128)[:, :, 64 : 64 + VARS].sum(-1)
    bias_grad = jnp.stack([bias_rows[:, 0], bias_rows[:, 1] - bias_rows[:, 0]])

    def gains_of(rows_of):
        found = rows_of.sum(1).reshape(rows_of.shape[0], -1, head_dim).sum(1)
        return jnp.concatenate([found[1], found[0]])

    key_halo = gain_halo[0].sum(0).reshape(heads, head_dim).sum(0)
    gain_heads = gains_of(gain_first) + jnp.pad(key_halo, (head_dim, 0))
    squares = jnp.stack([sums[0].sum(), branch_sum.sum(), sums[1].sum()])
    small = jnp.concatenate([rows_halo.sum(0), sums[2].sum(0), gain_heads, bias_grad.reshape(-1), squares])
    used = small.shape[0]
    small = jnp.pad(small, (0, -used % (4 * width)))
    dq, first_grads, small = lax.optimization_barrier((dq, first_grads, small))
    first_grads = reduce_heads(first_grads)
    dn1_own, gain_second, attn_rows, *grads = project_back(1, dq, dk, dv, first_sums, *norms, (dn1_first,))
    grads, first_grads = lax.optimization_barrier((grads, first_grads))
    second_sums = reduce_cores(grads, 3)
    small = small.at[:width].add(attn_rows.sum(0))
    small = small.at[2 * width : 2 * width + 2 * head_dim].add(gains_of(gain_second))
    half = width // 2
    small = small + swap_cores(small)

    def with_small(values):
        high = lax.reduce_precision(small, 8, 7)
        rows_of = jnp.concatenate([high, small - high]).astype(bf16).reshape(-1, half)
        lead = values.shape[:-2]
        return jnp.concatenate([values, jnp.broadcast_to(rows_of, lead + rows_of.shape)], axis=-2)

    def small_total(values):
        sums_of = jnp.sum(values.reshape(values.shape[0], 2, -1).astype(f32), axis=(0, 1))
        return sums_of

    kept = second_sums.shape[-2]
    second_sums = exchange(with_small(second_sums), "head")
    small = small_total(second_sums[:, 0, kept:])
    second_sums = total(second_sums[:, :, :kept]).astype(bf16)
    second_sums = exchange(jnp.concatenate([first_grads, with_small(second_sums)], axis=-2), "chip")
    small = small_total(second_sums[:, 2 * kept :])
    attn_owned = total(second_sums[:, : 2 * kept])
    attn_owned = jnp.concatenate([attn_owned[:kept], attn_owned[kept:]], axis=1)

    dn1 = (
        dn1_own
        + jnp.pad(from_left.astype(f32), ((0, tok - HALF), (0, 0)))
        + jnp.pad(from_right.astype(f32), ((tok - HALF, 0), (0, 0)))
    )
    x_float = x.astype(f32)
    factor = lax.rsqrt(jnp.mean(x_float * x_float, axis=-1, keepdims=True) + EPS)
    unit = x_float * factor
    dunit = dn1 * gain_attn
    inner = jnp.mean(dunit * unit, axis=-1, keepdims=True)
    grad_inputs = (dh + factor * (dunit - unit * inner)).astype(bf16)

    at = 2 * width
    valid_count = jnp.maximum(jnp.sum((valid_mask == 1).astype(f32)), 1.0)
    rms_values = jnp.sqrt(small[at + 2 * head_dim + 2 * heads :][:3] / (valid_count * width))

    return (
        layer_out[None],
        grad_inputs[None],
        attn_owned[:rows],
        attn_owned[rows : 2 * rows],
        attn_owned[2 * rows :],
        early_owned,
        gate_owned,
        up_owned,
        down_owned,
        small[:width],
        small[width : 2 * width],
        small[at : at + head_dim],
        small[at + head_dim : at + 2 * head_dim],
        small[at + 2 * head_dim : at + 2 * head_dim + 2 * heads].reshape(2, heads),
        rms_values,
    )


def solution(mesh):
    heads, blks = mesh.devices.shape
    cores = 2 if blks % 2 == 0 else 1
    mesh = Mesh(mesh.devices.reshape(heads, blks // cores, cores), ("head", "chip", "core"))
    tokens = P(("chip", "core"), "head", None)
    weights = P(("head", "chip", "core"), None)
    in_specs = (tokens,) + (P(),) * 4 + (weights,) * 7 + (P(),) * 5 + (tokens,)
    out_specs = (tokens,) * 2 + (weights,) * 7 + (P(),) * 6
    return jax.shard_map(local, mesh=mesh, in_specs=in_specs, out_specs=out_specs, check_vma=False)
```

```python
import functools

import jax
import jax.numpy as jnp
from jax import lax
from jax.experimental import pallas as pl
from jax.experimental.pallas import tpu as pltpu
from jax.sharding import Mesh
from jax.sharding import PartitionSpec as P

HALF = 512
ROWS = 256
SIDE_ROWS = 384
FF_TILE = 512
VARS = 8
CODES = 8
CODE_SIZE = 64.0
OUTSIDE = 256.0
LOG2E = 1.4426950408889634
EPS = 1e-05
MIB = 1 << 20

LANE_HIGH = 64
LANE_LOW = 72
LANE_CODE = 80
LANE_ONE = 88
LANE_LSE = 90

SEG, VAR, VALID = 0, 1, 2

f32 = jnp.float32
bf16 = jnp.bfloat16
shape_of = jax.ShapeDtypeStruct


def mm(a, b):
    return lax.dot_general(a, b, (((1,), (0,)), ((), ())), preferred_element_type=f32)


def mm_nt(a, b):
    return lax.dot_general(a, b, (((1,), (1,)), ((), ())), preferred_element_type=f32)


def mm_tn(a, b):
    return lax.dot_general(a, b, (((0,), (0,)), ((), ())), preferred_element_type=f32)


def params(vmem=56):
    return pltpu.CompilerParams(vmem_limit_bytes=vmem * MIB)


def cost(us):
    return pl.CostEstimate(flops=int(us * 1e9), bytes_accessed=1 << 20, transcendentals=0)


def whole(shape):
    return pl.BlockSpec(shape, lambda *_: (0,) * len(shape), pipeline_mode=pl.Buffered(1))


def lane_of(shape):
    return lax.broadcasted_iota(jnp.int32, shape, len(shape) - 1)


def row_of(shape):
    return lax.broadcasted_iota(jnp.int32, shape, len(shape) - 2)


def head_ones(size=128):
    shape = (size, size)
    return jnp.where((row_of(shape) // 64) == (lane_of(shape) // 64), 1.0, 0.0).astype(bf16)


def head_mean(values, ones):
    high = values.astype(bf16)
    low = (values - high.astype(f32)).astype(bf16)
    return (mm(high, ones) + mm(low, ones)) * (1.0 / 64.0)


def swap_halves(values):
    first = (lane_of(values.shape) % 64) < 32
    return jnp.where(first, pltpu.roll(values, 96, 1), pltpu.roll(values, 32, 1))


def fold_rows(values):
    rows, width = values.shape
    return jnp.sum(values.reshape(rows // 8, 8, width), axis=0)


def flag(ids_ref, rows=slice(None)):
    return jnp.where(ids_ref[rows, VALID : VALID + 1] == 1, 1.0, 0.0)


def key_extra(ids):
    lane = lane_of((ids.shape[0], 128))
    var = ids[:, VAR : VAR + 1]
    seg = ids[:, SEG : SEG + 1]
    invalid = jnp.where(ids[:, VALID : VALID + 1] == 1, 0.0, 1.0)
    bit = jnp.right_shift(seg, jnp.clip(lane - LANE_CODE, 0, CODES - 1)) & 1
    extra = jnp.where((var == lane - LANE_HIGH) | (var == lane - LANE_LOW) & (lane >= LANE_LOW), 1.0, 0.0)
    extra = jnp.where(lane >= LANE_CODE, CODE_SIZE * (2 * bit - 1).astype(f32), extra)
    extra = jnp.where(lane >= LANE_ONE, -CODE_SIZE * (CODES + 2.0 * invalid), extra)
    extra = jnp.where(lane > LANE_ONE, jnp.where((lane >= LANE_LSE) & (lane < LANE_LSE + 3), 1.0, 0.0), extra)
    return extra


def query_extra(ids):
    lane = lane_of((ids.shape[0], 128))
    var = ids[:, VAR : VAR + 1]
    seg = ids[:, SEG : SEG + 1]
    bit = jnp.right_shift(seg, jnp.clip(lane - LANE_CODE, 0, CODES - 1)) & 1
    extra = jnp.where((var == lane - LANE_HIGH) | (var == lane - LANE_LOW) & (lane >= LANE_LOW), 1.0, 0.0)
    extra = jnp.where(lane >= LANE_CODE, (2 * bit - 1).astype(f32), extra)
    return jnp.where(lane >= LANE_ONE, jnp.where(lane == LANE_ONE, 1.0, 0.0), extra)


def part(ref, index, rows):
    block = ref[:, index * rows : (index + 1) * rows, :]
    return block.reshape(block.shape[0] * rows, block.shape[2])


def core_at(slot, cores):
    if cores == 1:
        return 0
    own = lax.axis_index("core")
    return own if slot == 0 else 1 - own


def fill_weights(full_ref, w_refs):
    parts, _, cores, rows, _ = full_ref.shape
    for slot in range(cores):
        for index in range(parts):
            full_ref[index, :, core_at(slot, cores)] = w_refs[slot][:, index * rows : (index + 1) * rows, :]


def weight(full_ref, index):
    _, chips, cores, rows, width = full_ref.shape
    return full_ref[index].reshape(chips * cores * rows, width)


def put_grads(out_refs, acc_ref, first):
    _, cores, rows, _ = acc_ref.shape
    for slot in range(cores):
        out_refs[slot][:, first : first + rows, :] = acc_ref[:, core_at(slot, cores)].astype(bf16)


def project_kernel(
    own_first, own_last, cores,
    x_ref, gain_ref, cos_ref, sin_ref, gq_ref, gk_ref, ids_ref, diff_ref, *refs,
):
    w_refs = refs[:cores]
    n1_ref, q0_ref, qf_ref, k0_ref, kf_ref, q_ref, k_ref, v_ref, full_ref = refs[cores:]
    step = pl.program_id(0)

    @pl.when(step == 0)
    def _():
        fill_weights(full_ref, w_refs)

    x = x_ref[...].astype(f32)
    factor = lax.rsqrt(jnp.mean(x * x, axis=-1, keepdims=True) + EPS)
    n1 = (x * factor * gain_ref[...]).astype(bf16)
    n1_ref[...] = n1
    ones = head_ones()
    cosine = cos_ref[...]
    sine = sin_ref[...]
    kaug = key_extra(ids_ref[...])
    own_lane = lane_of(kaug.shape) < 64
    pairs = x.shape[1] // 128

    k0 = mm(n1, weight(full_ref, 1))
    k0_ref[...] = k0
    value = mm(n1, weight(full_ref, 2))
    vaug = jnp.where(lane_of(kaug.shape) < 67, 1.0, 0.0)
    for pair in range(pairs):
        cols = slice(pair * 128, pair * 128 + 128)
        raw = k0[:, cols]
        factor = lax.rsqrt(head_mean(raw * raw, ones) + EPS)
        kf_ref[:, cols] = factor
        normed = raw * factor * gk_ref[...]
        turned = normed * cosine + swap_halves(normed) * sine
        k_ref[2 * pair] = jnp.where(own_lane, turned, kaug).astype(bf16)
        k_ref[2 * pair + 1] = jnp.where(own_lane, pltpu.roll(turned, 64, 1), kaug).astype(bf16)
        val = value[:, cols]
        v_ref[2 * pair] = jnp.where(own_lane, val, vaug).astype(bf16)
        v_ref[2 * pair + 1] = jnp.where(own_lane, pltpu.roll(val, 64, 1), vaug).astype(bf16)

    @pl.when((step >= own_first) & (step < own_last))
    def _():
        q0 = mm(n1, weight(full_ref, 0))
        q0_ref[...] = q0
        qaug = query_extra(ids_ref[...])
        for pair in range(pairs):
            cols = slice(pair * 128, pair * 128 + 128)
            raw = q0[:, cols]
            factor = lax.rsqrt(head_mean(raw * raw, ones) + EPS)
            qf_ref[:, cols] = factor
            normed = raw * factor * gq_ref[...]
            turned = (normed * cosine + swap_halves(normed) * sine) * (0.125 * LOG2E)
            first = qaug * diff_ref[2 * pair : 2 * pair + 1, :]
            second = qaug * diff_ref[2 * pair + 1 : 2 * pair + 2, :]
            q_ref[2 * pair] = jnp.where(own_lane, turned, first).astype(bf16)
            q_ref[2 * pair + 1] = jnp.where(own_lane, pltpu.roll(turned, 64, 1), second).astype(bf16)


def full_weights(w, rows):
    chips, total, width = w[0].shape
    return pltpu.VMEM((total // rows, chips, len(w), rows, width), bf16)


def project(x_ext, gain, w, w_rows, cosine, sine, gq, gk, ids, diff, tok, heads):
    ext, width = x_ext.shape
    own_first = HALF // ROWS
    own_last = own_first + tok // ROWS
    row = lambda i: (i, 0)
    own = lambda i: (jnp.clip(i - own_first, 0, own_last - own_first - 1), 0)
    head_row = lambda i: (0, i, 0)
    head_own = lambda i: (0, own(i)[0], 0)
    return pl.pallas_call(
        functools.partial(project_kernel, own_first, own_last, len(w)),
        name="project",
        grid=(ext // ROWS,),
        in_specs=[
            pl.BlockSpec((ROWS, width), row),
            whole((1, width)),
            pl.BlockSpec((ROWS, 128), row),
            pl.BlockSpec((ROWS, 128), row),
            whole((1, 128)),
            whole((1, 128)),
            pl.BlockSpec((ROWS, ids.shape[1]), row),
            whole(diff.shape),
        ]
        + [whole(each.shape) for each in w],
        out_specs=[
            pl.BlockSpec((ROWS, width), row),
            pl.BlockSpec((ROWS, width), own),
            pl.BlockSpec((ROWS, width), own),
            pl.BlockSpec((ROWS, width), row),
            pl.BlockSpec((ROWS, width), row),
            pl.BlockSpec((heads, ROWS, 128), head_own),
            pl.BlockSpec((heads, ROWS, 128), head_row),
            pl.BlockSpec((heads, ROWS, 128), head_row),
        ],
        out_shape=[
            shape_of((ext, width), bf16),
            shape_of((tok, width), f32),
            shape_of((tok, width), f32),
            shape_of((ext, width), f32),
            shape_of((ext, width), f32),
            shape_of((heads, tok, 128), bf16),
            shape_of((heads, ext, 128), bf16),
            shape_of((heads, ext, 128), bf16),
        ],
        scratch_shapes=[full_weights(w, w_rows)],
        compiler_params=params(),
        cost_estimate=cost(27),
    )(x_ext, gain, cosine, sine, gq, gk, ids, diff, *w)


def fill_masks(ids_ref, diag_ref, edge_ref, key_axis):
    shape = (ROWS, ROWS)
    key = lax.broadcasted_iota(jnp.int32, shape, key_axis)
    query = lax.broadcasted_iota(jnp.int32, shape, 1 - key_axis)
    edge_ref[0] = jnp.where(key > query, 0.0, -OUTSIDE)
    edge_ref[1] = jnp.where(key < query, 0.0, -OUTSIDE)
    for i in range(diag_ref.shape[0] // ROWS):
        rows = slice(i * ROWS, i * ROWS + ROWS)
        diag_ref[rows, :] = jnp.where(key == query, 2.0 * CODE_SIZE * (1.0 - flag(ids_ref, rows)), 0.0)


def attend_kernel(q_ref, k_ref, v_ref, ids_ref, o_ref, qb_ref, diag_ref, edge_ref):
    @pl.when(pl.program_id(0) == 0)
    def _():
        fill_masks(ids_ref, diag_ref, edge_ref, 1)

    tiles = 1 + 2 * HALF // ROWS
    tok = q_ref.shape[1]

    def block(i, carry):
        first_row = pl.multiple_of(i * ROWS, ROWS)
        outs = []
        for head in range(2):
            query = q_ref[head, pl.ds(first_row, ROWS), :]
            total = jnp.zeros((ROWS, 128), f32)
            for j in range(tiles):
                keys = pl.ds(first_row + j * ROWS, ROWS)
                score = mm_nt(query, k_ref[head, keys, :])
                if j == 0:
                    score = score + edge_ref[0]
                elif j == tiles - 1:
                    score = score + edge_ref[1]
                elif j == tiles // 2:
                    score = score + diag_ref[pl.ds(first_row, ROWS), :]
                total = total + mm(jnp.exp2(score).astype(bf16), v_ref[head, keys, :])
            weight = total[:, 64:65]
            outs.append(total / weight)
            lse = jnp.log2(weight)
            high = lse.astype(bf16).astype(f32)
            middle = (lse - high).astype(bf16).astype(f32)
            low = lse - high - middle
            lane = lane_of((ROWS, 128))
            updated = jnp.where(lane == LANE_LSE, -high, query.astype(f32))
            updated = jnp.where(lane == LANE_LSE + 1, -middle, updated)
            updated = jnp.where(lane == LANE_LSE + 2, -low, updated)
            qb_ref[head, pl.ds(first_row, ROWS), :] = updated.astype(bf16)
        lane = lane_of((ROWS, 128))
        joined = jnp.where(lane < 64, outs[0], pltpu.roll(outs[1], 64, 1))
        o_ref[pl.ds(first_row, ROWS), :] = joined.astype(bf16)
        return carry

    lax.fori_loop(0, tok // ROWS, block, 0)


def attend(q, k, v, ids):
    heads, tok, _ = q.shape
    ext = k.shape[1]
    pair = lambda p: (p, 0, 0)
    return pl.pallas_call(
        attend_kernel,
        name="attend",
        grid=(heads // 2,),
        in_specs=[
            pl.BlockSpec((2, tok, 128), pair),
            pl.BlockSpec((2, ext, 128), pair),
            pl.BlockSpec((2, ext, 128), pair),
            whole(ids.shape),
        ],
        out_specs=[
            pl.BlockSpec((tok, 128), lambda p: (0, p)),
            pl.BlockSpec((2, tok, 128), pair),
        ],
        out_shape=[shape_of((tok, heads * 64), bf16), shape_of((heads, tok, 128), bf16)],
        scratch_shapes=[pltpu.VMEM((tok, ROWS), f32), pltpu.VMEM((2, ROWS, ROWS), f32)],
        compiler_params=params(),
        cost_estimate=cost(36),
    )(q, k, v, ids)


def attend_back_kernel(
    tiles, final, q_ref, k_ref, v_ref, o_ref, do_ref, ids_ref, *refs,
):
    sums_ref, refs = refs[0], refs[final:]
    dq_ref, dk_ref, dv_ref, bias_ref, diag_ref, edge_ref, kt_ref, dkey_ref, dval_ref, dout_ref, dqt_ref = refs

    @pl.when(pl.program_id(0) == 0)
    def _():
        fill_masks(ids_ref, diag_ref, edge_ref, 0)

    span = 2 * HALF // ROWS
    tok = q_ref.shape[1]
    blocks = tok // ROWS

    def one_head(head):
        shift = head * 64

        def put(ref, rows, values, added=None):
            turned = pltpu.roll(values, shift, 1) if head else values
            if added is not None:
                turned = turned + added
            if head:
                turned = jnp.where(lane_of(values.shape) < 64, ref[rows, :].astype(f32), turned)
            ref[rows, :] = turned.astype(ref.dtype)

        for i in range(blocks):
            rows = slice(i * ROWS, i * ROWS + ROWS)
            lane = lane_of((ROWS, 128))
            dout = do_ref[rows, :].astype(f32)
            product = o_ref[rows, :].astype(f32) * dout
            if head:
                dout = pltpu.roll(dout, shift, 1)
                product = pltpu.roll(product, shift, 1)
            delta = jnp.sum(jnp.where(lane < 64, product, 0.0), axis=-1, keepdims=True)
            high = delta.astype(bf16).astype(f32)
            middle = (delta - high).astype(bf16).astype(f32)
            low = delta - high - middle
            aug = jnp.where(lane == 64, -high, jnp.where(lane == 65, -middle, jnp.where(lane == 66, -low, 0.0)))
            dout_ref[rows, :] = jnp.where(lane < 64, dout, aug).astype(bf16)

        for at, t in enumerate(tiles):
            kt_ref[:, at * ROWS : (at + 1) * ROWS] = k_ref[head, t * ROWS : (t + 1) * ROWS, :].T

        for i in range(blocks):
            rows = slice(i * ROWS, i * ROWS + ROWS)
            query = q_ref[head, rows, :]
            dout = dout_ref[rows, :]
            group = [(at, t) for at, t in enumerate(tiles) if 0 <= t - i <= span]
            stack = lambda ref: jnp.concatenate([ref[head, t * ROWS : (t + 1) * ROWS, :] for _, t in group], axis=0)
            scores = mm_nt(stack(k_ref), query)
            dweights = mm_nt(stack(v_ref), dout)
            weights, dscores = [], []
            for index, (_, t) in enumerate(group):
                piece = slice(index * ROWS, (index + 1) * ROWS)
                score = scores[piece, :]
                if t == i:
                    score = score + edge_ref[0]
                elif t == i + span:
                    score = score + edge_ref[1]
                elif 2 * (t - i) == span:
                    score = score + diag_ref[rows, :]
                weight = jnp.exp2(score)
                weights.append(weight.astype(bf16))
                dscores.append((weight * dweights[piece, :]).astype(bf16))
            dvals = mm(jnp.concatenate(weights, axis=0), dout)
            dscore = jnp.concatenate(dscores, axis=0)
            dkeys = mm(dscore, query)
            for index, (at, t) in enumerate(group):
                piece = slice(index * ROWS, (index + 1) * ROWS)
                local = slice(at * ROWS, (at + 1) * ROWS)
                if i == max(0, t - span):
                    dval_ref[local, :] = dvals[piece, :]
                    dkey_ref[local, :] = dkeys[piece, :]
                else:
                    dval_ref[local, :] += dvals[piece, :]
                    dkey_ref[local, :] += dkeys[piece, :]
            dqt = mm(kt_ref[:, group[0][0] * ROWS : (group[-1][0] + 1) * ROWS], dscore)
            dqt_ref[:, rows] = dqt
        for at in range(len(tiles)):
            rows = slice(at * ROWS, at * ROWS + ROWS)
            put(dk_ref, rows, dkey_ref[rows, :] * (1.0 / LOG2E))
            put(dv_ref, rows, dval_ref[rows, :])

        dquery = dqt_ref[...].T
        base = query_extra(ids_ref[...])
        bias_ref[2 * head : 2 * head + 1, :] = jnp.sum(dquery * base, axis=0, keepdims=True)
        bias_ref[2 * head + 1 : 2 * head + 2, :] = jnp.sum(dquery, axis=0, keepdims=True)
        put(dq_ref, slice(0, tok), dquery * 0.125, sums_ref[...] if final else None)

    one_head(0)
    one_head(1)


def attend_back(tiles, first_pair, pairs, q, k, v, o, do, ids, sums=()):
    heads, tok, _ = q.shape
    ext = k.shape[1]
    rows = len(tiles) * ROWS
    pair = lambda p: (p + first_pair, 0, 0)
    cols = pl.BlockSpec((tok, 128), lambda p: (0, p + first_pair))
    out = lambda p: (0, p)
    return pl.pallas_call(
        functools.partial(attend_back_kernel, tiles, len(sums)),
        name="attend_back",
        grid=(pairs,),
        in_specs=[
            pl.BlockSpec((2, tok, 128), pair),
            pl.BlockSpec((2, ext, 128), pair),
            pl.BlockSpec((2, ext, 128), pair),
            cols,
            cols,
            whole(ids.shape),
        ]
        + [cols] * len(sums),
        out_specs=[
            pl.BlockSpec((tok, 128), out),
            pl.BlockSpec((rows, 128), out),
            pl.BlockSpec((rows, 128), out),
            pl.BlockSpec((8, 128), lambda p: (p, 0)),
        ],
        out_shape=[
            shape_of((tok, pairs * 128), bf16 if sums else f32),
            shape_of((rows, pairs * 128), bf16),
            shape_of((rows, pairs * 128), bf16),
            shape_of((pairs * 8, 128), f32),
        ],
        scratch_shapes=[
            pltpu.VMEM((tok, ROWS), f32),
            pltpu.VMEM((2, ROWS, ROWS), f32),
            pltpu.VMEM((128, rows), bf16),
            pltpu.VMEM((rows, 128), f32),
            pltpu.VMEM((rows, 128), f32),
            pltpu.VMEM((tok, 128), bf16),
            pltpu.VMEM((128, tok), f32),
        ],
        compiler_params=params(),
        cost_estimate=cost(40 if sums else 30),
    )(q, k, v, o, do, ids, *sums)


def branch_kernel(o_ref, x_ref, w_ref, gain_ref, ids_ref, h_ref, n2_ref, sum_ref):
    branch = mm(o_ref[...], part(w_ref, 0, w_ref.shape[1]))
    h = x_ref[...].astype(f32) + branch
    h_ref[...] = h
    factor = lax.rsqrt(jnp.mean(h * h, axis=-1, keepdims=True) + EPS)
    n2_ref[...] = (h * factor * gain_ref[...]).astype(bf16)

    @pl.when(pl.program_id(0) == 0)
    def _():
        sum_ref[...] = jnp.zeros_like(sum_ref)

    sum_ref[...] += fold_rows(branch * branch * flag(ids_ref))


def branch_forward(o, x, w, w_spec, gain, ids):
    tok, width = x.shape
    row = lambda i: (i, 0)
    return pl.pallas_call(
        branch_kernel,
        name="branch",
        grid=(tok // SIDE_ROWS,),
        in_specs=[
            pl.BlockSpec((SIDE_ROWS, width), row),
            pl.BlockSpec((SIDE_ROWS, width), row),
            w_spec,
            whole((1, width)),
            pl.BlockSpec((SIDE_ROWS, ids.shape[1]), row),
        ],
        out_specs=[
            pl.BlockSpec((SIDE_ROWS, width), row),
            pl.BlockSpec((SIDE_ROWS, width), row),
            pl.BlockSpec((8, width), lambda i: (0, 0)),
        ],
        out_shape=[
            shape_of((tok, width), f32),
            shape_of((tok, width), bf16),
            shape_of((8, width), f32),
        ],
        compiler_params=params(),
        cost_estimate=cost(7),
    )(o, x, w, gain, ids)


def ffn_grads_kernel(
    places, n2_ref, dy_ref, wg_ref, wu_ref, wd_ref,
    hidden_ref, dgate_ref, dup_ref, out_ref,
    n2t_ref, gate_stage, up_stage, down_stage, sems,
):
    j = pl.program_id(0)
    last = pl.num_programs(0) - 1
    slot = lax.rem(j, 2)

    def copies(which, at):
        stages = (gate_stage, up_stage, down_stage)
        return [
            pltpu.make_async_copy(stage.at[at], out_ref.at[place], sems.at[index, at])
            for index, (stage, place) in enumerate(zip(stages, places(which)))
        ]

    @pl.when(j == 0)
    def _():
        n2t_ref[...] = n2_ref[...].T

    width = n2_ref.shape[1]
    n2 = n2_ref[...]
    dy = dy_ref[...]
    wd = wd_ref[...].reshape(FF_TILE, width)
    gate = mm(n2, wg_ref[...].reshape(width, FF_TILE))
    up = mm(n2, wu_ref[...].reshape(width, FF_TILE))
    dhid = mm_nt(dy, wd)
    sig = 1.0 / (1.0 + jnp.exp(-gate))
    act = gate * sig
    hidden = (act * up).astype(bf16)
    dgate = (dhid * up * sig * (1.0 + gate * (1.0 - sig))).astype(bf16)
    dup = (dhid * act).astype(bf16)
    hidden_ref[...] = hidden
    dgate_ref[...] = dgate
    dup_ref[...] = dup

    @pl.when(j >= 2)
    def _():
        for copy in copies(j - 2, slot):
            copy.wait()

    n2t = n2t_ref[...]
    gate_stage[slot] = mm(n2t, dgate).astype(bf16).reshape(gate_stage.shape[1:])
    up_stage[slot] = mm(n2t, dup).astype(bf16).reshape(up_stage.shape[1:])
    down_stage[slot] = mm_tn(hidden, dy).astype(bf16).reshape(down_stage.shape[1:])
    for copy in copies(j, slot):
        copy.start()

    @pl.when(j == last)
    def _():
        for copy in copies(j - 1, 1 - slot):
            copy.wait()
        for copy in copies(j, slot):
            copy.wait()


def ffn_sums_kernel(hidden_ref, dgate_ref, dup_ref, wg_ref, wu_ref, wd_ref, f_ref, dn2_ref):
    width = f_ref.shape[1]
    wg = wg_ref[...].reshape(width, FF_TILE)
    wu = wu_ref[...].reshape(width, FF_TILE)
    wd = wd_ref[...].reshape(FF_TILE, width)

    @pl.when(pl.program_id(0) == 0)
    def _():
        f_ref[...] = jnp.zeros_like(f_ref)
        dn2_ref[...] = jnp.zeros_like(dn2_ref)

    f_ref[...] += mm(hidden_ref[...], wd)
    dn2_ref[...] += mm_nt(dgate_ref[...], wg) + mm_nt(dup_ref[...], wu)


def ffn_blocks(width, devices, rows, blocks):
    parts = width // FF_TILE
    down_rows = blocks * rows
    if devices > 1:
        down_block = (FF_TILE // down_rows, down_rows, width)
        down_map = lambda j: (j, 0, 0)
    else:
        down_block = (1, FF_TILE, width)
        down_map = lambda j: (0, j, 0)
    side_block = (devices, rows, FF_TILE)
    specs = [
        pl.BlockSpec(side_block, lambda j: (0, blocks + j // parts, j % parts)),
        pl.BlockSpec(side_block, lambda j: (0, 2 * blocks + j // parts, j % parts)),
        pl.BlockSpec(down_block, down_map),
    ]
    return specs, side_block, down_block


def ffn_grads(n2, dy, w, devices, rows, blocks):
    tok, width = n2.shape
    ff = blocks * width
    parts = width // FF_TILE
    down_rows = blocks * rows
    w_specs, side_block, down_block = ffn_blocks(width, devices, rows, blocks)

    def places(j):
        cols = pl.ds(pl.multiple_of(lax.rem(j, parts) * FF_TILE, FF_TILE), FF_TILE)
        first = pl.multiple_of(down_rows + (j // parts) * rows, rows)
        second = pl.multiple_of(2 * down_rows + (j // parts) * rows, rows)
        if devices > 1:
            down_at = (pl.ds(j * down_block[0], down_block[0]), pl.ds(0, down_rows))
        else:
            down_at = (slice(None), pl.ds(pl.multiple_of(j * FF_TILE, FF_TILE), FF_TILE))
        return (slice(None), pl.ds(first, rows), cols), (slice(None), pl.ds(second, rows), cols), down_at

    tile = pl.BlockSpec((tok, FF_TILE), lambda j: (0, j))
    return pl.pallas_call(
        functools.partial(ffn_grads_kernel, places),
        name="ffn_grads",
        grid=(ff // FF_TILE,),
        in_specs=[whole((tok, width)), whole((tok, width))] + w_specs,
        out_specs=[tile, tile, tile, pl.BlockSpec(memory_space=pl.ANY)],
        out_shape=[shape_of((tok, ff), bf16)] * 3 + [shape_of((devices, 3 * down_rows, width), bf16)],
        scratch_shapes=[
            pltpu.VMEM((width, tok), bf16),
            pltpu.VMEM((2,) + side_block, bf16),
            pltpu.VMEM((2,) + side_block, bf16),
            pltpu.VMEM((2,) + down_block, bf16),
            pltpu.SemaphoreType.DMA((3, 2)),
        ],
        compiler_params=params(60),
        cost_estimate=cost(50),
    )(n2, dy, w, w, w)


def ffn_sums(hidden, dgate, dup, w, devices, rows, blocks):
    tok, ff = hidden.shape
    width = ff // blocks
    w_specs, _, _ = ffn_blocks(width, devices, rows, blocks)
    tile = pl.BlockSpec((tok, FF_TILE), lambda j: (0, j))
    return pl.pallas_call(
        ffn_sums_kernel,
        name="ffn_sums",
        grid=(ff // FF_TILE,),
        in_specs=[tile, tile, tile] + w_specs,
        out_specs=[whole((tok, width)), whole((tok, width))],
        out_shape=[shape_of((tok, width), f32)] * 2,
        compiler_params=params(60),
        cost_estimate=cost(25),
    )(hidden, dgate, dup, w, w, w)


def pair_grads_kernel(
    places, n2_ref, n2_other_ref, dy_ref, dy_other_ref, wg_ref, wu_ref, wd_ref,
    hidden_ref, dgate_ref, dup_ref, wgc_ref, wuc_ref, wdc_ref, out_ref,
    n2t_ref, gate_stage, up_stage, down_stage, sems,
):
    j = pl.program_id(0)
    last = pl.num_programs(0) - 1
    slot = lax.rem(j, 2)
    core = lax.axis_index("core")
    width = n2_ref.shape[1]
    token_sets = ((n2_ref, dy_ref), (n2_other_ref, dy_other_ref))

    def copies(which, at):
        stages = (gate_stage, up_stage, down_stage)
        return [
            pltpu.make_async_copy(stage.at[at], out_ref.at[place], sems.at[index, at])
            for index, (stage, place) in enumerate(zip(stages, places(which)))
        ]

    @pl.when(j == 0)
    def _():
        n2t_ref[0] = n2_ref[...].T
        n2t_ref[1] = n2_other_ref[...].T

    for chunk in range(FF_TILE // 128):
        cols = slice(chunk * 128, chunk * 128 + 128)
        at = pl.ds(pl.multiple_of(core * 128 + chunk * 256, 128), 128)
        wgc_ref[:, cols] = wg_ref[:, :, at].reshape(width, 128)
        wuc_ref[:, cols] = wu_ref[:, :, at].reshape(width, 128)
        wdc_ref[cols, :] = wd_ref[2 * chunk + core]
    wd = wdc_ref[...]
    for index, (n2_at, dy_at) in enumerate(token_sets):
        n2 = n2_at[...]
        gate = mm(n2, wgc_ref[...])
        up = mm(n2, wuc_ref[...])
        dhid = mm_nt(dy_at[...], wd)
        sig = 1.0 / (1.0 + jnp.exp(-gate))
        act = gate * sig
        hidden_ref[index] = (act * up).astype(bf16)
        dgate_ref[index] = (dhid * up * sig * (1.0 + gate * (1.0 - sig))).astype(bf16)
        dup_ref[index] = (dhid * act).astype(bf16)

    @pl.when(j >= 2)
    def _():
        for copy in copies(j - 2, slot):
            copy.wait()

    def both(left, right):
        return (left(0, right[0]) + left(1, right[1])).astype(bf16)

    side = lambda index, grad: mm(n2t_ref[index], grad)
    down = lambda index, hidden: mm_tn(hidden, token_sets[index][1][...])
    gate_stage[slot] = both(side, dgate_ref).reshape(gate_stage.shape[1:])
    up_stage[slot] = both(side, dup_ref).reshape(up_stage.shape[1:])
    down_stage[slot] = both(down, hidden_ref).reshape(down_stage.shape[1:])
    for copy in copies(j, slot):
        copy.start()

    @pl.when(j == last)
    def _():
        for copy in copies(j - 1, 1 - slot):
            copy.wait()
        for copy in copies(j, slot):
            copy.wait()


def pair_grads(n2, n2_other, dy, dy_other, w, rows, blocks):
    tok, width = n2.shape
    devices = w.shape[0]
    chips = devices // 2
    ff = blocks * width // 2
    parts = width // FF_TILE
    down_rows = blocks * rows
    down_chips = FF_TILE // down_rows

    def places(j):
        cols = pl.ds(pl.multiple_of(lax.rem(j, parts) * FF_TILE, FF_TILE), FF_TILE)
        first = pl.multiple_of(down_rows + (j // parts) * 2 * rows, rows)
        second = pl.multiple_of(2 * down_rows + (j // parts) * 2 * rows, rows)
        return (
            (slice(None), pl.ds(first, 2 * rows), cols),
            (slice(None), pl.ds(second, 2 * rows), cols),
            (pl.ds(j * down_chips, down_chips), pl.ds(0, down_rows)),
        )

    tile = pl.BlockSpec((2, tok, FF_TILE), lambda j: (0, 0, j))
    side = pl.BlockSpec((width, FF_TILE), lambda j: (0, j))
    side_stage = pltpu.VMEM((2, chips, 2 * rows, FF_TILE), bf16)
    return pl.pallas_call(
        functools.partial(pair_grads_kernel, places),
        name="pair_grads",
        grid=(ff // FF_TILE,),
        in_specs=[whole((tok, width))] * 4
        + [
            pl.BlockSpec((devices, rows, width), lambda j: (0, blocks + j, 0)),
            pl.BlockSpec((devices, rows, width), lambda j: (0, 2 * blocks + j, 0)),
            pl.BlockSpec((2 * down_chips, down_rows, width), lambda j: (j, 0, 0)),
        ],
        out_specs=[tile, tile, tile, side, side, pl.BlockSpec((FF_TILE, width), lambda j: (j, 0))]
        + [pl.BlockSpec(memory_space=pl.ANY)],
        out_shape=[shape_of((2, tok, ff), bf16)] * 3
        + [shape_of((width, ff), bf16)] * 2
        + [shape_of((ff, width), bf16), shape_of((chips, 3 * down_rows, width), bf16)],
        scratch_shapes=[
            pltpu.VMEM((2, width, tok), bf16),
            side_stage,
            side_stage,
            pltpu.VMEM((2, down_chips, down_rows, width), bf16),
            pltpu.SemaphoreType.DMA((3, 2)),
        ],
        compiler_params=params(62),
        cost_estimate=cost(53),
    )(n2, n2_other, dy, dy_other, w, w, w)


def pair_sums_kernel(sent, hidden_ref, dgate_ref, dup_ref, wg_ref, wu_ref, wd_ref, *refs):
    f_ref, dn2_ref = refs[-2:]

    @pl.when(pl.program_id(0) == 0)
    def _():
        f_ref[...] = jnp.zeros_like(f_ref)
        dn2_ref[...] = jnp.zeros_like(dn2_ref)

    f_ref[...] += mm(hidden_ref[0], wd_ref[...])
    dn2_ref[...] += mm_nt(dgate_ref[0], wg_ref[...]) + mm_nt(dup_ref[0], wu_ref[...])

    if sent:

        @pl.when(pl.program_id(0) == pl.num_programs(0) - 1)
        def _():
            refs[0][0] = f_ref[...].astype(bf16)
            refs[0][1] = dn2_ref[...].astype(bf16)


def pair_sums(sent, hidden, dgate, dup, wg, wu, wd):
    _, tok, ff = hidden.shape
    width = wd.shape[1]
    tile = pl.BlockSpec((1, tok, FF_TILE), lambda j: (int(sent), 0, j))
    side = pl.BlockSpec((width, FF_TILE), lambda j: (0, j))
    down = pl.BlockSpec((FF_TILE, width), lambda j: (j, 0))
    if sent:
        out = dict(
            out_specs=whole((2, tok, width)),
            out_shape=shape_of((2, tok, width), bf16),
            scratch_shapes=[pltpu.VMEM((tok, width), f32)] * 2,
        )
    else:
        out = dict(out_specs=[whole((tok, width))] * 2, out_shape=[shape_of((tok, width), f32)] * 2)
    return pl.pallas_call(
        functools.partial(pair_sums_kernel, sent),
        name="pair_sums_sent" if sent else "pair_sums_own",
        grid=(ff // FF_TILE,),
        in_specs=[tile, tile, tile, side, side, down],
        compiler_params=params(60),
        cost_estimate=cost(14),
        **out,
    )(hidden, dgate, dup, wg, wu, wd)


def residual_back_kernel(
    paired, h_ref, f_ref, dn2_ref, dy_ref, o_ref, w_ref, gain_ref, ids_ref, *refs,
):
    got_ref, refs = refs[0], refs[paired:]
    out_ref, dh_ref, do_ref, sum_ref = refs[:4]
    dw_refs, acc_ref = refs[4:-1], refs[-1]
    step = pl.program_id(0)
    h = h_ref[...]
    f = f_ref[...]
    dn2 = dn2_ref[...]
    if paired:
        f = f + got_ref[0].astype(f32)
        dn2 = dn2 + got_ref[1].astype(f32)
    y = h + f
    out_ref[...] = y.astype(bf16)
    valid = flag(ids_ref)
    factor = lax.rsqrt(jnp.mean(h * h, axis=-1, keepdims=True) + EPS)
    unit = h * factor
    dunit = dn2 * gain_ref[...]
    inner = jnp.mean(dunit * unit, axis=-1, keepdims=True)
    dh = dy_ref[...].astype(f32) + factor * (dunit - unit * inner)
    dh_ref[...] = dh
    da = dh.astype(bf16)
    do_ref[...] = mm_nt(da, part(w_ref, 0, w_ref.shape[1])).astype(bf16)

    @pl.when(step == 0)
    def _():
        sum_ref[...] = jnp.zeros_like(sum_ref)
        acc_ref[...] = jnp.zeros_like(acc_ref)

    sum_ref[0] += fold_rows(y * y * valid)
    sum_ref[1] += fold_rows(f * f * valid)
    sum_ref[2] += fold_rows(dn2 * unit)
    acc_ref[...] += mm_tn(o_ref[...], da).reshape(acc_ref.shape)

    @pl.when(step == pl.num_programs(0) - 1)
    def _():
        put_grads(dw_refs, acc_ref, 0)


def residual_back(h, f, dn2, dy, o, w, w_spec, gain, ids, grad_shape, got):
    chips, cores, rows_each, _ = grad_shape
    tok, width = h.shape
    row = lambda i: (i, 0)
    rows = pl.BlockSpec((SIDE_ROWS, width), row)
    return pl.pallas_call(
        functools.partial(residual_back_kernel, len(got)),
        name="residual_back",
        grid=(tok // SIDE_ROWS,),
        in_specs=[
            rows, rows, rows, rows, rows, w_spec, whole((1, width)),
            pl.BlockSpec((SIDE_ROWS, ids.shape[1]), row),
        ]
        + [pl.BlockSpec((2, SIDE_ROWS, width), lambda i: (0, i, 0))] * len(got),
        out_specs=[
            rows,
            rows,
            rows,
            pl.BlockSpec((3, 8, width), lambda i: (0, 0, 0)),
        ]
        + [whole((chips, rows_each, width))] * cores,
        out_shape=[
            shape_of((tok, width), bf16),
            shape_of((tok, width), f32),
            shape_of((tok, width), bf16),
            shape_of((3, 8, width), f32),
        ]
        + [shape_of((chips, rows_each, width), bf16)] * cores,
        scratch_shapes=[pltpu.VMEM(grad_shape, f32)],
        compiler_params=params(),
        cost_estimate=cost(13),
    )(h, f, dn2, dy, o, w, gain, ids, *got)


CHUNK = 256


def through_norm(grad_ref, raws, factors, gain, gain_ref, index, low_ref, turns):
    ones = head_ones(CHUNK)
    for tile, (raw_ref, factor_ref, (cosine, sine)) in enumerate(zip(raws, factors, turns)):
        rows = slice(tile * ROWS, tile * ROWS + ROWS)
        units, dunits = [], []
        for pair in range(CHUNK // 128):
            cols = slice(pair * 128, pair * 128 + 128)
            grad = grad_ref[rows, cols].astype(f32)
            grad = grad * cosine - swap_halves(grad) * sine
            unit = raw_ref[:, cols] * factor_ref[:, cols]
            gain_ref[index, :, cols] += fold_rows(grad * unit)
            units.append(unit)
            dunits.append(grad * gain)
        unit = jnp.concatenate(units, axis=1)
        dunit = jnp.concatenate(dunits, axis=1)
        inner = head_mean(dunit * unit, ones)
        low_ref[rows, :] = (factor_ref[...] * (dunit - unit * inner)).astype(bf16)
    return low_ref[...]


def unit_rows(x_ref):
    x = x_ref[...].astype(f32)
    return x * lax.rsqrt(jnp.mean(x * x, axis=-1, keepdims=True) + EPS)


def split(refs, *counts):
    found = []
    for count in counts:
        found.append(refs[:count])
        refs = refs[count:]
    return *found, refs


def halo_back_kernel(cores, sides, dk_ref, dv_ref, gk_ref, *refs):
    count = 2 * sides
    raws, factors, n1s, xs, cosines, sines, w_refs, refs = split(refs, *(count,) * 6, cores)
    left_ref, right_ref, gain_ref, rows_ref, acck_ref, accv_ref, n1t_ref, dn1_ref, low_ref, full_ref = refs
    step = pl.program_id(0)

    @pl.when(step == 0)
    def _():
        for tile, ref in enumerate(n1s):
            n1t_ref[:, tile * ROWS : (tile + 1) * ROWS] = ref[...].T
        dn1_ref[...] = jnp.zeros_like(dn1_ref)

    gain_ref[...] = jnp.zeros_like(gain_ref)
    fill_weights(full_ref, w_refs)
    turns = [(cosine[...], sine[...]) for cosine, sine in zip(cosines, sines)]
    dv = dv_ref[...]
    accv_ref[...] = mm(n1t_ref[...], dv).reshape(accv_ref.shape)
    dk0 = through_norm(dk_ref, raws, factors, gk_ref[...], gain_ref, 0, low_ref, turns)
    acck_ref[...] = mm(n1t_ref[...], dk0).reshape(acck_ref.shape)
    dn1_ref[...] += mm_nt(dv, weight(full_ref, 2)) + mm_nt(dk0, weight(full_ref, 1))

    @pl.when(step == pl.num_programs(0) - 1)
    def _():
        found = jnp.zeros(rows_ref.shape, f32)
        for tile, ref in enumerate(xs):
            dn1 = dn1_ref[tile * ROWS : (tile + 1) * ROWS, :]
            found = found + fold_rows(dn1 * unit_rows(ref))
            out_ref, at = (left_ref, tile) if tile < sides else (right_ref, tile - sides)
            out_ref[at * ROWS : (at + 1) * ROWS, :] = dn1.astype(bf16)
        rows_ref[...] = found


def tile_specs(tiles, shape, cols=None):
    if cols is None:
        return [pl.BlockSpec(shape, lambda i, t=t: (t, 0), pipeline_mode=pl.Buffered(1)) for t in tiles]
    return [pl.BlockSpec(shape, lambda i, t=t: (t, cols(i))) for t in tiles]


def halo_back(dk, dv, k0, kf, n1, x_ext, cosine, sine, gk, w, w_rows):
    ext, width = n1.shape
    cores = len(w)
    sides = HALF // ROWS
    last = ext // ROWS
    tiles = (*range(sides), *range(last - sides, last))
    count = len(tiles)
    chunk_acc = (w[0].shape[0], cores, w_rows, CHUNK)
    column = lambda i: i
    rows = count * ROWS
    cut = pl.BlockSpec((rows, CHUNK), lambda i: (0, i))
    acc = pl.BlockSpec(chunk_acc, lambda i: (0, 0, 0, i))
    return pl.pallas_call(
        functools.partial(halo_back_kernel, cores, sides),
        name="halo_back",
        grid=(width // CHUNK,),
        in_specs=[cut, cut, whole((1, 128))]
        + tile_specs(tiles, (ROWS, CHUNK), column) * 2
        + tile_specs(tiles, (ROWS, width)) * 2
        + tile_specs(tiles, (ROWS, 128)) * 2
        + [pl.BlockSpec(each.shape[:2] + (CHUNK,), lambda i: (0, 0, i)) for each in w],
        out_specs=[
            whole((HALF, width)),
            whole((HALF, width)),
            pl.BlockSpec((1, 8, CHUNK), lambda i: (0, 0, i)),
            whole((8, width)),
            acc,
            acc,
        ],
        out_shape=[
            shape_of((HALF, width), bf16),
            shape_of((HALF, width), bf16),
            shape_of((1, 8, width), f32),
            shape_of((8, width), f32),
            shape_of(chunk_acc[:3] + (width,), f32),
            shape_of(chunk_acc[:3] + (width,), f32),
        ],
        scratch_shapes=[
            pltpu.VMEM((width, rows), bf16),
            pltpu.VMEM((rows, width), f32),
            pltpu.VMEM((rows, CHUNK), bf16),
            pltpu.VMEM((w[0].shape[1] // w_rows,) + chunk_acc, bf16),
        ],
        compiler_params=params(60),
        cost_estimate=cost(18),
    )(
        dk, dv, gk,
        *[k0] * count, *[kf] * count, *[n1] * count, *[x_ext] * count, *[cosine] * count, *[sine] * count, *w,
    )


def project_back_kernel(
    half, cores, count, dk_ref, dv_ref, dq_ref, q0_ref, qf_ref, gk_ref, gq_ref, firstk_ref, firstv_ref, *refs,
):
    raws, factors, n1s, cosines, sines, w_refs, refs = split(refs, *(count,) * 5, cores)
    if half:
        xs, (before_ref, dn1_ref, gain_ref, rows_ref), refs = split(refs, count, 4)
    else:
        (dn1_ref, gain_ref), refs = split(refs, 2)
    dw_refs, (acc_ref, n1t_ref, low_ref, full_ref) = split(refs, cores)
    step = pl.program_id(0)

    @pl.when(step == 0)
    def _():
        for tile, ref in enumerate(n1s):
            n1t_ref[:, tile * ROWS : (tile + 1) * ROWS] = ref[...].T
        if half:
            dn1_ref[...] = before_ref[...]
        else:
            dn1_ref[...] = jnp.zeros_like(dn1_ref)

    gain_ref[...] = jnp.zeros_like(gain_ref)
    fill_weights(full_ref, w_refs)
    turns = [(cosine[...], sine[...]) for cosine, sine in zip(cosines, sines)]
    cuts = [slice(tile * ROWS, (tile + 1) * ROWS) for tile in range(count)]

    def grads(index, values, first_ref):
        found = mm(n1t_ref[...], values).reshape(acc_ref.shape)
        acc_ref[...] = found if first_ref is None else found + first_ref[...]
        put_grads(dw_refs, acc_ref, index * acc_ref.shape[2])

    dv = dv_ref[...]
    grads(2, dv, firstv_ref)
    dk0 = through_norm(dk_ref, raws, factors, gk_ref[...], gain_ref, 0, low_ref, turns)
    grads(1, dk0, firstk_ref)
    dn1 = mm_nt(dv, weight(full_ref, 2)) + mm_nt(dk0, weight(full_ref, 1))
    q_raws, q_factors = ([ref.at[cut] for cut in cuts] for ref in (q0_ref, qf_ref))
    dq0 = through_norm(dq_ref, q_raws, q_factors, gq_ref[...], gain_ref, 1, low_ref, turns)
    grads(0, dq0, None)
    dn1_ref[...] += dn1 + mm_nt(dq0, weight(full_ref, 0))

    if half:

        @pl.when(step == pl.num_programs(0) - 1)
        def _():
            found = jnp.zeros(rows_ref.shape, f32)
            for cut, ref in zip(cuts, xs):
                found = found + fold_rows(dn1_ref[cut, :] * unit_rows(ref))
            rows_ref[...] = found


def project_back(
    half, dq, dk, dv, first_sums, q0, qf, k0, kf, n1, x_ext, cosine, sine, gq, gk, w, w_rows, before=()
):
    ext, width = n1.shape
    tok = q0.shape[0]
    cores = len(w)
    part_width = width // 2
    chunks = part_width // CHUNK
    first = HALF // ROWS
    tiles = tuple(range(first, first + tok // ROWS))
    count = len(tiles)
    w_shape = w[0].shape[:2] + (part_width,)
    chunk_acc = (w[0].shape[0], cores, w_rows, CHUNK)
    column = lambda i: half * chunks + i
    cut = pl.BlockSpec((tok, CHUNK), lambda i: (0, column(i)))
    sums = pl.BlockSpec(chunk_acc, lambda i: (0, 0, 0, column(i)))
    return pl.pallas_call(
        functools.partial(project_back_kernel, half, cores, count),
        name="project_back",
        grid=(chunks,),
        in_specs=[cut] * 5
        + [whole((1, 128))] * 2
        + [sums] * 2
        + tile_specs(tiles, (ROWS, CHUNK), column) * 2
        + tile_specs(tiles, (ROWS, width))
        + tile_specs(tiles, (ROWS, 128)) * 2
        + [pl.BlockSpec(each.shape[:2] + (CHUNK,), lambda i: (0, 0, column(i))) for each in w]
        + (tile_specs(tiles, (ROWS, width)) + [whole((tok, width))]) * half,
        out_specs=[whole((tok, width)), pl.BlockSpec((2, 8, CHUNK), lambda i: (0, 0, i))]
        + [whole((8, width))] * half
        + [pl.BlockSpec(w_shape[:2] + (CHUNK,), lambda i: (0, 0, i))] * cores,
        out_shape=[shape_of((tok, width), f32), shape_of((2, 8, part_width), f32)]
        + [shape_of((8, width), f32)] * half
        + [shape_of(w_shape, bf16)] * cores,
        scratch_shapes=[
            pltpu.VMEM(chunk_acc, f32),
            pltpu.VMEM((width, tok), bf16),
            pltpu.VMEM((tok, CHUNK), bf16),
            pltpu.VMEM((w[0].shape[1] // w_rows,) + chunk_acc, bf16),
        ],
        compiler_params=params(60),
        cost_estimate=cost(15),
    )(
        dk, dv, dq, q0, qf, gk, gq, *first_sums,
        *[k0] * count, *[kf] * count, *[n1] * count, *[cosine] * count, *[sine] * count, *w,
        *([x_ext] * count) * half, *before,
    )


def assemble_kernel(rows, blocks, grads_ref, got_ref, down_ref, gate_ref, up_ref):
    core = lax.axis_index("core")
    width = grads_ref.shape[1]
    down_rows = blocks * rows
    down_ref[...] = grads_ref[0:down_rows, :].astype(f32)
    for index, out_ref in enumerate((gate_ref, up_ref)):
        for block in range(blocks // 2):
            first = down_rows + (index * (blocks // 2) + block) * 2 * rows
            mine = grads_ref[pl.ds(pl.multiple_of(first + core * rows, rows), rows), :].astype(f32)
            other = got_ref[index, block].astype(f32)
            for chunk in range(width // 128):
                at = block * 2 * width + chunk * 256
                cols = slice(chunk * 128, chunk * 128 + 128)
                out_ref[:, pl.ds(pl.multiple_of(at + core * 128, 128), 128)] = mine[:, cols]
                out_ref[:, pl.ds(pl.multiple_of(at + (1 - core) * 128, 128), 128)] = other[:, cols]


def assemble(grads, got, rows, blocks):
    width = grads.shape[1]
    return pl.pallas_call(
        functools.partial(assemble_kernel, rows, blocks),
        name="assemble",
        out_shape=[
            shape_of((blocks * rows, width), f32),
            shape_of((rows, blocks * width), f32),
            shape_of((rows, blocks * width), f32),
        ],
        compiler_params=params(16),
        cost_estimate=cost(2),
    )(grads, got)


def pack_kernel(copies_spread, blocks, rows, wq, wk, wv, wo, wg, wu, wd, attn_out, rest_out, sems):
    width = wq.shape[1]
    jobs = [(wd, rest_out.at[pl.ds(0, blocks * rows)])]
    for index, side in enumerate((wg, wu)):
        for part_at in range(blocks):
            at = (blocks * (1 + index) + part_at) * rows
            jobs.append((side.at[:, pl.ds(part_at * width, width)], rest_out.at[pl.ds(at, rows)]))
    jobs.append((wo, rest_out.at[pl.ds(3 * blocks * rows, rows)]))
    for copy in range(copies_spread):
        for index, each in enumerate((wq, wk, wv)):
            jobs.append((each, attn_out.at[copy, pl.ds(index * rows, rows)]))
    found = [pltpu.make_async_copy(source, target, sems.at[i]) for i, (source, target) in enumerate(jobs)]
    for copy in found:
        copy.start()
    for copy in found:
        copy.wait()


def pack(weights, copies_spread, blocks):
    rows, width = weights[0].shape
    total = (3 * blocks + 1) * rows
    return pl.pallas_call(
        functools.partial(pack_kernel, copies_spread, blocks, rows),
        name="pack",
        in_specs=[pl.BlockSpec(memory_space=pl.ANY)] * 7,
        out_specs=[pl.BlockSpec(memory_space=pl.ANY)] * 2,
        out_shape=[shape_of((copies_spread, 3 * rows, width), bf16), shape_of((total, width), bf16)],
        scratch_shapes=[pltpu.SemaphoreType.DMA((2 + 2 * blocks + 3 * copies_spread,))],
        compiler_params=params(4),
    )(*weights)


def local(
    inputs, seg_ids, var_ids, time_ids, valid_mask,
    w_query, w_key, w_value, w_out, w_gate, w_up, w_down,
    gain_attn, gain_ffn, gain_query, gain_key, variate_bias, out_grad,
):
    axes = ("head", "chip", "core")
    head_count, chip_count, core_count = (lax.axis_size(axis) for axis in axes)
    blk_count = chip_count * core_count
    devices = head_count * blk_count
    chips = head_count * chip_count
    tok, width = inputs.shape[1:]
    heads = variate_bias.shape[1]
    head_dim = gain_query.shape[0]
    rows = w_query.shape[0]
    blocks = w_gate.shape[1] // width
    ext = tok + 2 * HALF
    blk = lax.axis_index("chip") * core_count + lax.axis_index("core")
    place = blk * head_count + lax.axis_index("head")
    fast = rows % 16 == 0
    k_cores, k_devices, k_rows = (core_count, devices, rows) if fast else (1, 1, width)
    k_chips = k_devices // k_cores

    def flat(p):
        return (p % head_count) * blk_count + p // head_count

    onward = [(flat(p), flat(p + 1)) for p in range(devices - 1)]
    back = [(b, a) for a, b in onward]

    def exchange(values, axis):
        return lax.all_to_all(values, axis, split_axis=0, concat_axis=0, tiled=True)

    def swap_cores(values):
        return lax.ppermute(values, "core", [(0, 1), (1, 0)])

    def spread_to_all(full, parts):
        full = exchange(jnp.broadcast_to(full[None], (head_count,) + full.shape), "head")
        full = full.reshape(chips, parts * rows, width)
        other = swap_cores(full)
        if fast:
            return [full, other]
        swapped = lax.axis_index("core") == 1
        both = jnp.stack([jnp.where(swapped, other, full), jnp.where(swapped, full, other)])
        pieces = both.reshape(core_count, chips, parts, rows, width).transpose(2, 1, 0, 3, 4)
        return [pieces.reshape(1, parts * width, width)]

    def total(values):
        return jnp.sum(values.astype(f32), axis=0)

    def reduce_cores(grads, parts):
        wide = grads[0].shape[-1]
        if not fast:
            pieces = grads[0].reshape(parts, chips, core_count, rows, wide).transpose(2, 1, 0, 3, 4)
            core = lax.axis_index("core")
            grads = [lax.dynamic_index_in_dim(pieces, at, 0, False) for at in (core, 1 - core)]
        mine, other = (each.reshape(head_count, chip_count, parts * rows, wide) for each in grads)
        return (mine.astype(f32) + swap_cores(other).astype(f32)).astype(bf16)

    def reduce_heads(grads):
        return total(exchange(grads, "head")).astype(bf16)

    def reduce_chips(grads):
        return total(exchange(grads, "chip"))

    def gather_rest(shard):
        full = lax.all_gather(shard, axes, axis=0, tiled=False)
        if fast:
            return full
        parts = shard.shape[0] // rows
        down = full[:, : blocks * rows].reshape(1, blocks * width, width)
        rest = full[:, blocks * rows :].reshape(devices, parts - blocks, rows, width)
        rest = rest.transpose(1, 0, 2, 3).reshape(1, (parts - blocks) * width, width)
        return jnp.concatenate([down, rest], axis=1)

    def scatter_pair(grads):
        pieces = grads[blocks * rows :].reshape(2, blocks // 2, 2, rows, width)
        other = lax.dynamic_index_in_dim(pieces, 1 - lax.axis_index("core"), 2, False)
        return assemble(grads, swap_cores(other), rows, blocks)

    def scatter_stage(grads, axis):
        return lax.psum_scatter(grads.reshape(-1, width), axis, scatter_dimension=0, tiled=True)

    def scatter_rest(grads):
        if not fast:
            down = grads[0, : blocks * width].reshape(devices, blocks * rows, width)
            rest = grads[0, blocks * width :].reshape(2 * blocks, devices, rows, width).transpose(1, 0, 2, 3)
            grads = jnp.concatenate([down, rest.reshape(devices, -1, width)], axis=1)
        grads = grads.reshape(devices * 3 * blocks * rows, width)
        return lax.psum_scatter(grads, axes, scatter_dimension=0, tiled=True).astype(f32)

    def columns(shard):
        return [shard[:, i * width : (i + 1) * width] for i in range(blocks)]

    def sides(owned):
        return jnp.concatenate([owned[i * rows : (i + 1) * rows] for i in range(blocks)], axis=1)

    if fast:
        attn_part, rest_part = pack((w_query, w_key, w_value, w_out, w_gate, w_up, w_down), chip_count, blocks)
    else:
        attn_part = jnp.concatenate([w_query, w_key, w_value], axis=0)
        attn_part = jnp.broadcast_to(attn_part[None], (chip_count,) + attn_part.shape)
        rest_part = jnp.concatenate([w_down] + columns(w_gate) + columns(w_up) + [w_out], axis=0)
    rest_w = gather_rest(rest_part)
    x = inputs[0]
    attn_w = exchange(attn_part, "chip")
    ids = jnp.stack([seg_ids, var_ids, valid_mask, time_ids]).reshape(4, -1)
    ids = jnp.pad(ids, ((0, 0), (HALF, HALF)))
    ids = lax.dynamic_slice_in_dim(ids, place * tok, ext, 1).T
    own = slice(HALF, HALF + tok)
    quarter = jnp.arange(128) % (head_dim // 2)
    frequency = 10000.0 ** (-quarter.astype(f32) * 2.0 / head_dim)
    angles = ids[:, 3:].astype(f32) * frequency[None, :]
    cosine = jnp.cos(angles)
    sine = jnp.sin(angles) * jnp.where(jnp.arange(128) % head_dim < head_dim // 2, -1.0, 1.0)
    diff = (variate_bias[0] - variate_bias[1]) * LOG2E
    diff_high = lax.reduce_precision(diff, 8, 7)
    diff_low = diff - diff_high
    lane = jnp.arange(128)[None, :]
    diff_rows = jnp.where(lane < LANE_LOW, diff_high[:, None], jnp.where(lane < LANE_CODE, diff_low[:, None], 1.0))
    gq = jnp.tile(gain_query, 2)[None]
    gk = jnp.tile(gain_key, 2)[None]

    before = lax.ppermute(x[tok - HALF :], axes, onward)
    after = lax.ppermute(x[:HALF], axes, back)
    attn_w, before, after, ids, cosine, sine = lax.optimization_barrier((attn_w, before, after, ids, cosine, sine))
    attn_w = spread_to_all(attn_w, 3)
    x_ext = jnp.concatenate([before, x, after], axis=0)

    own_ids = ids[own]

    n1, q0, qf, k0, kf, q, k, v = project(
        x_ext, gain_attn[None], attn_w, k_rows, cosine, sine, gq, gk, ids, diff_rows, tok, heads
    )
    o, qb = attend(q, k, v, own_ids)

    out_spec = pl.BlockSpec((k_devices, k_rows, width), lambda i: (0, 3 * blocks, 0), pipeline_mode=pl.Buffered(1))
    h, n2, branch_sum = branch_forward(o, x, rest_w, out_spec, gain_ffn[None], own_ids)
    dy = out_grad[0]
    if fast:
        *middle, ff_grads = pair_grads(n2, swap_cores(n2), dy, swap_cores(dy), rest_w, rows, blocks)
        ff_grads = scatter_stage(ff_grads, "head")
        got = [swap_cores(pair_sums(True, *middle))]
        f, dn2 = pair_sums(False, *middle)
    else:
        hidden, dgate, dup, ff_grads = ffn_grads(n2, dy, rest_w, k_devices, k_rows, blocks)
        ff_owned = scatter_rest(ff_grads)
        down_owned = ff_owned[: blocks * rows]
        gate_owned = sides(ff_owned[blocks * rows : 2 * blocks * rows])
        up_owned = sides(ff_owned[2 * blocks * rows :])
        got = []
        f, dn2 = ffn_sums(hidden, dgate, dup, rest_w, k_devices, k_rows, blocks)
    layer_out, dh, do, sums, *out_grads = residual_back(
        h, f, dn2, dy, o, rest_w, out_spec, gain_ffn[None], own_ids, (k_chips, k_cores, k_rows, width), got
    )
    early = reduce_cores(out_grads, 1)
    do, early = lax.optimization_barrier((do, early))
    early = reduce_heads(early)
    norms = (q0, qf, k0, kf, n1, x_ext, cosine, sine, gq, gk, attn_w, k_rows)
    edge, count = HALF // ROWS, ext // ROWS
    halo_tiles = (*range(edge), *range(count - edge, count))
    own_tiles = tuple(range(edge, count - edge))
    pairs = heads // 2
    attention = (qb, k, v, o)
    dq_sums, dk, dv, bias_halo = attend_back(halo_tiles, 0, pairs, *attention, do, own_ids)
    dk, early = lax.optimization_barrier((dk, early))
    early_owned = reduce_chips(early)
    left, right, gain_halo, rows_halo, *first_sums = halo_back(
        dk, dv, k0, kf, n1, x_ext, cosine, sine, gk, attn_w, k_rows
    )
    from_left = lax.ppermute(right, axes, onward)
    from_right = lax.ppermute(left, axes, back)
    do, early_owned, left = lax.optimization_barrier((do, early_owned, left))
    dq, dk, dv, bias_own = attend_back(own_tiles, 0, pairs, *attention, do, own_ids, (dq_sums,))
    if fast:
        dq, ff_grads = lax.optimization_barrier((dq, ff_grads))
        down_owned, gate_owned, up_owned = scatter_pair(scatter_stage(ff_grads, "chip"))
    dn1_first, gain_first, *grads = project_back(0, dq, dk, dv, first_sums, *norms)
    grads, from_left, from_right = lax.optimization_barrier((grads, from_left, from_right))
    first_grads = reduce_cores(grads, 3)
    bias_rows = bias_halo + bias_own
    bias_rows = bias_rows.reshape(heads // 2, 8, 128)[:, :4].reshape(heads, 2, 128)[:, :, 64 : 64 + VARS].sum(-1)
    bias_grad = jnp.stack([bias_rows[:, 0], bias_rows[:, 1] - bias_rows[:, 0]])

    def gains_of(rows_of):
        found = rows_of.sum(1).reshape(rows_of.shape[0], -1, head_dim).sum(1)
        return jnp.concatenate([found[1], found[0]])

    key_halo = gain_halo[0].sum(0).reshape(heads, head_dim).sum(0)
    gain_heads = gains_of(gain_first) + jnp.pad(key_halo, (head_dim, 0))
    squares = jnp.stack([sums[0].sum(), branch_sum.sum(), sums[1].sum()])
    small = jnp.concatenate([rows_halo.sum(0), sums[2].sum(0), gain_heads, bias_grad.reshape(-1), squares])
    used = small.shape[0]
    small = jnp.pad(small, (0, -used % (4 * width)))
    dq, first_grads, small = lax.optimization_barrier((dq, first_grads, small))
    first_grads = reduce_heads(first_grads)
    dn1_own, gain_second, attn_rows, *grads = project_back(1, dq, dk, dv, first_sums, *norms, (dn1_first,))
    grads, first_grads = lax.optimization_barrier((grads, first_grads))
    second_sums = reduce_cores(grads, 3)
    small = small.at[:width].add(attn_rows.sum(0))
    small = small.at[2 * width : 2 * width + 2 * head_dim].add(gains_of(gain_second))
    half = width // 2
    small = small + swap_cores(small)

    def with_small(values):
        high = lax.reduce_precision(small, 8, 7)
        rows_of = jnp.concatenate([high, small - high]).astype(bf16).reshape(-1, half)
        lead = values.shape[:-2]
        return jnp.concatenate([values, jnp.broadcast_to(rows_of, lead + rows_of.shape)], axis=-2)

    def small_total(values):
        sums_of = jnp.sum(values.reshape(values.shape[0], 2, -1).astype(f32), axis=(0, 1))
        return sums_of

    kept = second_sums.shape[-2]
    second_sums = exchange(with_small(second_sums), "head")
    small = small_total(second_sums[:, 0, kept:])
    second_sums = total(second_sums[:, :, :kept]).astype(bf16)
    second_sums = exchange(jnp.concatenate([first_grads, with_small(second_sums)], axis=-2), "chip")
    small = small_total(second_sums[:, 2 * kept :])
    attn_owned = total(second_sums[:, : 2 * kept])
    attn_owned = jnp.concatenate([attn_owned[:kept], attn_owned[kept:]], axis=1)

    dn1 = (
        dn1_own
        + jnp.pad(from_left.astype(f32), ((0, tok - HALF), (0, 0)))
        + jnp.pad(from_right.astype(f32), ((tok - HALF, 0), (0, 0)))
    )
    x_float = x.astype(f32)
    factor = lax.rsqrt(jnp.mean(x_float * x_float, axis=-1, keepdims=True) + EPS)
    unit = x_float * factor
    dunit = dn1 * gain_attn
    inner = jnp.mean(dunit * unit, axis=-1, keepdims=True)
    grad_inputs = (dh + factor * (dunit - unit * inner)).astype(bf16)

    at = 2 * width
    valid_count = jnp.maximum(jnp.sum((valid_mask == 1).astype(f32)), 1.0)
    rms_values = jnp.sqrt(small[at + 2 * head_dim + 2 * heads :][:3] / (valid_count * width))

    return (
        layer_out[None],
        grad_inputs[None],
        attn_owned[:rows],
        attn_owned[rows : 2 * rows],
        attn_owned[2 * rows :],
        early_owned,
        gate_owned,
        up_owned,
        down_owned,
        small[:width],
        small[width : 2 * width],
        small[at : at + head_dim],
        small[at + head_dim : at + 2 * head_dim],
        small[at + 2 * head_dim : at + 2 * head_dim + 2 * heads].reshape(2, heads),
        rms_values,
    )


def solution(mesh):
    heads, blks = mesh.devices.shape
    cores = 2 if blks % 2 == 0 else 1
    mesh = Mesh(mesh.devices.reshape(heads, blks // cores, cores), ("head", "chip", "core"))
    tokens = P(("chip", "core"), "head", None)
    weights = P(("head", "chip", "core"), None)
    in_specs = (tokens,) + (P(),) * 4 + (weights,) * 7 + (P(),) * 5 + (tokens,)
    out_specs = (tokens,) * 2 + (weights,) * 7 + (P(),) * 6
    return jax.shard_map(local, mesh=mesh, in_specs=in_specs, out_specs=out_specs, check_vma=False)
```
